512 devices in a mesh: slab: 64 (over z, x), sec: 8 (over y, core).
Axes of the slice: x: 4, y: 4, z: 16, core: 2. Of those that a mesh axis runs over, the one named last changes fastest.
Arguments:
- source: float32 [64, 65536], P(None, ('slab', 'sec'))
- fine_blocks: bfloat16 [3, 64, 64, 65536], P(None, None, None, ('slab', 'sec'))
- fine_pattern: int32 [3, 65536], P(None, ('slab', 'sec')), may hold values from 0 to 65535, as said below
- fine_prolong: bfloat16 [3, 64, 6, 65536], P(None, None, None, ('slab', 'sec')), may hold values from -0.75 to 0.75
- prolong_pattern: int32 [3, 65536], P(None, ('slab', 'sec')), may hold values from 0 to 65535, as said below
- coarse_blocks: bfloat16 [3, 6, 6, 65536], P(None, None, None, 'slab')
- coarse_pattern: int32 [3, 65536], P(None, 'slab'), may hold values from 0 to 65535, as said below
- section_prolong: bfloat16 [3, 6, 24, 65536], P(None, None, None, 'slab'), may hold values from -0.046875 to 0.046875
- coarsest_inverse: float32 [1536, 1536], P('slab')
Outputs:
- solution: float32 [64, 65536], P(None, ('slab', 'sec'))
The draws below stay inside these ranges and needn't reach their ends.
Inputs may be any that keep to these rules, and one draw needn't show every extreme that they name: `fine_pattern`: row 0 names the aggregate itself; the other rows name aggregates at most 96 away, and distance exactly 96 occurs in every draw. `prolong_pattern`: row 0 names the aggregate's own coarse block; the other rows name coarse blocks at most 96 away, and distance exactly 96 occurs in every draw. `coarse_pattern`: row 0 names the block itself; the other rows name coarse blocks at most 96 away, and distance exactly 96 occurs in every draw.
All inputs are finite; a program needn't handle non-finite values.
Results may differ from the reference program's by a relative error of at most 0.0003.
Values sent between devices are 32-bit elements; how exact they have to be, the bound alone decides.
No kernel may reach another device: no remote copies, remote signals or barrier semaphores. Data moves between devices by JAX's collectives and lax.ppermute only.
A program may use at most 64 MiB of HBM per device.

```python
import jax
import jax.numpy as jnp
from jax import lax

NB_DEV = 128
BS = 64
MODES = 6
NBR = 3
HB = 96
CS = 24
CYCLES = 2
NB0 = 65536
NBS = 1024
NC = 1536
N_SLAB = 64


def band_pattern(key, total):
    first = jnp.arange(total, dtype=jnp.int32)
    lower = jax.random.randint(jax.random.fold_in(key, 1), (total,), 1, HB + 1, dtype=jnp.int32)
    upper = jax.random.randint(jax.random.fold_in(key, 2), (total,), 1, HB + 1, dtype=jnp.int32)
    lower = jnp.where(first % 8 == 3, HB, lower)
    upper = jnp.where(first % 8 == 5, HB, upper)
    below = jnp.where(first - lower >= 0, first - lower, first + lower)
    above = jnp.where(first + upper < total, first + upper, first - upper)
    return jnp.stack([first, below, above], 0).astype(jnp.int32)


def dominant_blocks(key, rows):
    spread = 0.35 / (NBR * rows) ** 0.5
    shape = (NBR, rows, rows, NB0)
    noise = jnp.clip(jax.random.normal(jax.random.fold_in(key, 1), shape, jnp.float32), -4.0, 4.0) * spread
    top = 0.916
    logs = jax.random.uniform(jax.random.fold_in(key, 2), (rows, NB0), jnp.float32, 0.0, top)
    diagonal = jnp.exp(logs)
    unit = (jnp.arange(rows)[:, None] == jnp.arange(rows)[None, :]).astype(jnp.float32)
    lead = noise[0] + unit[:, :, None] * diagonal[:, None, :]
    return jnp.concatenate([lead[None], noise[1:]], 0).astype(jnp.bfloat16)


def draw_source(key, part):
    base = jax.random.normal(jax.random.fold_in(key, 31), (BS, NB0), jnp.float32)
    return base


def draw_fine_blocks(key, part):
    return dominant_blocks(jax.random.fold_in(key, 41), BS)


def draw_coarse_blocks(key, part):
    return dominant_blocks(jax.random.fold_in(key, 42), MODES)


def draw_fine_pattern(key, part):
    return band_pattern(jax.random.fold_in(key, 11), NB0)


def draw_prolong_pattern(key, part):
    return band_pattern(jax.random.fold_in(key, 12), NB0)


def draw_coarse_pattern(key, part):
    return band_pattern(jax.random.fold_in(key, 13), NB0)


def draw_coarsest_inverse(key, part):
    scale = 6.0 * (6.0 * NBS / CS) ** 0.5
    logs = jax.random.uniform(jax.random.fold_in(key, 52), (NC,), jnp.float32, 0.0, 0.693)
    noise = jnp.clip(jax.random.normal(jax.random.fold_in(key, 51), (NC, NC), jnp.float32), -4.0, 4.0)
    unit = (jnp.arange(NC)[:, None] == jnp.arange(NC)[None, :]).astype(jnp.float32)
    return scale * (noise * (0.5 / NC ** 0.5) + unit * jnp.exp(logs)[:, None])


def shard_levels(stream_key, dims, pieces, least, high):
    gain, own = 1.0, jax.random.fold_in(stream_key, 6)
    for axis_at, shards_of in pieces:
        steps = jnp.exp(jax.random.uniform(jax.random.fold_in(own, axis_at), (shards_of,), jnp.float32, least / len(pieces), high / len(pieces)))
        gain = gain * jnp.repeat(steps, dims[axis_at] // shards_of).reshape([-1 if axis == axis_at else 1 for axis in range(len(dims))])
    return gain


def bell_draw(rng, extent, deviation, reach, pieces=(), kind=jnp.bfloat16):
    drawn = jax.random.normal(rng, extent, jnp.float32) * deviation
    if len(pieces) > 0:
        drawn = shard_levels(rng, extent, pieces, -0.22, 0.18) * drawn
    return jnp.clip(drawn, min=-reach, max=reach).astype(kind)


def setup_inputs(seed: int = 0) -> dict:
    streams_of = jax.random.split(jax.random.key(seed), 10)
    return {
        "source": draw_source(jax.random.fold_in(streams_of[9], 71), 0),
        "fine_blocks": draw_fine_blocks(jax.random.fold_in(streams_of[9], 71), 0),
        "fine_pattern": draw_fine_pattern(jax.random.fold_in(streams_of[9], 71), 0),
        "fine_prolong": bell_draw(streams_of[3], (NBR, BS, MODES, NB0), BS ** -0.5, 0.75, ((3, 512),)),
        "prolong_pattern": draw_prolong_pattern(jax.random.fold_in(streams_of[9], 71), 0),
        "coarse_blocks": draw_coarse_blocks(jax.random.fold_in(streams_of[9], 71), 0),
        "coarse_pattern": draw_coarse_pattern(jax.random.fold_in(streams_of[9], 71), 0),
        "section_prolong": bell_draw(streams_of[7], (3, MODES, CS, NB0), (3 * MODES * NBS) ** -0.5, 0.046875, ((3, 64),)),
        "coarsest_inverse": draw_coarsest_inverse(jax.random.fold_in(streams_of[9], 71), 0),
    }


KEEP = 1.0 / 7.0
FRESH = 8.0 / 7.0


def apply_blocks(matrix, pattern, field):
    count = pattern.shape[1] // NB_DEV

    def one_group(index):
        start = index * NB_DEV
        tile = lax.dynamic_slice_in_dim(matrix, start, NB_DEV, 3)
        columns = lax.dynamic_slice_in_dim(pattern, start, NB_DEV, 1)
        picked = jnp.swapaxes(field[:, columns], 0, 1)
        return jnp.sum(tile * picked[:, None, :, :], axis=(0, 2))

    groups = lax.map(one_group, jnp.arange(count, dtype=jnp.int32))
    return jnp.moveaxis(groups, 0, 1).reshape(field.shape[0], -1)


def inverse_diagonal(matrix):
    return 1.0 / jnp.diagonal(matrix[0], axis1=0, axis2=1).T.astype(jnp.float32)


def smooth(operator, inverse, rhs, start):
    if start is None:
        change = inverse * rhs
        field = change
    else:
        change = inverse * (rhs - operator(start))
        field = start + change
    change = KEEP * change + FRESH * inverse * (rhs - operator(field))
    return field + change


def restrict_fine(prolong, pattern, residual):
    terms = jnp.sum(prolong * residual[None, :, None, :], axis=1)
    flat = jnp.swapaxes(terms, 0, 1).reshape(terms.shape[1], -1)
    summed = jax.ops.segment_sum(flat.T, pattern.reshape(-1), num_segments=pattern.shape[1])
    return summed.T


def prolong_fine(prolong, pattern, coarse):
    picked = jnp.swapaxes(coarse[:, pattern], 0, 1)
    return jnp.sum(prolong * picked[:, None, :, :], axis=(0, 2))


def restrict_coarse(sections, residual):
    terms = jnp.sum(sections * residual[None, :, None, :], axis=1)
    parts = jnp.sum(terms.reshape(3, CS, N_SLAB, NBS), axis=3)
    zero = jnp.zeros((CS, 1), jnp.float32)
    total = parts[1] + jnp.concatenate([parts[0][:, 1:], zero], 1) + jnp.concatenate([zero, parts[2][:, :-1]], 1)
    return total.T.reshape(-1)


def prolong_coarse(sections, coarse):
    grid = coarse.reshape(N_SLAB, CS)
    zero = jnp.zeros((1, CS), jnp.float32)
    padded = jnp.concatenate([zero, grid, zero], 0)
    near = jnp.stack([padded[:-2], padded[1:-1], padded[2:]], 0)
    spread = jnp.repeat(near, NBS, axis=1)
    return jnp.sum(sections * jnp.swapaxes(spread, 1, 2)[:, None, :, :], axis=(0, 2))


def reference(source, fine_blocks, fine_pattern, fine_prolong, prolong_pattern, coarse_blocks, coarse_pattern, section_prolong, coarsest_inverse):
    fine_inverse = inverse_diagonal(fine_blocks)
    coarse_inverse = inverse_diagonal(coarse_blocks)

    def fine_apply(field):
        return apply_blocks(fine_blocks, fine_pattern, field)

    def coarse_apply(field):
        return apply_blocks(coarse_blocks, coarse_pattern, field)

    solution = None
    for turn_index in range(CYCLES):
        solution = smooth(fine_apply, fine_inverse, source, solution)
        residual = source - fine_apply(solution)
        coarse_rhs = restrict_fine(fine_prolong, prolong_pattern, residual)
        coarse_sol = smooth(coarse_apply, coarse_inverse, coarse_rhs, None)
        coarse_res = coarse_rhs - coarse_apply(coarse_sol)
        top_rhs = restrict_coarse(section_prolong, coarse_res)
        top_sol = jnp.dot(coarsest_inverse, top_rhs, precision=lax.Precision.HIGHEST)
        coarse_sol = coarse_sol + prolong_coarse(section_prolong, top_sol)
        coarse_sol = smooth(coarse_apply, coarse_inverse, coarse_rhs, coarse_sol)
        solution = solution + prolong_fine(fine_prolong, prolong_pattern, coarse_sol)
        solution = smooth(fine_apply, fine_inverse, source, solution)
    return solution
```

```python
import jax
import jax.numpy as jnp
from jax import lax
from jax.experimental import pallas as pl
from jax.experimental.pallas import tpu as pltpu
from jax.sharding import PartitionSpec as P

CYCLES = 2
KEEP = 1.0 / 7.0
FRESH = 8.0 / 7.0
LANES = 128
SUB = 8
EXT = 3
SPILL = EXT + 1
F32 = jnp.float32
BF16 = jnp.bfloat16
VMEM = pl.BlockSpec(memory_space=pltpu.VMEM)
SMEM = pl.BlockSpec(memory_space=pltpu.SMEM)


def call(body, outs, in_specs, scratch=(), flops=1 << 20, moved=1 << 20):
    return pl.pallas_call(
        body,
        out_shape=outs,
        in_specs=in_specs,
        out_specs=[VMEM] * len(outs),
        scratch_shapes=list(scratch),
        compiler_params=pltpu.CompilerParams(vmem_limit_bytes=24 << 20),
        cost_estimate=pl.CostEstimate(flops=flops, bytes_accessed=moved, transcendentals=0),
    )


def struct(*shape, dtype=F32):
    return jax.ShapeDtypeStruct(shape, dtype)


def take(x, lane):
    return jnp.take_along_axis(x, lane, axis=1, mode="promise_in_bounds")


def pick(three, target):
    lane = jnp.broadcast_to(target & (LANES - 1), three[0].shape)
    block = jnp.broadcast_to((target + LANES) >> 7, three[0].shape)
    a, b, c = (take(x, lane) for x in three)
    return jnp.where(block == 0, a, jnp.where(block == 1, b, c))


def fold_rows(terms):
    row = lax.broadcasted_iota(jnp.int32, (SUB, LANES), 0)
    for step in (4, 2, 1):
        high = (row & step) != 0
        half = len(terms) // 2
        folded = []
        for i in range(half):
            low_sum = terms[i] + pltpu.roll(terms[i], SUB - step, 0)
            high_sum = terms[i + half] + pltpu.roll(terms[i + half], step, 0)
            folded.append(jnp.where(high, high_sum, low_sum))
        terms = folded
    return terms[0]


def split3(x):
    high = x.astype(BF16)
    rest = x - high.astype(F32)
    middle = rest.astype(BF16)
    low = (rest - middle.astype(F32)).astype(BF16)
    return high, middle, low


def lanes_dot(a, b):
    return lax.dot_general(a, b, (((1,), (1,)), ((), ())), preferred_element_type=F32)


def base_and_iota(where_ref, slot):
    return where_ref[slot]


def load_halo(where_ref, pair_ref, odd_ref, ext):
    parity = where_ref[0]
    ext[1] = pair_ref[parity]
    ext[2 - 2 * parity] = pair_ref[1 - parity]
    ext[2 * parity] = odd_ref[...]


def fine_product(where_ref, matrix_ref, pattern_ref, ext, picked, out):
    rows = out.shape[0]
    base = where_ref[1]
    picked[0] = ext[1]
    for k in (1, 2):
        target = pattern_ref[k : k + 1, :] - base
        lane = jnp.broadcast_to(target & (LANES - 1), (SUB, LANES))
        block = jnp.broadcast_to((target + LANES) >> 7, (SUB, LANES))
        for t in range(rows // SUB):
            part = pl.ds(t * SUB, SUB)
            a, b, c = (take(ext[i, part, :], lane) for i in range(3))
            picked[k, part, :] = jnp.where(block == 0, a, jnp.where(block == 1, b, c))

    def group(g, carry):
        terms = []
        for p in range(SUB):
            total = None
            for k in range(3):
                block = matrix_ref[k, g * SUB + p].astype(F32)
                product = jnp.sum((block * picked[k]).reshape(rows // SUB, SUB, LANES), axis=0)
                total = product if total is None else total + product
            terms.append(total)
        out[pl.ds(pl.multiple_of(g * SUB, SUB), SUB), :] = fold_rows(terms)
        return carry

    lax.fori_loop(0, rows // SUB, group, 0)


def first_body(matrix_ref, source_ref, inverse_ref, field_ref):
    rows = source_ref.shape[0]
    row = lax.broadcasted_iota(jnp.int32, (SUB, LANES), 0)
    for g in range(rows // SUB):
        part = pl.ds(g * SUB, SUB)
        diagonal = jnp.zeros((SUB, LANES), F32)
        for p in range(SUB):
            entry = matrix_ref[0, g * SUB + p].astype(F32)[g * SUB : (g + 1) * SUB]
            diagonal = jnp.where(row == p, entry, diagonal)
        inverse = 1.0 / diagonal
        inverse_ref[part, :] = inverse
        field_ref[part, :] = inverse * source_ref[part, :]


def field_body(where_ref, pair_ref, odd_ref, matrix_ref, pattern_ref, source_ref, inverse_ref, change_ref, field_ref, ext, picked, out):
    load_halo(where_ref, pair_ref, odd_ref, ext)
    fine_product(where_ref, matrix_ref, pattern_ref, ext, picked, out)
    change = inverse_ref[...] * (source_ref[...] - out[...])
    change_ref[...] = change
    field_ref[...] = ext[1] + change


def solution_body(where_ref, pair_ref, odd_ref, matrix_ref, pattern_ref, source_ref, inverse_ref, change_ref, field_ref, ext, picked, out):
    load_halo(where_ref, pair_ref, odd_ref, ext)
    fine_product(where_ref, matrix_ref, pattern_ref, ext, picked, out)
    second = KEEP * change_ref[...] + FRESH * inverse_ref[...] * (source_ref[...] - out[...])
    field_ref[...] = ext[1] + second


def restrict_body(where_ref, pair_ref, odd_ref, matrix_ref, pattern_ref, source_ref, prolong_ref, targets_ref, sums_ref, ext, picked, out):
    load_halo(where_ref, pair_ref, odd_ref, ext)
    fine_product(where_ref, matrix_ref, pattern_ref, ext, picked, out)
    residual = source_ref[...] - out[...]
    modes = prolong_ref.shape[1]
    rows = residual.shape[0]
    slots = lax.broadcasted_iota(jnp.int32, (3 * LANES, LANES), 0)
    total = None
    for k in range(3):
        terms = []
        for m in range(SUB):
            if m < modes:
                product = prolong_ref[k, m].astype(F32) * residual
                terms.append(jnp.sum(product.reshape(rows // SUB, SUB, LANES), axis=0))
            else:
                terms.append(jnp.zeros((SUB, LANES), F32))
        parts = split3(fold_rows(terms))
        target = targets_ref[k : k + 1, :] - where_ref[1] + LANES
        hot = (slots == target).astype(F32).astype(BF16)
        stacked = jnp.concatenate([p.astype(F32) for p in parts] + [jnp.zeros((SUB, LANES), F32)], axis=0)
        spread = lanes_dot(stacked.astype(BF16), hot)
        total = spread if total is None else total + spread
    sums = total[0:SUB] + total[SUB : 2 * SUB] + total[2 * SUB : 3 * SUB]
    for i in range(sums_ref.shape[0]):
        sums_ref[i] = sums


def setup_body(own_cols, where_ref, left_ref, right_ref, blocks_ref, pattern_ref, section_ref, matrix_ref, sections_ref, offset_ref, inverse_ref):
    modes = blocks_ref.shape[1]
    count = own_cols // LANES
    width = section_ref.shape[2]
    matrix_ref[...] = jnp.zeros_like(matrix_ref)
    row = lax.broadcasted_iota(jnp.int32, (SUB, LANES), 0)
    column = lax.broadcasted_iota(jnp.int32, (1, LANES), 1)
    at_offset = 3 * modes * modes
    at_section = at_offset + 2
    for b in range(count + 2 * EXT):
        inner = EXT <= b < EXT + count
        side = left_ref if b < EXT else right_ref
        at = b - EXT if inner else (b if b < EXT else b - EXT - count)
        cols = pl.ds(at * LANES, LANES)
        diagonal = jnp.zeros((SUB, LANES), F32)
        for k in range(3):
            for p in range(modes):
                if inner:
                    entry = blocks_ref[k, p, :, cols].astype(F32)
                else:
                    entry = side[pl.ds((k * modes + p) * modes, modes), cols]
                matrix_ref[b, k, p, 0:modes, :] = entry
                if k == 0:
                    diagonal = jnp.where(row == p, entry[p : p + 1, :], diagonal)
            for p in range(modes):
                if inner:
                    sections_ref[b, k, p] = section_ref[k, p, :, cols].astype(F32)
                else:
                    sections_ref[b, k, p] = side[pl.ds(at_section + (k * modes + p) * width, width), cols]
        inverse_ref[b] = jnp.where(row < modes, 1.0 / jnp.where(row < modes, diagonal, 1.0), 0.0)
        for k in range(2):
            if inner:
                offset = pattern_ref[k + 1 : k + 2, cols] - (where_ref[2] + at * LANES) - column
            else:
                offset = side[at_offset + k : at_offset + k + 1, cols].astype(jnp.int32)
            offset_ref[b, k : k + 1, :] = jnp.clip(offset, -LANES, LANES)


def coarse_product(matrix_ref, offset_ref, field, b):
    lanes = lax.broadcasted_iota(jnp.int32, (1, LANES), 1)
    three = [field[b + i] for i in range(3)]
    picked = [three[1]] + [pick(three, lanes + offset_ref[b, k : k + 1, :]) for k in range(2)]
    terms = []
    modes = matrix_ref.shape[2]
    for p in range(SUB):
        if p < modes:
            terms.append(sum(matrix_ref[b, k, p] * picked[k] for k in range(3)))
        else:
            terms.append(jnp.zeros((SUB, LANES), F32))
    return fold_rows(terms)


def gather_body(parts_ref, low_ref, all_ref, high_ref):
    count = parts_ref.shape[0]
    blocks = []
    for b in range(-1, count + 1):
        total = None
        for device in (b - 1, b, b + 1):
            if 0 <= device < count:
                at = (b - device + 1) * LANES
                term = parts_ref[device, :, at : at + LANES]
                total = term if total is None else total + term
        blocks.append(total)
    for i, block in enumerate(blocks):
        all_ref[i] = block
    for i in range(SPILL):
        low_ref[i] = blocks[i]
        high_ref[i] = blocks[count + 2 - SPILL + i]


def coarse_down_body(all_ref, below_ref, above_ref, matrix_ref, offset_ref, inverse_ref, section_ref, rhs_ref, sol_ref, top_ref, field, other):
    total = matrix_ref.shape[0]
    count = total - 2 * EXT
    modes = matrix_ref.shape[2]
    width = section_ref.shape[2]
    zero = jnp.zeros((SUB, LANES), F32)
    for b in range(total):
        terms = []
        at = b - (EXT - 1)
        if 0 <= at < count + 2:
            terms.append(all_ref[at])
        if b < SPILL:
            terms.append(below_ref[b])
        if b >= total - SPILL:
            terms.append(above_ref[b - (total - SPILL)])
        value = sum(terms[1:], terms[0])
        rhs_ref[b] = value
        field[b + 1] = inverse_ref[b] * value
    for edge in (0, total + 1):
        field[edge] = zero
        other[edge] = zero

    def first(b, carry):
        start = field[b + 1]
        second = KEEP * start + FRESH * inverse_ref[b] * (rhs_ref[b] - coarse_product(matrix_ref, offset_ref, field, b))
        other[b + 1] = start + second
        sol_ref[b] = start + second
        return carry

    lax.fori_loop(0, total, first, 0)

    def down(i, carry):
        b = i + EXT
        residual = rhs_ref[b] - coarse_product(matrix_ref, offset_ref, other, b)
        cols = pl.ds(pl.multiple_of(i * LANES, LANES), LANES)
        out = []
        for k in range(3):
            value = carry[k]
            for p in range(modes):
                value = value + section_ref[k, p, :, cols].astype(F32) * residual[p : p + 1, :]
            out.append(value)
        return tuple(out)

    sums = lax.fori_loop(0, count, down, tuple(jnp.zeros((width, LANES), F32) for _ in range(3)))
    stacked = jnp.concatenate(list(sums) + [jnp.zeros((LANES - 3 * width, LANES), F32)], axis=0)
    ones = jnp.ones((16, LANES), BF16)
    row = sum(lanes_dot(ones, part) for part in split3(stacked))
    top_ref[...] = jnp.broadcast_to(row[0:1], top_ref.shape)


def coarse_up_body(where_ref, parts_ref, top_inverse_ref, rhs_ref, sol_ref, matrix_ref, offset_ref, inverse_ref, sections_ref, fine_ref, prolong_ref, targets_ref, field_out, padded, column, field, other, final):
    total = matrix_ref.shape[0]
    count = total - 2 * EXT
    modes = matrix_ref.shape[2]
    width = sections_ref.shape[3]
    sections = parts_ref.shape[0]
    zero = jnp.zeros((SUB, LANES), F32)
    padded[0:SUB, :] = zero
    padded[pl.ds(SUB + sections, SUB), :] = zero
    padded[pl.ds(SUB, sections), :] = parts_ref[...]
    same = pltpu.roll(parts_ref[...], LANES - width, 1)
    upper = padded[pl.ds(SUB + 1, sections), :]
    lower = pltpu.roll(padded[pl.ds(SUB - 1, sections), :], LANES - 2 * width, 1)
    top = same + upper + lower
    answer = jnp.zeros((sections, LANES), F32)
    for c in range(width):
        answer = answer + top_inverse_ref[c] * top[:, c : c + 1]
    answer = jnp.sum(answer, axis=0, keepdims=True)
    rows = lax.broadcasted_iota(jnp.int32, (LANES, LANES), 0)
    lanes = lax.broadcasted_iota(jnp.int32, (LANES, LANES), 1)
    spread = jnp.sum(jnp.where(rows == lanes, answer, 0.0), axis=1, keepdims=True)
    column[...] = jnp.broadcast_to(spread, (LANES, LANES))
    for edge in (0, total + 1):
        field[edge] = zero
        other[edge] = zero

    def correct(b, carry):
        shift = jnp.where(b < EXT, 0, jnp.where(b < EXT + count, 1, 2)) * width
        terms = []
        for p in range(SUB):
            if p < modes:
                value = sum(
                    sections_ref[b, k, p] * column[pl.ds(pl.multiple_of(shift + k * width, SUB), width), :] for k in range(3)
                )
                terms.append(jnp.sum(value.reshape(width // SUB, SUB, LANES), axis=0))
            else:
                terms.append(zero)
        field[b + 1] = sol_ref[b] + fold_rows(terms)
        return carry

    lax.fori_loop(0, total, correct, 0)

    def smooth_first(b, carry):
        change = inverse_ref[b] * (rhs_ref[b] - coarse_product(matrix_ref, offset_ref, field, b))
        final[b] = change
        other[b + 1] = field[b + 1] + change
        return carry

    lax.fori_loop(0, total, smooth_first, 0)

    def smooth_second(b, carry):
        second = KEEP * final[b] + FRESH * inverse_ref[b] * (rhs_ref[b] - coarse_product(matrix_ref, offset_ref, other, b))
        final[b] = other[b + 1] + second
        return carry

    lax.fori_loop(EXT - 1, EXT + count + 1, smooth_second, 0)
    at = where_ref[3] + EXT - 1
    three = [final[at + i] for i in range(3)]
    picked = [three[1]] + [pick(three, targets_ref[k : k + 1, :] - where_ref[1]) for k in (1, 2)]
    for t in range(fine_ref.shape[0] // SUB):
        part = pl.ds(t * SUB, SUB)
        value = fine_ref[part, :]
        for k in range(3):
            for m in range(modes):
                value = value + prolong_ref[k, m, part, :].astype(F32) * picked[k][m : m + 1, :]
        field_out[part, :] = value


def shards(
    source,
    fine_blocks,
    fine_pattern,
    fine_prolong,
    prolong_pattern,
    coarse_blocks,
    coarse_pattern,
    section_prolong,
    coarsest_inverse,
):
    both = ("slab", "sec")
    slabs, secs = lax.axis_size("slab"), lax.axis_size("sec")
    devices = slabs * secs
    rows, own = source.shape
    modes = fine_prolong.shape[2]
    section_rows = coarse_blocks.shape[3]
    width = section_prolong.shape[2]
    blocks = section_rows // LANES + 2 * EXT
    halo = EXT * LANES
    section = lax.axis_index("slab")
    place = lax.axis_index("sec")
    device = section * secs + place
    where = jnp.stack([place % 2, device * own, section * section_rows, place]).astype(jnp.int32)

    prolong = jnp.transpose(fine_prolong, (0, 2, 1, 3))
    swap = [(i, i + 1) for i in range(1, devices - 1, 2)] + [(i + 1, i) for i in range(1, devices - 1, 2)]
    pairs = [[2 * i, 2 * i + 1] for i in range(secs // 2)]

    def nearby(field):
        odd = lax.ppermute(field, both, swap)
        pair = lax.all_gather(field, "sec", axis_index_groups=pairs, axis=0)
        return pair, odd

    def beside(value, step):
        return lax.ppermute(value, "slab", [(i, i + step) for i in range(max(0, -step), min(slabs, slabs - step))])

    offsets = coarse_pattern[1:] - section * section_rows - jnp.arange(section_rows, dtype=jnp.int32)

    def packed(at):
        def cut(x):
            return lax.slice_in_dim(x, at, at + halo, axis=x.ndim - 1).astype(F32).reshape(-1, halo)

        return jnp.concatenate([cut(coarse_blocks), cut(offsets), cut(section_prolong)], axis=0)

    left_data = beside(packed(section_rows - halo), 1)
    right_data = beside(packed(0), -1)
    near = [beside(coarsest_inverse, step) for step in (2, 1)] + [coarsest_inverse] + [beside(coarsest_inverse, step) for step in (-1, -2)]
    top_inverse = jnp.concatenate(near + [jnp.zeros((LANES - 5 * width, coarsest_inverse.shape[1]), F32)], axis=0)
    top_inverse = jnp.transpose(top_inverse.reshape(LANES, slabs, width), (2, 1, 0))
    matrix, sections, offset, coarse_inverse = call(
        lambda *refs: setup_body(section_rows, *refs),
        [
            struct(blocks, 3, modes, SUB, LANES),
            struct(blocks, 3, modes, width, LANES),
            struct(blocks, SUB, LANES, dtype=jnp.int32),
            struct(blocks, SUB, LANES),
        ],
        [SMEM] + [VMEM] * 5,
    )(where, left_data, right_data, coarse_blocks, coarse_pattern, section_prolong)

    fine = struct(rows, own)
    work = [pltpu.VMEM((3, rows, own), F32), pltpu.VMEM((3, rows, own), F32), pltpu.VMEM((rows, own), F32)]
    inverse, start = call(first_body, [fine, fine], [VMEM] * 2)(fine_blocks, source)

    def step(body, outs, field, *rest):
        pair, odd = nearby(field)
        return call(body, outs, [SMEM] + [VMEM] * (4 + len(rest)), work)(where, pair, odd, fine_blocks, fine_pattern, *rest)

    def smooth(field):
        change, field = step(field_body, [fine, fine], field, source, inverse)
        return step(solution_body, [fine], field, source, inverse, change)[0]

    coarse = struct(blocks, SUB, LANES)
    ends = struct(SPILL, SUB, LANES)
    line = pltpu.VMEM((blocks + 2, SUB, LANES), F32)
    for cycle in range(CYCLES):
        if cycle == 0:
            solution = step(solution_body, [fine], start, source, inverse, start)[0]
        else:
            solution = smooth(solution)
        sums = step(restrict_body, [struct(secs, SUB, 3 * LANES)], solution, source, prolong, prolong_pattern)[0]
        parts = lax.all_to_all(sums, "sec", 0, 0, tiled=True)
        low, everything, high = call(gather_body, [ends, struct(secs + 2, SUB, LANES), ends], [VMEM])(parts)
        below, above = beside(high, 1), beside(low, -1)
        rhs, coarse_sol, top = call(
            coarse_down_body, [coarse, coarse, struct(slabs, LANES)], [VMEM] * 7, [line, line]
        )(everything, below, above, matrix, offset, coarse_inverse, section_prolong)
        tops = lax.all_to_all(top, "slab", 0, 0, tiled=True)
        solution = call(
            coarse_up_body,
            [fine],
            [SMEM] + [VMEM] * 11,
            [pltpu.VMEM((slabs + 2 * SUB, LANES), F32), pltpu.VMEM((LANES, LANES), F32), line, line, line],
        )(where, tops, top_inverse, rhs, coarse_sol, matrix, offset, coarse_inverse, sections, solution, prolong, prolong_pattern)[0]
        solution = smooth(solution)
    return solution


def solution(mesh):
    in_specs = (
        P(None, ("slab", "sec")),
        P(None, None, None, ("slab", "sec")),
        P(None, ("slab", "sec")),
        P(None, None, None, ("slab", "sec")),
        P(None, ("slab", "sec")),
        P(None, None, None, "slab"),
        P(None, "slab"),
        P(None, None, None, "slab"),
        P("slab", None),
    )
    out_specs = P(None, ("slab", "sec"))
    return jax.shard_map(shards, mesh=mesh, in_specs=in_specs, out_specs=out_specs, check_vma=False)
```

```python
import jax
import jax.numpy as jnp
from jax import lax
from jax.experimental import pallas as pl
from jax.experimental.pallas import tpu as pltpu
from jax.sharding import PartitionSpec as P

CYCLES = 2
KEEP = 1.0 / 7.0
FRESH = 8.0 / 7.0
LANES = 128
SUB = 8
EXT = 3
SPILL = EXT + 1
F32 = jnp.float32
BF16 = jnp.bfloat16
VMEM = pl.BlockSpec(memory_space=pltpu.VMEM)
SMEM = pl.BlockSpec(memory_space=pltpu.SMEM)


def call(body, outs, in_specs, scratch=(), flops=1 << 20, moved=1 << 20):
    return pl.pallas_call(
        body,
        out_shape=outs,
        in_specs=in_specs,
        out_specs=[VMEM] * len(outs),
        scratch_shapes=list(scratch),
        compiler_params=pltpu.CompilerParams(vmem_limit_bytes=24 << 20),
        cost_estimate=pl.CostEstimate(flops=flops, bytes_accessed=moved, transcendentals=0),
    )


def struct(*shape, dtype=F32):
    return jax.ShapeDtypeStruct(shape, dtype)


def take(x, lane):
    return jnp.take_along_axis(x, lane, axis=1, mode="promise_in_bounds")


def pick(three, target):
    lane = jnp.broadcast_to(target & (LANES - 1), three[0].shape)
    block = jnp.broadcast_to((target + LANES) >> 7, three[0].shape)
    a, b, c = (take(x, lane) for x in three)
    return jnp.where(block == 0, a, jnp.where(block == 1, b, c))


def fold_rows(terms):
    row = lax.broadcasted_iota(jnp.int32, (SUB, LANES), 0)
    for step in (4, 2, 1):
        high = (row & step) != 0
        half = len(terms) // 2
        folded = []
        for i in range(half):
            low_sum = terms[i] + pltpu.roll(terms[i], SUB - step, 0)
            high_sum = terms[i + half] + pltpu.roll(terms[i + half], step, 0)
            folded.append(jnp.where(high, high_sum, low_sum))
        terms = folded
    return terms[0]


def split3(x):
    high = x.astype(BF16)
    rest = x - high.astype(F32)
    middle = rest.astype(BF16)
    low = (rest - middle.astype(F32)).astype(BF16)
    return high, middle, low


def lanes_dot(a, b):
    return lax.dot_general(a, b, (((1,), (1,)), ((), ())), preferred_element_type=F32)


def load_halo(where_ref, pair_ref, odd_ref, ext):
    parity = where_ref[0]
    ext[1] = pair_ref[parity]
    ext[2 - 2 * parity] = pair_ref[1 - parity]
    ext[2 * parity] = odd_ref[...]


def fine_product(where_ref, matrix_ref, pattern_ref, ext, picked, out):
    rows = out.shape[0]
    base = where_ref[1]
    picked[0] = ext[1]
    for k in (1, 2):
        target = pattern_ref[k : k + 1, :] - base
        lane = jnp.broadcast_to(target & (LANES - 1), (SUB, LANES))
        block = jnp.broadcast_to((target + LANES) >> 7, (SUB, LANES))
        for t in range(rows // SUB):
            part = pl.ds(t * SUB, SUB)
            a, b, c = (take(ext[i, part, :], lane) for i in range(3))
            picked[k, part, :] = jnp.where(block == 0, a, jnp.where(block == 1, b, c))

    def group(g, carry):
        terms = []
        for p in range(SUB):
            total = None
            for k in range(3):
                block = matrix_ref[k, g * SUB + p].astype(F32)
                product = jnp.sum((block * picked[k]).reshape(rows // SUB, SUB, LANES), axis=0)
                total = product if total is None else total + product
            terms.append(total)
        out[pl.ds(pl.multiple_of(g * SUB, SUB), SUB), :] = fold_rows(terms)
        return carry

    lax.fori_loop(0, rows // SUB, group, 0)


def first_body(matrix_ref, source_ref, inverse_ref, field_ref):
    rows = source_ref.shape[0]
    row = lax.broadcasted_iota(jnp.int32, (SUB, LANES), 0)
    for g in range(rows // SUB):
        part = pl.ds(g * SUB, SUB)
        diagonal = jnp.zeros((SUB, LANES), F32)
        for p in range(SUB):
            entry = matrix_ref[0, g * SUB + p].astype(F32)[g * SUB : (g + 1) * SUB]
            diagonal = jnp.where(row == p, entry, diagonal)
        inverse = 1.0 / diagonal
        inverse_ref[part, :] = inverse
        field_ref[part, :] = inverse * source_ref[part, :]


def field_body(where_ref, pair_ref, odd_ref, matrix_ref, pattern_ref, source_ref, inverse_ref, change_ref, field_ref, ext, picked, out):
    load_halo(where_ref, pair_ref, odd_ref, ext)
    fine_product(where_ref, matrix_ref, pattern_ref, ext, picked, out)
    change = inverse_ref[...] * (source_ref[...] - out[...])
    change_ref[...] = change
    field_ref[...] = ext[1] + change


def solution_body(where_ref, pair_ref, odd_ref, matrix_ref, pattern_ref, source_ref, inverse_ref, change_ref, field_ref, ext, picked, out):
    load_halo(where_ref, pair_ref, odd_ref, ext)
    fine_product(where_ref, matrix_ref, pattern_ref, ext, picked, out)
    second = KEEP * change_ref[...] + FRESH * inverse_ref[...] * (source_ref[...] - out[...])
    field_ref[...] = ext[1] + second


def restrict_body(where_ref, pair_ref, odd_ref, matrix_ref, pattern_ref, source_ref, prolong_ref, targets_ref, sums_ref, ext, picked, out):
    load_halo(where_ref, pair_ref, odd_ref, ext)
    fine_product(where_ref, matrix_ref, pattern_ref, ext, picked, out)
    residual = source_ref[...] - out[...]
    modes = prolong_ref.shape[1]
    rows = residual.shape[0]
    slots = lax.broadcasted_iota(jnp.int32, (3 * LANES, LANES), 0)
    total = None
    for k in range(3):
        terms = []
        for m in range(SUB):
            if m < modes:
                product = prolong_ref[k, m].astype(F32) * residual
                terms.append(jnp.sum(product.reshape(rows // SUB, SUB, LANES), axis=0))
            else:
                terms.append(jnp.zeros((SUB, LANES), F32))
        parts = split3(fold_rows(terms))
        target = targets_ref[k : k + 1, :] - where_ref[1] + LANES
        hot = (slots == target).astype(F32).astype(BF16)
        stacked = jnp.concatenate([p.astype(F32) for p in parts] + [jnp.zeros((SUB, LANES), F32)], axis=0)
        spread = lanes_dot(stacked.astype(BF16), hot)
        total = spread if total is None else total + spread
    sums = total[0:SUB] + total[SUB : 2 * SUB] + total[2 * SUB : 3 * SUB]
    for i in range(sums_ref.shape[0]):
        sums_ref[i] = sums


def pack_body(where_ref, blocks_ref, pattern_ref, top_ref, prolong_ref, targets_ref, low_ref, high_ref, fine_ref):
    modes = blocks_ref.shape[1]
    total = blocks_ref.shape[3]
    halo = low_ref.shape[1]
    width = top_ref.shape[0]
    column = lax.broadcasted_iota(jnp.int32, (1, halo), 1)
    for out, at in ((low_ref, 0), (high_ref, total - halo)):
        cols = pl.ds(at, halo)
        for k in range(3):
            for p in range(modes):
                row = (k * modes + p) * SUB
                out[row : row + modes, :] = blocks_ref[k, p, :, cols].astype(F32)
        row = 3 * modes * SUB
        for k in range(2):
            offset = pattern_ref[k + 1 : k + 2, cols] - (where_ref[2] + at) - column
            out[row + k : row + k + 1, :] = offset.astype(F32)
        row += SUB
        for i in range(top_ref.shape[1] // halo):
            out[row + i * width : row + (i + 1) * width, :] = top_ref[:, i * halo : (i + 1) * halo]
    rows = prolong_ref.shape[2]
    for k in range(3):
        for m in range(modes):
            at = (k * modes + m) * rows
            fine_ref[at : at + rows, :] = prolong_ref[k, m].astype(F32)
        at = 3 * modes * rows + k
        fine_ref[at : at + 1, :] = targets_ref[k : k + 1, :].astype(F32)


def setup_body(where_ref, left_ref, right_ref, blocks_ref, pattern_ref, matrix_ref, offset_ref, inverse_ref):
    modes = blocks_ref.shape[1]
    count = blocks_ref.shape[3] // LANES
    matrix_ref[...] = jnp.zeros_like(matrix_ref)
    row = lax.broadcasted_iota(jnp.int32, (SUB, LANES), 0)
    column = lax.broadcasted_iota(jnp.int32, (1, LANES), 1)
    at_offset = 3 * modes * SUB
    for b in range(count + 2 * EXT):
        inner = EXT <= b < EXT + count
        side = left_ref if b < EXT else right_ref
        at = b - EXT if inner else (b if b < EXT else b - EXT - count)
        cols = pl.ds(at * LANES, LANES)
        diagonal = jnp.zeros((SUB, LANES), F32)
        for k in range(3):
            for p in range(modes):
                if inner:
                    entry = blocks_ref[k, p, :, cols].astype(F32)
                else:
                    entry = side[pl.ds((k * modes + p) * SUB, modes), cols]
                matrix_ref[b, k, p, 0:modes, :] = entry
                if k == 0:
                    diagonal = jnp.where(row == p, entry[p : p + 1, :], diagonal)
        inverse_ref[b] = jnp.where(row < modes, 1.0 / jnp.where(row < modes, diagonal, 1.0), 0.0)
        for k in range(2):
            if inner:
                offset = pattern_ref[k + 1 : k + 2, cols] - (where_ref[2] + at * LANES) - column
            else:
                offset = side[at_offset + k : at_offset + k + 1, cols].astype(jnp.int32)
            offset_ref[b, k : k + 1, :] = jnp.clip(offset, -LANES, LANES)


def coarse_product(matrix_ref, offset_ref, field, b):
    lanes = lax.broadcasted_iota(jnp.int32, (1, LANES), 1)
    three = [field[b + i] for i in range(3)]
    picked = [three[1]] + [pick(three, lanes + offset_ref[b, k : k + 1, :]) for k in range(2)]
    terms = []
    modes = matrix_ref.shape[2]
    for p in range(SUB):
        if p < modes:
            terms.append(sum(matrix_ref[b, k, p] * picked[k] for k in range(3)))
        else:
            terms.append(jnp.zeros((SUB, LANES), F32))
    return fold_rows(terms)


def gather_body(parts_ref, low_ref, all_ref, high_ref):
    count = parts_ref.shape[0]
    blocks = []
    for b in range(-1, count + 1):
        total = None
        for device in (b - 1, b, b + 1):
            if 0 <= device < count:
                at = (b - device + 1) * LANES
                term = parts_ref[device, :, at : at + LANES]
                total = term if total is None else total + term
        blocks.append(total)
    for i, block in enumerate(blocks):
        all_ref[i] = block
    for i in range(SPILL):
        low_ref[i] = blocks[i]
        high_ref[i] = blocks[count + 2 - SPILL + i]


def coarse_down_body(where_ref, all_ref, below_ref, above_ref, matrix_ref, offset_ref, inverse_ref, section_ref, rhs_ref, sol_ref, top_ref, field, other):
    total = matrix_ref.shape[0]
    count = total - 2 * EXT
    modes = matrix_ref.shape[2]
    width = section_ref.shape[2]
    zero = jnp.zeros((SUB, LANES), F32)
    for b in range(total):
        terms = []
        at = b - (EXT - 1)
        if 0 <= at < count + 2:
            terms.append(all_ref[at])
        if b < SPILL:
            terms.append(below_ref[b])
        if b >= total - SPILL:
            terms.append(above_ref[b - (total - SPILL)])
        value = sum(terms[1:], terms[0])
        rhs_ref[b] = value
        field[b + 1] = inverse_ref[b] * value
    for edge in (0, total + 1):
        field[edge] = zero
        other[edge] = zero

    def first(b, carry):
        start = field[b + 1]
        second = KEEP * start + FRESH * inverse_ref[b] * (rhs_ref[b] - coarse_product(matrix_ref, offset_ref, field, b))
        other[b + 1] = start + second
        sol_ref[b] = start + second
        return carry

    lax.fori_loop(0, total, first, 0)

    def down(i, carry):
        b = i + EXT
        residual = rhs_ref[b] - coarse_product(matrix_ref, offset_ref, other, b)
        cols = pl.ds(pl.multiple_of(i * LANES, LANES), LANES)
        out = []
        for k in range(3):
            value = carry[k]
            for p in range(modes):
                value = value + section_ref[k, p, :, cols].astype(F32) * residual[p : p + 1, :]
            out.append(value)
        return tuple(out)

    sums = lax.fori_loop(0, count, down, tuple(jnp.zeros((width, LANES), F32) for _ in range(3)))
    stacked = jnp.concatenate(list(sums) + [jnp.zeros((LANES - 3 * width, LANES), F32)], axis=0)
    ones = jnp.ones((16, LANES), BF16)
    row = sum(lanes_dot(ones, part) for part in split3(stacked))
    top_ref[...] = jnp.broadcast_to(pltpu.roll(row, where_ref[4], 1)[0:1], top_ref.shape)


def top_body(where_ref, parts_ref, left_ref, top_inverse_ref, right_ref, sol_ref, section_ref, field_ref, edge_ref, column):
    count, modes, width = section_ref.shape[3] // LANES, section_ref.shape[1], section_ref.shape[2]
    sections = parts_ref.shape[0]
    chunk_count = sections * width // LANES
    sub = lax.broadcasted_iota(jnp.int32, (SUB, LANES), 0)
    lane = lax.broadcasted_iota(jnp.int32, (SUB, LANES), 1)
    chunks = [None] * chunk_count
    for tile in range(sections // SUB):
        first = (sub + (tile * SUB - 1)) * width
        chunk = (first + ((lane - first) & (LANES - 1))) >> 7
        value = parts_ref[tile * SUB : (tile + 1) * SUB, :]
        low = (tile * SUB - 1) * width
        for q in range(max(0, low // LANES), min(chunk_count, (low + (SUB + 2) * width) // LANES + 1)):
            term = jnp.where(chunk == q, value, 0.0)
            chunks[q] = term if chunks[q] is None else chunks[q] + term
    chunks = [jnp.sum(c, axis=0, keepdims=True) for c in chunks]
    halo = left_ref.shape[1]
    at_top = 3 * modes * SUB + SUB
    answers = []
    for side in range(3):
        total = None
        for q in range(chunk_count):
            if side == 1:
                part = top_inverse_ref[:, q * LANES : (q + 1) * LANES]
            else:
                ref = left_ref if side == 0 else right_ref
                i, at = divmod(q * LANES, halo)
                part = ref[pl.ds(at_top + i * width, width), pl.ds(at, LANES)]
            term = part * chunks[q]
            total = term if total is None else total + term
        answers.append(jnp.sum(total, axis=1, keepdims=True))
    for side in range(3):
        column[side * width : (side + 1) * width, :] = jnp.broadcast_to(answers[side], (width, LANES))
    zero = jnp.zeros((SUB, LANES), F32)

    def correct(b, carry):
        cols = pl.ds(pl.multiple_of(b * LANES, LANES), LANES)
        terms = []
        for p in range(SUB):
            if p < modes:
                value = sum(section_ref[k, p, :, cols].astype(F32) * column[k * width : (k + 1) * width, :] for k in range(3))
                terms.append(jnp.sum(value.reshape(width // SUB, SUB, LANES), axis=0))
            else:
                terms.append(zero)
        field_ref[b] = sol_ref[b + EXT] + fold_rows(terms)
        return carry

    lax.fori_loop(0, count, correct, 0)
    start = jnp.where(where_ref[5] > 0, count - EXT, 0)
    for i in range(EXT):
        edge_ref[i] = field_ref[start + i]


def up_body(
    where_ref,
    middle_ref,
    edge_ref,
    rhs_ref,
    matrix_ref,
    offset_ref,
    inverse_ref,
    pair_ref,
    odd_ref,
    prolong_ref,
    even_prolong_ref,
    odd_prolong_ref,
    targets_ref,
    fine_matrix_ref,
    fine_pattern_ref,
    source_ref,
    fine_inverse_ref,
    change_ref,
    field_ref,
    field,
    other,
    final,
    ext,
    picked,
    out,
):
    total = matrix_ref.shape[0]
    count = total - 2 * EXT
    modes = matrix_ref.shape[2]
    zero = jnp.zeros((SUB, LANES), F32)
    from_left = where_ref[5] > 0
    for i in range(EXT):
        field[1 + i] = jnp.where(from_left, edge_ref[i], 0.0)
        field[1 + EXT + count + i] = jnp.where(from_left, 0.0, edge_ref[i])
    for i in range(count):
        field[1 + EXT + i] = middle_ref[i]
    for edge in (0, total + 1):
        field[edge] = zero
        other[edge] = zero

    def smooth_first(b, carry):
        change = inverse_ref[b] * (rhs_ref[b] - coarse_product(matrix_ref, offset_ref, field, b))
        final[b] = change
        other[b + 1] = field[b + 1] + change
        return carry

    lax.fori_loop(0, total, smooth_first, 0)

    def smooth_second(b, carry):
        second = KEEP * final[b] + FRESH * inverse_ref[b] * (rhs_ref[b] - coarse_product(matrix_ref, offset_ref, other, b))
        final[b] = other[b + 1] + second
        return carry

    lax.fori_loop(EXT - 2, EXT + count + 2, smooth_second, 0)
    load_halo(where_ref, pair_ref, odd_ref, ext)
    rows = ext.shape[1]
    parity = where_ref[0]
    for which in range(3):
        block = (1, 2 - 2 * parity, 2 * parity)[which]
        side = (None, even_prolong_ref, odd_prolong_ref)[which]
        at = where_ref[3] + EXT + block - 2
        three = [final[at + i] for i in range(3)]
        terms = []
        for k in range(3):
            if which == 0:
                target = targets_ref[k : k + 1, :] - where_ref[1]
            else:
                row = 3 * modes * rows + k
                target = side[row : row + 1, :].astype(jnp.int32) - (where_ref[1] + (block - 1) * LANES)
            terms.append(three[1] if k == 0 else pick(three, target))
        for t in range(rows // SUB):
            part = pl.ds(t * SUB, SUB)
            value = ext[block, part, :]
            for k in range(3):
                for m in range(modes):
                    if which == 0:
                        weight = prolong_ref[k, m, part, :].astype(F32)
                    else:
                        weight = side[pl.ds((k * modes + m) * rows + t * SUB, SUB), :]
                    value = value + weight * terms[k][m : m + 1, :]
            ext[block, part, :] = value
    fine_product(where_ref, fine_matrix_ref, fine_pattern_ref, ext, picked, out)
    change = fine_inverse_ref[...] * (source_ref[...] - out[...])
    change_ref[...] = change
    field_ref[...] = ext[1] + change


def shards(
    source,
    fine_blocks,
    fine_pattern,
    fine_prolong,
    prolong_pattern,
    coarse_blocks,
    coarse_pattern,
    section_prolong,
    coarsest_inverse,
):
    both = ("slab", "sec")
    slabs, secs = lax.axis_size("slab"), lax.axis_size("sec")
    devices = slabs * secs
    rows, own = source.shape
    modes = fine_prolong.shape[2]
    section_rows = coarse_blocks.shape[3]
    width = section_prolong.shape[2]
    count = section_rows // LANES
    blocks = count + 2 * EXT
    halo = EXT * LANES
    section = lax.axis_index("slab")
    place = lax.axis_index("sec")
    device = section * secs + place
    roll = ((section + LANES - 1) * width) % LANES
    from_left = (place < secs // 2).astype(jnp.int32)
    where = jnp.stack([place % 2, device * own, section * section_rows, place, roll, from_left]).astype(jnp.int32)

    prolong = jnp.transpose(fine_prolong, (0, 2, 1, 3))
    odd_swap = [(i, i + 1) for i in range(1, devices - 1, 2)] + [(i + 1, i) for i in range(1, devices - 1, 2)]
    even_swap = [(i, i ^ 1) for i in range(devices)]
    pairs = [[2 * i, 2 * i + 1] for i in range(secs // 2)]
    reach = [c for c in range(secs // 2) if c < EXT]
    edge_moves = [(s * secs + c, (s + 1) * secs + c) for s in range(slabs - 1) for c in reach]
    edge_moves += [((s + 1) * secs + secs - 1 - c, s * secs + secs - 1 - c) for s in range(slabs - 1) for c in reach]

    def nearby(field):
        odd = lax.ppermute(field, both, odd_swap)
        pair = lax.all_gather(field, "sec", axis_index_groups=pairs, axis=0)
        return pair, odd

    def beside(value, step):
        return lax.ppermute(value, "slab", [(i, i + step) for i in range(max(0, -step), min(slabs, slabs - step))])

    fine = struct(rows, own)
    work = [pltpu.VMEM((3, rows, own), F32), pltpu.VMEM((3, rows, own), F32), pltpu.VMEM((rows, own), F32)]
    inverse, start = call(first_body, [fine, fine], [VMEM] * 2)(fine_blocks, source)

    side = struct(3 * modes * SUB + SUB + width * (coarsest_inverse.shape[1] // halo), halo)
    low, high, fine_pack = call(pack_body, [side, side, struct(3 * modes * rows + SUB, own)], [SMEM] + [VMEM] * 5)(
        where, coarse_blocks, coarse_pattern, coarsest_inverse, prolong, prolong_pattern
    )
    left_data, right_data = beside(high, 1), beside(low, -1)
    odd_prolong = lax.ppermute(fine_pack, both, odd_swap)
    even_prolong = lax.ppermute(fine_pack, both, even_swap)
    matrix, offset, coarse_inverse = call(
        setup_body,
        [struct(blocks, 3, modes, SUB, LANES), struct(blocks, SUB, LANES, dtype=jnp.int32), struct(blocks, SUB, LANES)],
        [SMEM] + [VMEM] * 4,
    )(where, left_data, right_data, coarse_blocks, coarse_pattern)

    def step(body, outs, near, *rest):
        return call(body, outs, [SMEM] + [VMEM] * (4 + len(rest)), work)(where, *near, fine_blocks, fine_pattern, *rest)

    coarse = struct(blocks, SUB, LANES)
    ends = struct(SPILL, SUB, LANES)
    line = pltpu.VMEM((blocks + 2, SUB, LANES), F32)
    for cycle in range(CYCLES):
        if cycle == 0:
            change = field = start
        else:
            change, field = step(field_body, [fine, fine], nearby(solution), source, inverse)
        solution = step(solution_body, [fine], nearby(field), source, inverse, change)[0]
        near = nearby(solution)
        sums = step(restrict_body, [struct(secs, SUB, 3 * LANES)], near, source, prolong, prolong_pattern)[0]
        parts = lax.all_to_all(sums, "sec", 0, 0, tiled=True)
        low, everything, high = call(gather_body, [ends, struct(secs + 2, SUB, LANES), ends], [VMEM])(parts)
        below, above = beside(high, 1), beside(low, -1)
        rhs, coarse_sol, top = call(
            coarse_down_body, [coarse, coarse, struct(slabs, LANES)], [SMEM] + [VMEM] * 7, [line, line]
        )(where, everything, below, above, matrix, offset, coarse_inverse, section_prolong)
        tops = lax.all_to_all(top, "slab", 0, 0, tiled=True)
        middle, edge = call(
            top_body,
            [struct(count, SUB, LANES), struct(EXT, SUB, LANES)],
            [SMEM] + [VMEM] * 6,
            [pltpu.VMEM((3 * width, LANES), F32)],
        )(where, tops, left_data, coarsest_inverse, right_data, coarse_sol, section_prolong)
        edge = lax.ppermute(edge, both, edge_moves)
        change, field = call(up_body, [fine, fine], [SMEM] + [VMEM] * 16, [line, line, line] + work)(
            where, middle, edge, rhs, matrix, offset, coarse_inverse, *near, prolong, even_prolong, odd_prolong, prolong_pattern, fine_blocks, fine_pattern, source, inverse
        )
        solution = step(solution_body, [fine], nearby(field), source, inverse, change)[0]
    return solution


def solution(mesh):
    in_specs = (
        P(None, ("slab", "sec")),
        P(None, None, None, ("slab", "sec")),
        P(None, ("slab", "sec")),
        P(None, None, None, ("slab", "sec")),
        P(None, ("slab", "sec")),
        P(None, None, None, "slab"),
        P(None, "slab"),
        P(None, None, None, "slab"),
        P("slab", None),
    )
    out_specs = P(None, ("slab", "sec"))
    return jax.shard_map(shards, mesh=mesh, in_specs=in_specs, out_specs=out_specs, check_vma=False)
```

```python
import jax
import jax.numpy as jnp
from jax import lax
from jax.experimental import pallas as pl
from jax.experimental.pallas import tpu as pltpu
from jax.sharding import PartitionSpec as P

CYCLES = 2
KEEP = 1.0 / 7.0
FRESH = 8.0 / 7.0
LANES = 128
SUB = 8
EXT = 3
SPILL = EXT + 1
F32 = jnp.float32
BF16 = jnp.bfloat16
VMEM = pl.BlockSpec(memory_space=pltpu.VMEM)
SMEM = pl.BlockSpec(memory_space=pltpu.SMEM)


def call(body, outs, in_specs, scratch=(), flops=1 << 20, moved=1 << 20):
    return pl.pallas_call(
        body,
        out_shape=outs,
        in_specs=in_specs,
        out_specs=[VMEM] * len(outs),
        scratch_shapes=list(scratch),
        compiler_params=pltpu.CompilerParams(vmem_limit_bytes=24 << 20),
        cost_estimate=pl.CostEstimate(flops=flops, bytes_accessed=moved, transcendentals=0),
    )


def struct(*shape, dtype=F32):
    return jax.ShapeDtypeStruct(shape, dtype)


def take(x, lane):
    return jnp.take_along_axis(x, lane, axis=1, mode="promise_in_bounds")


def pick(three, target):
    lane = jnp.broadcast_to(target & (LANES - 1), three[0].shape)
    block = jnp.broadcast_to((target + LANES) >> 7, three[0].shape)
    a, b, c = (take(x, lane) for x in three)
    return jnp.where(block == 0, a, jnp.where(block == 1, b, c))


def fold_rows(terms):
    row = lax.broadcasted_iota(jnp.int32, (SUB, LANES), 0)
    for step in (4, 2, 1):
        high = (row & step) != 0
        half = len(terms) // 2
        folded = []
        for i in range(half):
            low_sum = terms[i] + pltpu.roll(terms[i], SUB - step, 0)
            high_sum = terms[i + half] + pltpu.roll(terms[i + half], step, 0)
            folded.append(jnp.where(high, high_sum, low_sum))
        terms = folded
    return terms[0]


def split3(x):
    high = x.astype(BF16)
    rest = x - high.astype(F32)
    middle = rest.astype(BF16)
    low = (rest - middle.astype(F32)).astype(BF16)
    return high, middle, low


def lanes_dot(a, b):
    return lax.dot_general(a, b, (((1,), (1,)), ((), ())), preferred_element_type=F32)


def load_halo(where_ref, pair_ref, odd_ref, ext):
    parity = where_ref[0]
    ext[1] = pair_ref[parity]
    ext[2 - 2 * parity] = pair_ref[1 - parity]
    ext[2 * parity] = odd_ref[...]


def product_rows(matrix_ref, ks, picked, out, before=None):
    rows = out.shape[0]

    def group(g, carry):
        part = pl.ds(pl.multiple_of(g * SUB, SUB), SUB)
        terms = []
        for p in range(SUB):
            total = None
            for k in ks:
                block = matrix_ref[k, g * SUB + p].astype(F32)
                product = jnp.sum((block * picked[k][...]).reshape(rows // SUB, SUB, LANES), axis=0)
                total = product if total is None else total + product
            terms.append(total)
        value = fold_rows(terms)
        out[part, :] = value if before is None else value + before[part, :]
        return carry

    lax.fori_loop(0, rows // SUB, group, 0)


def own_body(matrix_ref, field_ref, out_ref):
    product_rows(matrix_ref, (0,), [field_ref], out_ref)


def fine_product(where_ref, matrix_ref, pattern_ref, ext, picked, out, before=None):
    rows = out.shape[0]
    base = where_ref[1]
    for k in (1, 2):
        target = pattern_ref[k : k + 1, :] - base
        lane = jnp.broadcast_to(target & (LANES - 1), (SUB, LANES))
        block = jnp.broadcast_to((target + LANES) >> 7, (SUB, LANES))
        for t in range(rows // SUB):
            part = pl.ds(t * SUB, SUB)
            a, b, c = (take(ext[i, part, :], lane) for i in range(3))
            picked[k - 1, part, :] = jnp.where(block == 0, a, jnp.where(block == 1, b, c))

    near = {1: picked.at[0], 2: picked.at[1]}
    if before is None:
        near[0] = ext.at[1]
    product_rows(matrix_ref, sorted(near), near, out, before)


def first_body(matrix_ref, source_ref, inverse_ref, field_ref):
    rows = source_ref.shape[0]
    row = lax.broadcasted_iota(jnp.int32, (SUB, LANES), 0)
    for g in range(rows // SUB):
        part = pl.ds(g * SUB, SUB)
        diagonal = jnp.zeros((SUB, LANES), F32)
        for p in range(SUB):
            entry = matrix_ref[0, g * SUB + p].astype(F32)[g * SUB : (g + 1) * SUB]
            diagonal = jnp.where(row == p, entry, diagonal)
        inverse = 1.0 / diagonal
        inverse_ref[part, :] = inverse
        field_ref[part, :] = inverse * source_ref[part, :]


def field_body(where_ref, pair_ref, odd_ref, own_ref, matrix_ref, pattern_ref, source_ref, inverse_ref, change_ref, field_ref, ext, picked, out):
    load_halo(where_ref, pair_ref, odd_ref, ext)
    fine_product(where_ref, matrix_ref, pattern_ref, ext, picked, out, own_ref)
    change = inverse_ref[...] * (source_ref[...] - out[...])
    change_ref[...] = change
    field_ref[...] = ext[1] + change


def solution_body(where_ref, pair_ref, odd_ref, own_ref, matrix_ref, pattern_ref, source_ref, inverse_ref, change_ref, field_ref, ext, picked, out):
    load_halo(where_ref, pair_ref, odd_ref, ext)
    fine_product(where_ref, matrix_ref, pattern_ref, ext, picked, out, own_ref)
    second = KEEP * change_ref[...] + FRESH * inverse_ref[...] * (source_ref[...] - out[...])
    field_ref[...] = ext[1] + second


def restrict_body(where_ref, pair_ref, odd_ref, own_ref, matrix_ref, pattern_ref, source_ref, prolong_ref, targets_ref, sums_ref, ext, picked, out):
    load_halo(where_ref, pair_ref, odd_ref, ext)
    fine_product(where_ref, matrix_ref, pattern_ref, ext, picked, out, own_ref)
    residual = source_ref[...] - out[...]
    modes = prolong_ref.shape[1]
    rows = residual.shape[0]
    slots = lax.broadcasted_iota(jnp.int32, (3 * LANES, LANES), 0)
    total = None
    for k in range(3):
        terms = []
        for m in range(SUB):
            if m < modes:
                product = prolong_ref[k, m].astype(F32) * residual
                terms.append(jnp.sum(product.reshape(rows // SUB, SUB, LANES), axis=0))
            else:
                terms.append(jnp.zeros((SUB, LANES), F32))
        parts = split3(fold_rows(terms))
        target = targets_ref[k : k + 1, :] - where_ref[1] + LANES
        hot = (slots == target).astype(F32).astype(BF16)
        stacked = jnp.concatenate([p.astype(F32) for p in parts] + [jnp.zeros((SUB, LANES), F32)], axis=0)
        spread = lanes_dot(stacked.astype(BF16), hot)
        total = spread if total is None else total + spread
    sums = total[0:SUB] + total[SUB : 2 * SUB] + total[2 * SUB : 3 * SUB]
    for i in range(sums_ref.shape[0]):
        sums_ref[i] = sums


def pack_body(where_ref, blocks_ref, pattern_ref, top_ref, prolong_ref, targets_ref, low_ref, high_ref, fine_ref):
    modes = blocks_ref.shape[1]
    total = blocks_ref.shape[3]
    halo = low_ref.shape[1]
    width = top_ref.shape[0]
    column = lax.broadcasted_iota(jnp.int32, (1, halo), 1)
    for out, at in ((low_ref, 0), (high_ref, total - halo)):
        cols = pl.ds(at, halo)
        for k in range(3):
            for p in range(modes):
                row = (k * modes + p) * SUB
                out[row : row + modes, :] = blocks_ref[k, p, :, cols].astype(F32)
        row = 3 * modes * SUB
        for k in range(2):
            offset = pattern_ref[k + 1 : k + 2, cols] - (where_ref[2] + at) - column
            out[row + k : row + k + 1, :] = offset.astype(F32)
        row += SUB
        for i in range(top_ref.shape[1] // halo):
            out[row + i * width : row + (i + 1) * width, :] = top_ref[:, i * halo : (i + 1) * halo]
    rows = prolong_ref.shape[2]
    for k in range(3):
        for m in range(modes):
            at = (k * modes + m) * rows
            fine_ref[at : at + rows, :] = prolong_ref[k, m].astype(F32)
        at = 3 * modes * rows + k
        fine_ref[at : at + 1, :] = targets_ref[k : k + 1, :].astype(F32)


def setup_body(where_ref, left_ref, right_ref, blocks_ref, pattern_ref, matrix_ref, offset_ref, inverse_ref):
    modes = blocks_ref.shape[1]
    count = blocks_ref.shape[3] // LANES
    matrix_ref[...] = jnp.zeros_like(matrix_ref)
    row = lax.broadcasted_iota(jnp.int32, (SUB, LANES), 0)
    column = lax.broadcasted_iota(jnp.int32, (1, LANES), 1)
    at_offset = 3 * modes * SUB
    for b in range(count + 2 * EXT):
        inner = EXT <= b < EXT + count
        side = left_ref if b < EXT else right_ref
        at = b - EXT if inner else (b if b < EXT else b - EXT - count)
        cols = pl.ds(at * LANES, LANES)
        diagonal = jnp.zeros((SUB, LANES), F32)
        for k in range(3):
            for p in range(modes):
                if inner:
                    entry = blocks_ref[k, p, :, cols].astype(F32)
                else:
                    entry = side[pl.ds((k * modes + p) * SUB, modes), cols]
                matrix_ref[b, k, p, 0:modes, :] = entry
                if k == 0:
                    diagonal = jnp.where(row == p, entry[p : p + 1, :], diagonal)
        inverse_ref[b] = jnp.where(row < modes, 1.0 / jnp.where(row < modes, diagonal, 1.0), 0.0)
        for k in range(2):
            if inner:
                offset = pattern_ref[k + 1 : k + 2, cols] - (where_ref[2] + at * LANES) - column
            else:
                offset = side[at_offset + k : at_offset + k + 1, cols].astype(jnp.int32)
            offset_ref[b, k : k + 1, :] = jnp.clip(offset, -LANES, LANES)


def coarse_product(matrix_ref, offset_ref, field, b):
    lanes = lax.broadcasted_iota(jnp.int32, (1, LANES), 1)
    three = [field[b + i] for i in range(3)]
    picked = [three[1]] + [pick(three, lanes + offset_ref[b, k : k + 1, :]) for k in range(2)]
    terms = []
    modes = matrix_ref.shape[2]
    for p in range(SUB):
        if p < modes:
            terms.append(sum(matrix_ref[b, k, p] * picked[k] for k in range(3)))
        else:
            terms.append(jnp.zeros((SUB, LANES), F32))
    return fold_rows(terms)


def by_two(first, number, body):
    def trip(i, carry):
        body(first + 2 * i)
        body(first + 2 * i + 1)
        return carry

    lax.fori_loop(0, number // 2, trip, 0)
    if number % 2:
        body(first + number - 1)


def gather_body(parts_ref, ends_ref, all_ref):
    count = parts_ref.shape[0]
    blocks = []
    for b in range(-1, count + 1):
        total = None
        for device in (b - 1, b, b + 1):
            if 0 <= device < count:
                at = (b - device + 1) * LANES
                term = parts_ref[device, :, at : at + LANES]
                total = term if total is None else total + term
        blocks.append(total)
    for i, block in enumerate(blocks):
        all_ref[i] = block
    for i in range(SPILL):
        ends_ref[i] = blocks[i]
        ends_ref[SPILL + i] = blocks[count + 2 - SPILL + i]


def coarse_down_body(where_ref, all_ref, even_ref, odd_ref, matrix_ref, offset_ref, inverse_ref, section_ref, rhs_ref, sol_ref, top_ref, field, other):
    total = matrix_ref.shape[0]
    count = total - 2 * EXT
    modes = matrix_ref.shape[2]
    width = section_ref.shape[2]
    zero = jnp.zeros((SUB, LANES), F32)
    parity = where_ref[6]
    for b in range(total):
        terms = []
        at = b - (EXT - 1)
        if 0 <= at < count + 2:
            terms.append(all_ref[at])
        if b < SPILL:
            terms.append(jnp.where(parity == 0, odd_ref[SPILL + b], even_ref[1 - parity, SPILL + b]))
        if b >= total - SPILL:
            i = b - (total - SPILL)
            terms.append(jnp.where(parity == 0, even_ref[1 - parity, i], odd_ref[i]))
        value = sum(terms[1:], terms[0])
        rhs_ref[b] = value
        field[b + 1] = inverse_ref[b] * value
    for edge in (0, total + 1):
        field[edge] = zero
        other[edge] = zero

    def first(b):
        start = field[b + 1]
        second = KEEP * start + FRESH * inverse_ref[b] * (rhs_ref[b] - coarse_product(matrix_ref, offset_ref, field, b))
        other[b + 1] = start + second
        sol_ref[b] = start + second

    by_two(EXT - 1, count + 2, first)

    def down(i, carry):
        for j in range(2):
            b = 2 * i + j + EXT
            residual = rhs_ref[b] - coarse_product(matrix_ref, offset_ref, other, b)
            cols = pl.ds(pl.multiple_of((2 * i + j) * LANES, LANES), LANES)
            out = []
            for k in range(3):
                value = carry[k]
                for p in range(modes):
                    value = value + section_ref[k, p, :, cols].astype(F32) * residual[p : p + 1, :]
                out.append(value)
            carry = out
        return tuple(carry)

    sums = lax.fori_loop(0, count // 2, down, tuple(jnp.zeros((width, LANES), F32) for _ in range(3)))
    stacked = jnp.concatenate(list(sums) + [jnp.zeros((LANES - 3 * width, LANES), F32)], axis=0)
    ones = jnp.ones((16, LANES), BF16)
    row = sum(lanes_dot(ones, part) for part in split3(stacked))
    top_ref[...] = jnp.broadcast_to(pltpu.roll(row, where_ref[4], 1)[0:1], top_ref.shape)


def top_body(where_ref, parts_ref, left_ref, top_inverse_ref, right_ref, sol_ref, section_ref, field_ref, edge_ref, column):
    count, modes, width = section_ref.shape[3] // LANES, section_ref.shape[1], section_ref.shape[2]
    sections = parts_ref.shape[0]
    chunk_count = sections * width // LANES
    sub = lax.broadcasted_iota(jnp.int32, (SUB, LANES), 0)
    lane = lax.broadcasted_iota(jnp.int32, (SUB, LANES), 1)
    chunks = [None] * chunk_count
    for tile in range(sections // SUB):
        first = (sub + (tile * SUB - 1)) * width
        chunk = (first + ((lane - first) & (LANES - 1))) >> 7
        value = parts_ref[tile * SUB : (tile + 1) * SUB, :]
        low = (tile * SUB - 1) * width
        for q in range(max(0, low // LANES), min(chunk_count, (low + (SUB + 2) * width) // LANES + 1)):
            term = jnp.where(chunk == q, value, 0.0)
            chunks[q] = term if chunks[q] is None else chunks[q] + term
    chunks = [jnp.sum(c, axis=0, keepdims=True) for c in chunks]
    halo = left_ref.shape[1]
    at_top = 3 * modes * SUB + SUB
    answers = []
    for side in range(3):
        total = None
        for q in range(chunk_count):
            if side == 1:
                part = top_inverse_ref[:, q * LANES : (q + 1) * LANES]
            else:
                ref = left_ref if side == 0 else right_ref
                i, at = divmod(q * LANES, halo)
                part = ref[pl.ds(at_top + i * width, width), pl.ds(at, LANES)]
            term = part * chunks[q]
            total = term if total is None else total + term
        answers.append(jnp.sum(total, axis=1, keepdims=True))
    for side in range(3):
        column[side * width : (side + 1) * width, :] = jnp.broadcast_to(answers[side], (width, LANES))
    zero = jnp.zeros((SUB, LANES), F32)

    def correct(b):
        cols = pl.ds(pl.multiple_of(b * LANES, LANES), LANES)
        terms = []
        for p in range(SUB):
            if p < modes:
                value = sum(section_ref[k, p, :, cols].astype(F32) * column[k * width : (k + 1) * width, :] for k in range(3))
                terms.append(jnp.sum(value.reshape(width // SUB, SUB, LANES), axis=0))
            else:
                terms.append(zero)
        field_ref[b] = sol_ref[b + EXT] + fold_rows(terms)

    by_two(0, count, correct)
    start = jnp.where(where_ref[5] > 0, count - EXT, 0)
    for i in range(EXT):
        edge_ref[i] = field_ref[start + i]


def up_body(
    where_ref,
    middle_ref,
    edge_ref,
    rhs_ref,
    matrix_ref,
    offset_ref,
    inverse_ref,
    pair_ref,
    odd_ref,
    prolong_ref,
    even_prolong_ref,
    odd_prolong_ref,
    targets_ref,
    fine_matrix_ref,
    fine_pattern_ref,
    source_ref,
    fine_inverse_ref,
    change_ref,
    field_ref,
    field,
    other,
    final,
    ext,
    picked,
    out,
):
    total = matrix_ref.shape[0]
    count = total - 2 * EXT
    modes = matrix_ref.shape[2]
    zero = jnp.zeros((SUB, LANES), F32)
    from_left = where_ref[5] > 0
    for i in range(EXT):
        field[1 + i] = jnp.where(from_left, edge_ref[i], 0.0)
        field[1 + EXT + count + i] = jnp.where(from_left, 0.0, edge_ref[i])
    for i in range(count):
        field[1 + EXT + i] = middle_ref[i]
    for edge in (0, total + 1):
        field[edge] = zero
        other[edge] = zero

    def smooth_first(b):
        change = inverse_ref[b] * (rhs_ref[b] - coarse_product(matrix_ref, offset_ref, field, b))
        final[b] = change
        other[b + 1] = field[b + 1] + change

    middle = where_ref[3] + EXT
    by_two(middle - 3, 7, smooth_first)

    def smooth_second(b):
        second = KEEP * final[b] + FRESH * inverse_ref[b] * (rhs_ref[b] - coarse_product(matrix_ref, offset_ref, other, b))
        final[b] = other[b + 1] + second

    by_two(middle - 2, 5, smooth_second)
    load_halo(where_ref, pair_ref, odd_ref, ext)
    rows = ext.shape[1]
    parity = where_ref[0]
    for which in range(3):
        block = (1, 2 - 2 * parity, 2 * parity)[which]
        side = (None, even_prolong_ref, odd_prolong_ref)[which]
        at = where_ref[3] + EXT + block - 2
        three = [final[at + i] for i in range(3)]
        terms = []
        for k in range(3):
            if which == 0:
                target = targets_ref[k : k + 1, :] - where_ref[1]
            else:
                row = 3 * modes * rows + k
                target = side[row : row + 1, :].astype(jnp.int32) - (where_ref[1] + (block - 1) * LANES)
            terms.append(three[1] if k == 0 else pick(three, target))
        for t in range(rows // SUB):
            part = pl.ds(t * SUB, SUB)
            value = ext[block, part, :]
            for k in range(3):
                for m in range(modes):
                    if which == 0:
                        weight = prolong_ref[k, m, part, :].astype(F32)
                    else:
                        weight = side[pl.ds((k * modes + m) * rows + t * SUB, SUB), :]
                    value = value + weight * terms[k][m : m + 1, :]
            ext[block, part, :] = value
    fine_product(where_ref, fine_matrix_ref, fine_pattern_ref, ext, picked, out)
    change = fine_inverse_ref[...] * (source_ref[...] - out[...])
    change_ref[...] = change
    field_ref[...] = ext[1] + change


def shards(
    source,
    fine_blocks,
    fine_pattern,
    fine_prolong,
    prolong_pattern,
    coarse_blocks,
    coarse_pattern,
    section_prolong,
    coarsest_inverse,
):
    both = ("slab", "sec")
    slabs, secs = lax.axis_size("slab"), lax.axis_size("sec")
    devices = slabs * secs
    rows, own = source.shape
    modes = fine_prolong.shape[2]
    section_rows = coarse_blocks.shape[3]
    width = section_prolong.shape[2]
    count = section_rows // LANES
    blocks = count + 2 * EXT
    halo = EXT * LANES
    section = lax.axis_index("slab")
    place = lax.axis_index("sec")
    device = section * secs + place
    roll = ((section + LANES - 1) * width) % LANES
    from_left = (place < secs // 2).astype(jnp.int32)
    where = jnp.stack([place % 2, device * own, section * section_rows, place, roll, from_left, section % 2]).astype(jnp.int32)

    prolong = jnp.transpose(fine_prolong, (0, 2, 1, 3))
    odd_swap = [(i, i + 1) for i in range(1, devices - 1, 2)] + [(i + 1, i) for i in range(1, devices - 1, 2)]
    even_swap = [(i, i ^ 1) for i in range(devices)]
    pairs = [[2 * i, 2 * i + 1] for i in range(secs // 2)]
    reach = [c for c in range(secs // 2) if c < EXT]
    edge_moves = [(s * secs + c, (s + 1) * secs + c) for s in range(slabs - 1) for c in reach]
    edge_moves += [((s + 1) * secs + secs - 1 - c, s * secs + secs - 1 - c) for s in range(slabs - 1) for c in reach]

    slab_odd = [(i, i + 1) for i in range(1, slabs - 1, 2)] + [(i + 1, i) for i in range(1, slabs - 1, 2)]
    slab_pairs = [[2 * i, 2 * i + 1] for i in range(slabs // 2)]

    def nearby(field):
        odd = lax.ppermute(field, both, odd_swap)
        pair = lax.all_gather(field, "sec", axis_index_groups=pairs, axis=0)
        return pair, odd, call(own_body, [fine], [VMEM] * 2)(fine_blocks, field)[0]

    def beside(value, step):
        return lax.ppermute(value, "slab", [(i, i + step) for i in range(max(0, -step), min(slabs, slabs - step))])

    fine = struct(rows, own)
    work = [pltpu.VMEM((3, rows, own), F32), pltpu.VMEM((2, rows, own), F32), pltpu.VMEM((rows, own), F32)]
    inverse, start = call(first_body, [fine, fine], [VMEM] * 2)(fine_blocks, source)

    first_near = nearby(start)
    held = lax.optimization_barrier((first_near[0], coarse_blocks, coarse_pattern, coarsest_inverse, prolong, prolong_pattern))
    side = struct(3 * modes * SUB + SUB + width * (coarsest_inverse.shape[1] // halo), halo)
    low, high, fine_pack = call(pack_body, [side, side, struct(3 * modes * rows + SUB, own)], [SMEM] + [VMEM] * 5)(
        where, *held[1:]
    )
    first_near = (held[0], *first_near[1:])
    left_data, right_data = beside(high, 1), beside(low, -1)
    odd_prolong = lax.ppermute(fine_pack, both, odd_swap)
    even_prolong = lax.ppermute(fine_pack, both, even_swap)
    matrix, offset, coarse_inverse = call(
        setup_body,
        [struct(blocks, 3, modes, SUB, LANES), struct(blocks, SUB, LANES, dtype=jnp.int32), struct(blocks, SUB, LANES)],
        [SMEM] + [VMEM] * 4,
    )(where, left_data, right_data, coarse_blocks, coarse_pattern)

    def step(body, outs, near, *rest):
        return call(body, outs, [SMEM] + [VMEM] * (5 + len(rest)), work)(where, *near, fine_blocks, fine_pattern, *rest)

    coarse = struct(blocks, SUB, LANES)
    line = pltpu.VMEM((blocks + 2, SUB, LANES), F32)
    for cycle in range(CYCLES):
        if cycle == 0:
            change, near = start, first_near
        else:
            change, field = step(field_body, [fine, fine], nearby(solution), source, inverse)
            near = nearby(field)
        solution = step(solution_body, [fine], near, source, inverse, change)[0]
        near = nearby(solution)
        sums = step(restrict_body, [struct(secs, SUB, 3 * LANES)], near, source, prolong, prolong_pattern)[0]
        parts = lax.all_to_all(sums, "sec", 0, 0, tiled=True)
        ends, everything = call(gather_body, [struct(2 * SPILL, SUB, LANES), struct(secs + 2, SUB, LANES)], [VMEM])(parts)
        odd = lax.ppermute(ends, "slab", slab_odd)
        even = lax.all_gather(ends, "slab", axis_index_groups=slab_pairs, axis=0)
        rhs, coarse_sol, top = call(
            coarse_down_body, [coarse, coarse, struct(slabs, LANES)], [SMEM] + [VMEM] * 7, [line, line]
        )(where, everything, even, odd, matrix, offset, coarse_inverse, section_prolong)
        tops = lax.all_to_all(top, "slab", 0, 0, tiled=True)
        middle, edge = call(
            top_body,
            [struct(count, SUB, LANES), struct(EXT, SUB, LANES)],
            [SMEM] + [VMEM] * 6,
            [pltpu.VMEM((3 * width, LANES), F32)],
        )(where, tops, left_data, coarsest_inverse, right_data, coarse_sol, section_prolong)
        edge = lax.ppermute(edge, both, edge_moves)
        change, field = call(up_body, [fine, fine], [SMEM] + [VMEM] * 16, [line, line, line] + work)(
            where, middle, edge, rhs, matrix, offset, coarse_inverse, *near[:2], prolong, even_prolong, odd_prolong, prolong_pattern, fine_blocks, fine_pattern, source, inverse
        )
        solution = step(solution_body, [fine], nearby(field), source, inverse, change)[0]
    return solution


def solution(mesh):
    in_specs = (
        P(None, ("slab", "sec")),
        P(None, None, None, ("slab", "sec")),
        P(None, ("slab", "sec")),
        P(None, None, None, ("slab", "sec")),
        P(None, ("slab", "sec")),
        P(None, None, None, "slab"),
        P(None, "slab"),
        P(None, None, None, "slab"),
        P("slab", None),
    )
    out_specs = P(None, ("slab", "sec"))
    return jax.shard_map(shards, mesh=mesh, in_specs=in_specs, out_specs=out_specs, check_vma=False)
```

```python
import jax
import jax.numpy as jnp
from jax import lax
from jax.experimental import pallas as pl
from jax.experimental.pallas import tpu as pltpu
from jax.sharding import PartitionSpec as P

CYCLES = 2
KEEP = 1.0 / 7.0
FRESH = 8.0 / 7.0
LANES = 128
SUB = 8
EXT = 4
FAR = 3
SPILL = EXT + 1
F32 = jnp.float32
BF16 = jnp.bfloat16
VMEM = pl.BlockSpec(memory_space=pltpu.VMEM)
SMEM = pl.BlockSpec(memory_space=pltpu.SMEM)


def call(body, outs, in_specs, scratch=(), flops=1 << 20, moved=1 << 20):
    return pl.pallas_call(
        body,
        out_shape=outs,
        in_specs=in_specs,
        out_specs=[VMEM] * len(outs),
        scratch_shapes=list(scratch),
        compiler_params=pltpu.CompilerParams(vmem_limit_bytes=24 << 20),
        cost_estimate=pl.CostEstimate(flops=flops, bytes_accessed=moved, transcendentals=0),
    )


def struct(*shape, dtype=F32):
    return jax.ShapeDtypeStruct(shape, dtype)


def take(x, lane):
    return jnp.take_along_axis(x, lane, axis=1, mode="promise_in_bounds")


def pick(three, target):
    lane = jnp.broadcast_to(target & (LANES - 1), three[0].shape)
    block = jnp.broadcast_to((target + LANES) >> 7, three[0].shape)
    a, b, c = (take(x, lane) for x in three)
    return jnp.where(block == 0, a, jnp.where(block == 1, b, c))


def fold_rows(terms):
    row = lax.broadcasted_iota(jnp.int32, (SUB, LANES), 0)
    for step in (4, 2, 1):
        high = (row & step) != 0
        half = len(terms) // 2
        folded = []
        for i in range(half):
            low_sum = terms[i] + pltpu.roll(terms[i], SUB - step, 0)
            high_sum = terms[i + half] + pltpu.roll(terms[i + half], step, 0)
            folded.append(jnp.where(high, high_sum, low_sum))
        terms = folded
    return terms[0]


def split3(x):
    high = x.astype(BF16)
    rest = x - high.astype(F32)
    middle = rest.astype(BF16)
    low = (rest - middle.astype(F32)).astype(BF16)
    return high, middle, low


def lanes_dot(a, b):
    return lax.dot_general(a, b, (((1,), (1,)), ((), ())), preferred_element_type=F32)


def load_halo(where_ref, pair_ref, odd_ref, ext):
    parity = where_ref[0]
    ext[1] = pair_ref[parity]
    ext[2 - 2 * parity] = pair_ref[1 - parity]
    ext[2 * parity] = odd_ref[...]


def product_rows(matrix_ref, ks, picked, out, before=None):
    rows = out.shape[0]

    def group(g, carry):
        part = pl.ds(pl.multiple_of(g * SUB, SUB), SUB)
        terms = []
        for p in range(SUB):
            total = None
            for k in ks:
                block = matrix_ref[k, g * SUB + p].astype(F32)
                product = jnp.sum((block * picked[k][...]).reshape(rows // SUB, SUB, LANES), axis=0)
                total = product if total is None else total + product
            terms.append(total)
        value = fold_rows(terms)
        out[part, :] = value if before is None else value + before[part, :]
        return carry

    lax.fori_loop(0, rows // SUB, group, 0)


def own_body(matrix_ref, field_ref, out_ref):
    product_rows(matrix_ref, (0,), [field_ref], out_ref)


def fine_product(where_ref, matrix_ref, pattern_ref, ext, picked, out, before=None):
    rows = out.shape[0]
    base = where_ref[1]
    for k in (1, 2):
        target = pattern_ref[k : k + 1, :] - base
        lane = jnp.broadcast_to(target & (LANES - 1), (SUB, LANES))
        block = jnp.broadcast_to((target + LANES) >> 7, (SUB, LANES))
        for t in range(rows // SUB):
            part = pl.ds(t * SUB, SUB)
            a, b, c = (take(ext[i, part, :], lane) for i in range(3))
            picked[k - 1, part, :] = jnp.where(block == 0, a, jnp.where(block == 1, b, c))

    near = {1: picked.at[0], 2: picked.at[1]}
    if before is None:
        near[0] = ext.at[1]
    product_rows(matrix_ref, sorted(near), near, out, before)


def first_body(matrix_ref, source_ref, inverse_ref, field_ref):
    rows = source_ref.shape[0]
    row = lax.broadcasted_iota(jnp.int32, (SUB, LANES), 0)
    for g in range(rows // SUB):
        part = pl.ds(g * SUB, SUB)
        diagonal = jnp.zeros((SUB, LANES), F32)
        for p in range(SUB):
            entry = matrix_ref[0, g * SUB + p].astype(F32)[g * SUB : (g + 1) * SUB]
            diagonal = jnp.where(row == p, entry, diagonal)
        inverse = 1.0 / diagonal
        inverse_ref[part, :] = inverse
        field_ref[part, :] = inverse * source_ref[part, :]


def field_body(where_ref, pair_ref, odd_ref, own_ref, matrix_ref, pattern_ref, source_ref, inverse_ref, change_ref, field_ref, ext, picked, out):
    load_halo(where_ref, pair_ref, odd_ref, ext)
    fine_product(where_ref, matrix_ref, pattern_ref, ext, picked, out, own_ref)
    change = inverse_ref[...] * (source_ref[...] - out[...])
    change_ref[...] = change
    field_ref[...] = ext[1] + change


def solution_body(where_ref, pair_ref, odd_ref, own_ref, matrix_ref, pattern_ref, source_ref, inverse_ref, change_ref, field_ref, ext, picked, out):
    load_halo(where_ref, pair_ref, odd_ref, ext)
    fine_product(where_ref, matrix_ref, pattern_ref, ext, picked, out, own_ref)
    second = KEEP * change_ref[...] + FRESH * inverse_ref[...] * (source_ref[...] - out[...])
    field_ref[...] = ext[1] + second


def restrict_body(where_ref, pair_ref, odd_ref, own_ref, matrix_ref, pattern_ref, source_ref, prolong_ref, targets_ref, sums_ref, ext, picked, out):
    load_halo(where_ref, pair_ref, odd_ref, ext)
    fine_product(where_ref, matrix_ref, pattern_ref, ext, picked, out, own_ref)
    residual = source_ref[...] - out[...]
    modes = prolong_ref.shape[1]
    rows = residual.shape[0]
    slots = lax.broadcasted_iota(jnp.int32, (3 * LANES, LANES), 0)
    total = None
    for k in range(3):
        terms = []
        for m in range(SUB):
            if m < modes:
                product = prolong_ref[k, m].astype(F32) * residual
                terms.append(jnp.sum(product.reshape(rows // SUB, SUB, LANES), axis=0))
            else:
                terms.append(jnp.zeros((SUB, LANES), F32))
        parts = split3(fold_rows(terms))
        target = targets_ref[k : k + 1, :] - where_ref[1] + LANES
        hot = (slots == target).astype(F32).astype(BF16)
        stacked = jnp.concatenate([p.astype(F32) for p in parts] + [jnp.zeros((SUB, LANES), F32)], axis=0)
        spread = lanes_dot(stacked.astype(BF16), hot)
        total = spread if total is None else total + spread
    sums = total[0:SUB] + total[SUB : 2 * SUB] + total[2 * SUB : 3 * SUB]
    for i in range(sums_ref.shape[0]):
        sums_ref[i] = sums


def pack_body(where_ref, blocks_ref, pattern_ref, top_ref, low_ref, high_ref):
    modes = blocks_ref.shape[1]
    total = blocks_ref.shape[3]
    halo = low_ref.shape[1]
    width = top_ref.shape[0]
    column = lax.broadcasted_iota(jnp.int32, (1, halo), 1)
    for out, at in ((low_ref, 0), (high_ref, total - halo)):
        cols = pl.ds(at, halo)
        for k in range(3):
            for p in range(modes):
                row = (k * modes + p) * SUB
                out[row : row + modes, :] = blocks_ref[k, p, :, cols].astype(F32)
        row = 3 * modes * SUB
        for k in range(2):
            offset = pattern_ref[k + 1 : k + 2, cols] - (where_ref[2] + at) - column
            out[row + k : row + k + 1, :] = offset.astype(F32)
        row += SUB
        for i in range(pl.cdiv(top_ref.shape[1], halo)):
            part = top_ref[:, i * halo : (i + 1) * halo]
            out[row + i * width : row + (i + 1) * width, 0 : part.shape[1]] = part


def pack_prolong_body(where_ref, prolong_ref, targets_ref, section_ref, fine_ref, far_ref):
    modes, rows = prolong_ref.shape[1:3]
    width, total = section_ref.shape[2:]
    for k in range(3):
        for m in range(modes):
            at = (k * modes + m) * rows
            fine_ref[at : at + rows, :] = prolong_ref[k, m].astype(F32)
        at = 3 * modes * rows + k
        fine_ref[at : at + 1, :] = targets_ref[k : k + 1, :].astype(F32)
    reach = far_ref.shape[1]
    cols = pl.ds(pl.multiple_of(where_ref[5] * (total - reach), LANES), reach)
    for k in range(3):
        for p in range(modes):
            at = (k * modes + p) * width
            far_ref[at : at + width, :] = section_ref[k, p, :, cols].astype(F32)


def setup_body(where_ref, left_ref, right_ref, blocks_ref, pattern_ref, matrix_ref, offset_ref, inverse_ref):
    modes = blocks_ref.shape[1]
    count = blocks_ref.shape[3] // LANES
    matrix_ref[...] = jnp.zeros_like(matrix_ref)
    row = lax.broadcasted_iota(jnp.int32, (SUB, LANES), 0)
    column = lax.broadcasted_iota(jnp.int32, (1, LANES), 1)
    at_offset = 3 * modes * SUB
    for b in range(count + 2 * EXT):
        inner = EXT <= b < EXT + count
        side = left_ref if b < EXT else right_ref
        at = b - EXT if inner else (b if b < EXT else b - EXT - count)
        cols = pl.ds(at * LANES, LANES)
        diagonal = jnp.zeros((SUB, LANES), F32)
        for k in range(3):
            for p in range(modes):
                if inner:
                    entry = blocks_ref[k, p, :, cols].astype(F32)
                else:
                    entry = side[pl.ds((k * modes + p) * SUB, modes), cols]
                matrix_ref[b, k, p, 0:modes, :] = entry
                if k == 0:
                    diagonal = jnp.where(row == p, entry[p : p + 1, :], diagonal)
        inverse_ref[b] = jnp.where(row < modes, 1.0 / jnp.where(row < modes, diagonal, 1.0), 0.0)
        for k in range(2):
            if inner:
                offset = pattern_ref[k + 1 : k + 2, cols] - (where_ref[2] + at * LANES) - column
            else:
                offset = side[at_offset + k : at_offset + k + 1, cols].astype(jnp.int32)
            offset_ref[b, k : k + 1, :] = jnp.clip(offset, -LANES, LANES)


def coarse_product(matrix_ref, offset_ref, field, b):
    lanes = lax.broadcasted_iota(jnp.int32, (1, LANES), 1)
    three = [field[b + i] for i in range(3)]
    picked = [three[1]] + [pick(three, lanes + offset_ref[b, k : k + 1, :]) for k in range(2)]
    terms = []
    modes = matrix_ref.shape[2]
    for p in range(SUB):
        if p < modes:
            terms.append(sum(matrix_ref[b, k, p] * picked[k] for k in range(3)))
        else:
            terms.append(jnp.zeros((SUB, LANES), F32))
    return fold_rows(terms)


def by_two(first, number, body):
    def trip(i, carry):
        body(first + 2 * i)
        body(first + 2 * i + 1)
        return carry

    lax.fori_loop(0, number // 2, trip, 0)
    if number % 2:
        body(first + number - 1)


def gather_body(parts_ref, ends_ref, all_ref):
    count = parts_ref.shape[0]
    blocks = []
    for b in range(-1, count + 1):
        total = None
        for device in (b - 1, b, b + 1):
            if 0 <= device < count:
                at = (b - device + 1) * LANES
                term = parts_ref[device, :, at : at + LANES]
                total = term if total is None else total + term
        blocks.append(total)
    for i, block in enumerate(blocks):
        all_ref[i] = block
    for i in range(SPILL):
        ends_ref[i] = blocks[i]
        ends_ref[SPILL + i] = blocks[count + 2 - SPILL + i]


def coarse_down_body(where_ref, all_ref, even_ref, odd_ref, matrix_ref, offset_ref, inverse_ref, section_ref, rhs_ref, sol_ref, top_ref, field, other):
    total = matrix_ref.shape[0]
    count = total - 2 * EXT
    modes = matrix_ref.shape[2]
    width = section_ref.shape[2]
    zero = jnp.zeros((SUB, LANES), F32)
    parity = where_ref[6]
    for b in range(total):
        terms = []
        at = b - (EXT - 1)
        if 0 <= at < count + 2:
            terms.append(all_ref[at])
        if b < SPILL:
            terms.append(jnp.where(parity == 0, odd_ref[SPILL + b], even_ref[1 - parity, SPILL + b]))
        if b >= total - SPILL:
            i = b - (total - SPILL)
            terms.append(jnp.where(parity == 0, even_ref[1 - parity, i], odd_ref[i]))
        value = sum(terms[1:], terms[0])
        rhs_ref[b] = value
        field[b + 1] = inverse_ref[b] * value
    for edge in (0, total + 1):
        field[edge] = zero
        other[edge] = zero

    def first(b):
        start = field[b + 1]
        second = KEEP * start + FRESH * inverse_ref[b] * (rhs_ref[b] - coarse_product(matrix_ref, offset_ref, field, b))
        other[b + 1] = start + second
        sol_ref[b] = start + second

    by_two(EXT - FAR, count + 2 * FAR, first)

    def down(i, carry):
        for j in range(2):
            b = 2 * i + j + EXT
            residual = rhs_ref[b] - coarse_product(matrix_ref, offset_ref, other, b)
            cols = pl.ds(pl.multiple_of((2 * i + j) * LANES, LANES), LANES)
            out = []
            for k in range(3):
                value = carry[k]
                for p in range(modes):
                    value = value + section_ref[k, p, :, cols].astype(F32) * residual[p : p + 1, :]
                out.append(value)
            carry = out
        return tuple(carry)

    sums = lax.fori_loop(0, count // 2, down, tuple(jnp.zeros((width, LANES), F32) for _ in range(3)))
    stacked = jnp.concatenate(list(sums) + [jnp.zeros((LANES - 3 * width, LANES), F32)], axis=0)
    ones = jnp.ones((16, LANES), BF16)
    row = sum(lanes_dot(ones, part) for part in split3(stacked))
    top_ref[...] = jnp.broadcast_to(pltpu.roll(row, where_ref[4], 1)[0:1], top_ref.shape)


def top_answers(parts_ref, rows_of, width, column, slots):
    sections = parts_ref.shape[0]
    chunk_count = sections * width // LANES
    sub = lax.broadcasted_iota(jnp.int32, (SUB, LANES), 0)
    lane = lax.broadcasted_iota(jnp.int32, (SUB, LANES), 1)
    chunks = [None] * chunk_count
    for tile in range(sections // SUB):
        first = (sub + (tile * SUB - 1)) * width
        chunk = (first + ((lane - first) & (LANES - 1))) >> 7
        value = parts_ref[tile * SUB : (tile + 1) * SUB, :]
        low = (tile * SUB - 1) * width
        for q in range(max(0, low // LANES), min(chunk_count, (low + (SUB + 2) * width) // LANES + 1)):
            term = jnp.where(chunk == q, value, 0.0)
            chunks[q] = term if chunks[q] is None else chunks[q] + term
    chunks = [jnp.sum(c, axis=0, keepdims=True) for c in chunks]
    for i, places in enumerate(slots):
        total = None
        for q in range(chunk_count):
            term = rows_of(i, q) * chunks[q]
            total = term if total is None else total + term
        answer = jnp.broadcast_to(jnp.sum(total, axis=1, keepdims=True), (width, LANES))
        for place in places:
            column[place * width : (place + 1) * width, :] = answer


def up_body(
    where_ref,
    parts_ref,
    left_ref,
    top_inverse_ref,
    right_ref,
    far_top_ref,
    section_ref,
    far_ref,
    sol_ref,
    rhs_ref,
    matrix_ref,
    offset_ref,
    inverse_ref,
    pair_ref,
    odd_ref,
    prolong_ref,
    even_prolong_ref,
    odd_prolong_ref,
    targets_ref,
    fine_matrix_ref,
    fine_pattern_ref,
    source_ref,
    fine_inverse_ref,
    change_ref,
    field_ref,
    column,
    field,
    other,
    final,
    ext,
    picked,
    out,
):
    total = matrix_ref.shape[0]
    count = total - 2 * EXT
    modes = matrix_ref.shape[2]
    zero = jnp.zeros((SUB, LANES), F32)
    width = section_ref.shape[2]
    halo = left_ref.shape[1]
    at_top = 3 * modes * SUB + SUB

    def rows_of(i, q):
        if i in (1, 3):
            return (top_inverse_ref if i == 1 else far_top_ref)[:, q * LANES : (q + 1) * LANES]
        chunk, at = divmod(q * LANES, halo)
        return (left_ref if i == 0 else right_ref)[pl.ds(at_top + chunk * width, width), pl.ds(at, LANES)]

    top_answers(parts_ref, rows_of, width, column, [(1,), (2,), (3,), (0, 4)])

    def corrected(b, slot, section_of):
        terms = []
        for p in range(SUB):
            if p < modes:
                value = sum(section_of(k, p) * column[(slot + k) * width : (slot + k + 1) * width, :] for k in range(3))
                terms.append(jnp.sum(value.reshape(width // SUB, SUB, LANES), axis=0))
            else:
                terms.append(zero)
        field[b + 1] = sol_ref[b] + fold_rows(terms)

    def far_block(slot, first):
        def body(b, carry):
            cols = pl.ds(pl.multiple_of((b - first) * LANES, LANES), LANES)
            corrected(b, slot, lambda k, p: far_ref[pl.ds((k * modes + p) * width, width), cols])
            return carry

        return body

    def own_block(b, carry):
        cols = pl.ds(pl.multiple_of((b - EXT) * LANES, LANES), LANES)
        corrected(b, 1, lambda k, p: section_ref[k, p, :, cols].astype(F32))
        return carry

    middle = where_ref[3] + EXT
    low, high = middle - FAR, middle + FAR + 1
    lax.fori_loop(low, jnp.minimum(high, EXT), far_block(0, EXT - FAR), 0)
    lax.fori_loop(jnp.maximum(low, EXT), jnp.minimum(high, EXT + count), own_block, 0)
    lax.fori_loop(jnp.maximum(low, EXT + count), high, far_block(2, EXT + count), 0)

    def smooth_first(b):
        change = inverse_ref[b] * (rhs_ref[b] - coarse_product(matrix_ref, offset_ref, field, b))
        final[b] = change
        other[b + 1] = field[b + 1] + change

    by_two(middle - 3, 7, smooth_first)

    def smooth_second(b):
        second = KEEP * final[b] + FRESH * inverse_ref[b] * (rhs_ref[b] - coarse_product(matrix_ref, offset_ref, other, b))
        final[b] = other[b + 1] + second

    by_two(middle - 2, 5, smooth_second)
    load_halo(where_ref, pair_ref, odd_ref, ext)
    rows = ext.shape[1]
    parity = where_ref[0]
    for which in range(3):
        block = (1, 2 - 2 * parity, 2 * parity)[which]
        side = (None, even_prolong_ref, odd_prolong_ref)[which]
        at = where_ref[3] + EXT + block - 2
        three = [final[at + i] for i in range(3)]
        terms = []
        for k in range(3):
            if which == 0:
                target = targets_ref[k : k + 1, :] - where_ref[1]
            else:
                row = 3 * modes * rows + k
                target = side[row : row + 1, :].astype(jnp.int32) - (where_ref[1] + (block - 1) * LANES)
            terms.append(three[1] if k == 0 else pick(three, target))
        for t in range(rows // SUB):
            part = pl.ds(t * SUB, SUB)
            value = ext[block, part, :]
            for k in range(3):
                for m in range(modes):
                    if which == 0:
                        weight = prolong_ref[k, m, part, :].astype(F32)
                    else:
                        weight = side[pl.ds((k * modes + m) * rows + t * SUB, SUB), :]
                    value = value + weight * terms[k][m : m + 1, :]
            ext[block, part, :] = value
    fine_product(where_ref, fine_matrix_ref, fine_pattern_ref, ext, picked, out)
    change = fine_inverse_ref[...] * (source_ref[...] - out[...])
    change_ref[...] = change
    field_ref[...] = ext[1] + change


def shards(
    source,
    fine_blocks,
    fine_pattern,
    fine_prolong,
    prolong_pattern,
    coarse_blocks,
    coarse_pattern,
    section_prolong,
    coarsest_inverse,
):
    both = ("slab", "sec")
    slabs, secs = lax.axis_size("slab"), lax.axis_size("sec")
    devices = slabs * secs
    rows, own = source.shape
    modes = fine_prolong.shape[2]
    section_rows = coarse_blocks.shape[3]
    width = section_prolong.shape[2]
    count = section_rows // LANES
    blocks = count + 2 * EXT
    halo = EXT * LANES
    section = lax.axis_index("slab")
    place = lax.axis_index("sec")
    device = section * secs + place
    roll = ((section + LANES - 1) * width) % LANES
    from_left = (place < secs // 2).astype(jnp.int32)
    where = jnp.stack([place % 2, device * own, section * section_rows, place, roll, from_left, section % 2]).astype(jnp.int32)

    prolong = jnp.transpose(fine_prolong, (0, 2, 1, 3))
    odd_swap = [(i, i + 1) for i in range(1, devices - 1, 2)] + [(i + 1, i) for i in range(1, devices - 1, 2)]
    even_swap = [(i, i ^ 1) for i in range(devices)]
    pairs = [[2 * i, 2 * i + 1] for i in range(secs // 2)]
    reach = [c for c in range(secs // 2) if c < FAR]

    def one_sided(value, step):
        moves = [(s * secs + c, (s + step) * secs + c) for s in range(slabs - step) for c in reach]
        moves += [((s + step) * secs + secs - 1 - c, s * secs + secs - 1 - c) for s in range(slabs - step) for c in reach]
        return lax.ppermute(value, both, moves)

    slab_odd = [(i, i + 1) for i in range(1, slabs - 1, 2)] + [(i + 1, i) for i in range(1, slabs - 1, 2)]
    slab_pairs = [[2 * i, 2 * i + 1] for i in range(slabs // 2)]

    def nearby(field):
        odd = lax.ppermute(field, both, odd_swap)
        pair = lax.all_gather(field, "sec", axis_index_groups=pairs, axis=0)
        return pair, odd, call(own_body, [fine], [VMEM] * 2)(fine_blocks, field)[0]

    def beside(value, step):
        return lax.ppermute(value, "slab", [(i, i + step) for i in range(max(0, -step), min(slabs, slabs - step))])

    fine = struct(rows, own)
    work = [pltpu.VMEM((3, rows, own), F32), pltpu.VMEM((2, rows, own), F32), pltpu.VMEM((rows, own), F32)]
    inverse, start = call(first_body, [fine, fine], [VMEM] * 2)(fine_blocks, source)

    near = nearby(start)
    pair, *held = lax.optimization_barrier((near[0], coarse_blocks, coarse_pattern, coarsest_inverse))
    near = (pair, *near[1:])
    side = struct(3 * modes * SUB + SUB + width * pl.cdiv(coarsest_inverse.shape[1], halo), halo)
    low, high = call(pack_body, [side, side], [SMEM] + [VMEM] * 3)(where, *held)
    left_data, right_data = beside(high, 1), beside(low, -1)
    def step(body, outs, near, *rest):
        return call(body, outs, [SMEM] + [VMEM] * (5 + len(rest)), work)(where, *near, fine_blocks, fine_pattern, *rest)

    coarse = struct(blocks, SUB, LANES)
    line = pltpu.VMEM((blocks + 2, SUB, LANES), F32)
    for cycle in range(CYCLES):
        if cycle == 0:
            change = start
        else:
            change, field = step(field_body, [fine, fine], nearby(solution), source, inverse)
            near = nearby(field)
        solution = step(solution_body, [fine], near, source, inverse, change)[0]
        if cycle == 0:
            solution, left_data, right_data = lax.optimization_barrier((solution, left_data, right_data))
            matrix, offset, coarse_inverse = call(
                setup_body,
                [struct(blocks, 3, modes, SUB, LANES), struct(blocks, SUB, LANES, dtype=jnp.int32), struct(blocks, SUB, LANES)],
                [SMEM] + [VMEM] * 4,
            )(where, left_data, right_data, coarse_blocks, coarse_pattern)
        near = nearby(solution)
        if cycle == 0:
            pair, *held = lax.optimization_barrier((near[0], prolong, prolong_pattern, section_prolong, coarsest_inverse))
            near = (pair, *near[1:])
            fine_pack, far = call(
                pack_prolong_body,
                [struct(3 * modes * rows + SUB, own), struct(3 * modes * width, FAR * LANES)],
                [SMEM] + [VMEM] * 3,
            )(where, *held[:3])
            far_sections, far_top = one_sided(far, 1), one_sided(held[3], 2)
            odd_prolong = lax.ppermute(fine_pack, both, odd_swap)
            even_prolong = lax.ppermute(fine_pack, both, even_swap)
        sums = step(restrict_body, [struct(secs, SUB, 3 * LANES)], near, source, prolong, prolong_pattern)[0]
        parts = lax.all_to_all(sums, "sec", 0, 0, tiled=True)
        ends, everything = call(gather_body, [struct(2 * SPILL, SUB, LANES), struct(secs + 2, SUB, LANES)], [VMEM])(parts)
        odd = lax.ppermute(ends, "slab", slab_odd)
        even = lax.all_gather(ends, "slab", axis_index_groups=slab_pairs, axis=0)
        rhs, coarse_sol, top = call(
            coarse_down_body, [coarse, coarse, struct(slabs, LANES)], [SMEM] + [VMEM] * 7, [line, line]
        )(where, everything, even, odd, matrix, offset, coarse_inverse, section_prolong)
        if cycle == 0:
            top, far_sections, far_top, odd_prolong, even_prolong = lax.optimization_barrier(
                (top, far_sections, far_top, odd_prolong, even_prolong)
            )
        tops = lax.all_to_all(top, "slab", 0, 0, tiled=True)
        change, field = call(
            up_body, [fine, fine], [SMEM] + [VMEM] * 22, [pltpu.VMEM((5 * width, LANES), F32), line, line, line] + work
        )(
            *(where, tops, left_data, coarsest_inverse, right_data, far_top, section_prolong, far_sections, coarse_sol, rhs),
            *(matrix, offset, coarse_inverse, *near[:2], prolong, even_prolong, odd_prolong, prolong_pattern),
            *(fine_blocks, fine_pattern, source, inverse),
        )
        solution = step(solution_body, [fine], nearby(field), source, inverse, change)[0]
    return solution


def solution(mesh):
    in_specs = (
        P(None, ("slab", "sec")),
        P(None, None, None, ("slab", "sec")),
        P(None, ("slab", "sec")),
        P(None, None, None, ("slab", "sec")),
        P(None, ("slab", "sec")),
        P(None, None, None, "slab"),
        P(None, "slab"),
        P(None, None, None, "slab"),
        P("slab", None),
    )
    out_specs = P(None, ("slab", "sec"))
    return jax.shard_map(shards, mesh=mesh, in_specs=in_specs, out_specs=out_specs, check_vma=False)
```

```python
import jax
import jax.numpy as jnp
from jax import lax
from jax.experimental import pallas as pl
from jax.experimental.pallas import tpu as pltpu
from jax.sharding import PartitionSpec as P

CYCLES = 2
KEEP = 1.0 / 7.0
FRESH = 8.0 / 7.0
LANES = 128
SUB = 8
EXT = 4
FAR = 3
SPILL = EXT + 1
F32 = jnp.float32
BF16 = jnp.bfloat16
VMEM = pl.BlockSpec(memory_space=pltpu.VMEM)
SMEM = pl.BlockSpec(memory_space=pltpu.SMEM)


def call(body, outs, in_specs, scratch=(), flops=1 << 20, moved=1 << 20):
    return pl.pallas_call(
        body,
        out_shape=outs,
        in_specs=in_specs,
        out_specs=[VMEM] * len(outs),
        scratch_shapes=list(scratch),
        compiler_params=pltpu.CompilerParams(vmem_limit_bytes=24 << 20),
        cost_estimate=pl.CostEstimate(flops=flops, bytes_accessed=moved, transcendentals=0),
    )


def struct(*shape, dtype=F32):
    return jax.ShapeDtypeStruct(shape, dtype)


def take(x, lane):
    return jnp.take_along_axis(x, lane, axis=1, mode="promise_in_bounds")


def pick(three, target):
    lane = jnp.broadcast_to(target & (LANES - 1), three[0].shape)
    block = jnp.broadcast_to((target + LANES) >> 7, three[0].shape)
    a, b, c = (take(x, lane) for x in three)
    return jnp.where(block == 0, a, jnp.where(block == 1, b, c))


def fold_rows(terms):
    row = lax.broadcasted_iota(jnp.int32, (SUB, LANES), 0)
    for step in (4, 2, 1):
        high = (row & step) != 0
        half = len(terms) // 2
        folded = []
        for i in range(half):
            low_sum = terms[i] + pltpu.roll(terms[i], SUB - step, 0)
            high_sum = terms[i + half] + pltpu.roll(terms[i + half], step, 0)
            folded.append(jnp.where(high, high_sum, low_sum))
        terms = folded
    return terms[0]


def split3(x):
    high = x.astype(BF16)
    rest = x - high.astype(F32)
    middle = rest.astype(BF16)
    low = (rest - middle.astype(F32)).astype(BF16)
    return high, middle, low


def lanes_dot(a, b):
    return lax.dot_general(a, b, (((1,), (1,)), ((), ())), preferred_element_type=F32)


def load_halo(where_ref, pair_ref, odd_ref, ext):
    parity = where_ref[0]
    ext[1] = pair_ref[parity]
    ext[2 - 2 * parity] = pair_ref[1 - parity]
    ext[2 * parity] = odd_ref[...]


def product_rows(matrix_ref, ks, picked, out, before=None):
    rows = out.shape[0]

    def group(g, carry):
        part = pl.ds(pl.multiple_of(g * SUB, SUB), SUB)
        terms = []
        for p in range(SUB):
            total = None
            for k in ks:
                block = matrix_ref[k, g * SUB + p].astype(F32)
                product = jnp.sum((block * picked[k][...]).reshape(rows // SUB, SUB, LANES), axis=0)
                total = product if total is None else total + product
            terms.append(total)
        value = fold_rows(terms)
        out[part, :] = value if before is None else value + before[part, :]
        return carry

    lax.fori_loop(0, rows // SUB, group, 0)


def own_body(matrix_ref, field_ref, out_ref):
    product_rows(matrix_ref, (0,), [field_ref], out_ref)


def fine_product(where_ref, matrix_ref, pattern_ref, ext, picked, out, before=None):
    rows = out.shape[0]
    base = where_ref[1]
    for k in (1, 2):
        target = pattern_ref[k : k + 1, :] - base
        lane = jnp.broadcast_to(target & (LANES - 1), (SUB, LANES))
        block = jnp.broadcast_to((target + LANES) >> 7, (SUB, LANES))
        for t in range(rows // SUB):
            part = pl.ds(t * SUB, SUB)
            a, b, c = (take(ext[i, part, :], lane) for i in range(3))
            picked[k - 1, part, :] = jnp.where(block == 0, a, jnp.where(block == 1, b, c))

    near = {1: picked.at[0], 2: picked.at[1]}
    if before is None:
        near[0] = ext.at[1]
    product_rows(matrix_ref, sorted(near), near, out, before)


def first_body(matrix_ref, source_ref, inverse_ref, field_ref):
    rows = source_ref.shape[0]
    row = lax.broadcasted_iota(jnp.int32, (SUB, LANES), 0)
    for g in range(rows // SUB):
        part = pl.ds(g * SUB, SUB)
        diagonal = jnp.zeros((SUB, LANES), F32)
        for p in range(SUB):
            entry = matrix_ref[0, g * SUB + p].astype(F32)[g * SUB : (g + 1) * SUB]
            diagonal = jnp.where(row == p, entry, diagonal)
        inverse = 1.0 / diagonal
        inverse_ref[part, :] = inverse
        field_ref[part, :] = inverse * source_ref[part, :]


def field_body(where_ref, pair_ref, odd_ref, own_ref, matrix_ref, pattern_ref, source_ref, inverse_ref, change_ref, field_ref, ext, picked, out):
    load_halo(where_ref, pair_ref, odd_ref, ext)
    fine_product(where_ref, matrix_ref, pattern_ref, ext, picked, out, own_ref)
    change = inverse_ref[...] * (source_ref[...] - out[...])
    change_ref[...] = change
    field_ref[...] = ext[1] + change


def solution_body(where_ref, pair_ref, odd_ref, own_ref, matrix_ref, pattern_ref, source_ref, inverse_ref, change_ref, field_ref, ext, picked, out):
    load_halo(where_ref, pair_ref, odd_ref, ext)
    fine_product(where_ref, matrix_ref, pattern_ref, ext, picked, out, own_ref)
    second = KEEP * change_ref[...] + FRESH * inverse_ref[...] * (source_ref[...] - out[...])
    field_ref[...] = ext[1] + second


def restrict_body(where_ref, pair_ref, odd_ref, own_ref, matrix_ref, pattern_ref, source_ref, prolong_ref, targets_ref, sums_ref, ext, picked, out):
    load_halo(where_ref, pair_ref, odd_ref, ext)
    fine_product(where_ref, matrix_ref, pattern_ref, ext, picked, out, own_ref)
    residual = source_ref[...] - out[...]
    modes = prolong_ref.shape[1]
    rows = residual.shape[0]
    slots = lax.broadcasted_iota(jnp.int32, (3 * LANES, LANES), 0)
    total = None
    for k in range(3):
        terms = []
        for m in range(SUB):
            if m < modes:
                product = prolong_ref[k, m].astype(F32) * residual
                terms.append(jnp.sum(product.reshape(rows // SUB, SUB, LANES), axis=0))
            else:
                terms.append(jnp.zeros((SUB, LANES), F32))
        parts = split3(fold_rows(terms))
        target = targets_ref[k : k + 1, :] - where_ref[1] + LANES
        hot = (slots == target).astype(F32).astype(BF16)
        stacked = jnp.concatenate([p.astype(F32) for p in parts] + [jnp.zeros((SUB, LANES), F32)], axis=0)
        spread = lanes_dot(stacked.astype(BF16), hot)
        total = spread if total is None else total + spread
    sums = total[0:SUB] + total[SUB : 2 * SUB] + total[2 * SUB : 3 * SUB]
    for i in range(sums_ref.shape[0]):
        sums_ref[i] = sums


def pack_body(where_ref, blocks_ref, pattern_ref, top_ref, low_ref, high_ref):
    modes = blocks_ref.shape[1]
    total = blocks_ref.shape[3]
    halo = low_ref.shape[1]
    width = top_ref.shape[0]
    column = lax.broadcasted_iota(jnp.int32, (1, halo), 1)
    for out, at in ((low_ref, 0), (high_ref, total - halo)):
        cols = pl.ds(at, halo)
        for k in range(3):
            for p in range(modes):
                row = (k * modes + p) * SUB
                out[row : row + modes, :] = blocks_ref[k, p, :, cols].astype(F32)
        row = 3 * modes * SUB
        for k in range(2):
            offset = pattern_ref[k + 1 : k + 2, cols] - (where_ref[2] + at) - column
            out[row + k : row + k + 1, :] = offset.astype(F32)
        row += SUB
        for i in range(pl.cdiv(top_ref.shape[1], halo)):
            part = top_ref[:, i * halo : (i + 1) * halo]
            out[row + i * width : row + (i + 1) * width, 0 : part.shape[1]] = part


def pack_prolong_body(where_ref, prolong_ref, targets_ref, section_ref, left_ref, right_ref, fine_ref, far_ref):
    modes, rows = prolong_ref.shape[1:3]
    width, total = section_ref.shape[2:]
    for k in range(3):
        for m in range(modes):
            at = (k * modes + m) * rows
            fine_ref[at : at + rows, :] = prolong_ref[k, m].astype(F32)
        at = 3 * modes * rows + k
        fine_ref[at : at + 1, :] = targets_ref[k : k + 1, :].astype(F32)
    reach = far_ref.shape[1]
    cols = pl.ds(pl.multiple_of(where_ref[5] * (total - reach), LANES), reach)
    for k in range(3):
        for p in range(modes):
            at = (k * modes + p) * width
            far_ref[at : at + width, :] = section_ref[k, p, :, cols].astype(F32)
    at_top = 3 * modes * SUB + SUB
    at_far = 3 * modes * width
    halo = left_ref.shape[1]
    for q in range((far_ref.shape[0] - at_far) // width * (reach // LANES)):
        chunk, at = divmod(q * LANES, halo)
        place = (pl.ds(at_top + chunk * width, width), pl.ds(at, LANES))
        if at_top + (chunk + 1) * width <= left_ref.shape[0]:
            chunk, at = divmod(q * LANES, reach)
            far_ref[at_far + chunk * width : at_far + (chunk + 1) * width, at : at + LANES] = jnp.where(
                where_ref[5] > 0, left_ref[place], right_ref[place]
            )


def setup_body(where_ref, left_ref, right_ref, blocks_ref, pattern_ref, matrix_ref, offset_ref, inverse_ref):
    modes = blocks_ref.shape[1]
    count = blocks_ref.shape[3] // LANES
    matrix_ref[...] = jnp.zeros_like(matrix_ref)
    row = lax.broadcasted_iota(jnp.int32, (SUB, LANES), 0)
    column = lax.broadcasted_iota(jnp.int32, (1, LANES), 1)
    at_offset = 3 * modes * SUB
    for b in range(count + 2 * EXT):
        inner = EXT <= b < EXT + count
        side = left_ref if b < EXT else right_ref
        at = b - EXT if inner else (b if b < EXT else b - EXT - count)
        cols = pl.ds(at * LANES, LANES)
        diagonal = jnp.zeros((SUB, LANES), F32)
        for k in range(3):
            for p in range(modes):
                if inner:
                    entry = blocks_ref[k, p, :, cols].astype(F32)
                else:
                    entry = side[pl.ds((k * modes + p) * SUB, modes), cols]
                matrix_ref[b, k, p, 0:modes, :] = entry
                if k == 0:
                    diagonal = jnp.where(row == p, entry[p : p + 1, :], diagonal)
        inverse_ref[b] = jnp.where(row < modes, 1.0 / jnp.where(row < modes, diagonal, 1.0), 0.0)
        for k in range(2):
            if inner:
                offset = pattern_ref[k + 1 : k + 2, cols] - (where_ref[2] + at * LANES) - column
            else:
                offset = side[at_offset + k : at_offset + k + 1, cols].astype(jnp.int32)
            offset_ref[b, k : k + 1, :] = jnp.clip(offset, -LANES, LANES)


def coarse_product(matrix_ref, offset_ref, field, b):
    lanes = lax.broadcasted_iota(jnp.int32, (1, LANES), 1)
    three = [field[b + i] for i in range(3)]
    picked = [three[1]] + [pick(three, lanes + offset_ref[b, k : k + 1, :]) for k in range(2)]
    terms = []
    modes = matrix_ref.shape[2]
    for p in range(SUB):
        if p < modes:
            terms.append(sum(matrix_ref[b, k, p] * picked[k] for k in range(3)))
        else:
            terms.append(jnp.zeros((SUB, LANES), F32))
    return fold_rows(terms)


def by_two(first, number, body):
    def trip(i, carry):
        body(first + 2 * i)
        body(first + 2 * i + 1)
        return carry

    lax.fori_loop(0, number // 2, trip, 0)
    if number % 2:
        body(first + number - 1)


def gather_body(parts_ref, ends_ref, all_ref):
    count = parts_ref.shape[0]
    blocks = []
    for b in range(-1, count + 1):
        total = None
        for device in (b - 1, b, b + 1):
            if 0 <= device < count:
                at = (b - device + 1) * LANES
                term = parts_ref[device, :, at : at + LANES]
                total = term if total is None else total + term
        blocks.append(total)
    for i, block in enumerate(blocks):
        all_ref[i] = block
    for i in range(SPILL):
        ends_ref[i] = blocks[i]
        ends_ref[SPILL + i] = blocks[count + 2 - SPILL + i]


def coarse_down_body(where_ref, all_ref, even_ref, odd_ref, matrix_ref, offset_ref, inverse_ref, section_ref, rhs_ref, sol_ref, top_ref, field, other):
    total = matrix_ref.shape[0]
    count = total - 2 * EXT
    modes = matrix_ref.shape[2]
    width = section_ref.shape[2]
    zero = jnp.zeros((SUB, LANES), F32)
    parity = where_ref[6]
    for b in range(total):
        terms = []
        at = b - (EXT - 1)
        if 0 <= at < count + 2:
            terms.append(all_ref[at])
        if b < SPILL:
            terms.append(jnp.where(parity == 0, odd_ref[SPILL + b], even_ref[1 - parity, SPILL + b]))
        if b >= total - SPILL:
            i = b - (total - SPILL)
            terms.append(jnp.where(parity == 0, even_ref[1 - parity, i], odd_ref[i]))
        value = sum(terms[1:], terms[0])
        rhs_ref[b] = value
        field[b + 1] = inverse_ref[b] * value
    for edge in (0, total + 1):
        field[edge] = zero
        other[edge] = zero

    def first(b):
        start = field[b + 1]
        second = KEEP * start + FRESH * inverse_ref[b] * (rhs_ref[b] - coarse_product(matrix_ref, offset_ref, field, b))
        other[b + 1] = start + second
        sol_ref[b] = start + second

    by_two(EXT - FAR, count + 2 * FAR, first)

    def down(i, carry):
        for j in range(2):
            b = 2 * i + j + EXT
            residual = rhs_ref[b] - coarse_product(matrix_ref, offset_ref, other, b)
            cols = pl.ds(pl.multiple_of((2 * i + j) * LANES, LANES), LANES)
            out = []
            for k in range(3):
                value = carry[k]
                for p in range(modes):
                    value = value + section_ref[k, p, :, cols].astype(F32) * residual[p : p + 1, :]
                out.append(value)
            carry = out
        return tuple(carry)

    sums = lax.fori_loop(0, count // 2, down, tuple(jnp.zeros((width, LANES), F32) for _ in range(3)))
    stacked = jnp.concatenate(list(sums) + [jnp.zeros((LANES - 3 * width, LANES), F32)], axis=0)
    ones = jnp.ones((16, LANES), BF16)
    row = sum(lanes_dot(ones, part) for part in split3(stacked))
    top_ref[...] = jnp.broadcast_to(pltpu.roll(row, where_ref[4], 1)[0:1], top_ref.shape)


def top_answers(parts_ref, rows_of, width, column, slots):
    sections = parts_ref.shape[0]
    chunk_count = sections * width // LANES
    sub = lax.broadcasted_iota(jnp.int32, (SUB, LANES), 0)
    lane = lax.broadcasted_iota(jnp.int32, (SUB, LANES), 1)
    chunks = [None] * chunk_count
    for tile in range(sections // SUB):
        first = (sub + (tile * SUB - 1)) * width
        chunk = (first + ((lane - first) & (LANES - 1))) >> 7
        value = parts_ref[tile * SUB : (tile + 1) * SUB, :]
        low = (tile * SUB - 1) * width
        for q in range(max(0, low // LANES), min(chunk_count, (low + (SUB + 2) * width) // LANES + 1)):
            term = jnp.where(chunk == q, value, 0.0)
            chunks[q] = term if chunks[q] is None else chunks[q] + term
    chunks = [jnp.sum(c, axis=0, keepdims=True) for c in chunks]
    for i, places in enumerate(slots):
        total = None
        for q in range(chunk_count):
            term = rows_of(i, q) * chunks[q]
            total = term if total is None else total + term
        answer = jnp.broadcast_to(jnp.sum(total, axis=1, keepdims=True), (width, LANES))
        for place in places:
            column[place * width : (place + 1) * width, :] = answer


def up_body(
    where_ref,
    parts_ref,
    left_ref,
    top_inverse_ref,
    right_ref,
    section_ref,
    far_ref,
    sol_ref,
    rhs_ref,
    matrix_ref,
    offset_ref,
    inverse_ref,
    pair_ref,
    odd_ref,
    prolong_ref,
    even_prolong_ref,
    odd_prolong_ref,
    targets_ref,
    fine_matrix_ref,
    fine_pattern_ref,
    source_ref,
    fine_inverse_ref,
    change_ref,
    field_ref,
    column,
    field,
    other,
    final,
    ext,
    picked,
    out,
):
    total = matrix_ref.shape[0]
    count = total - 2 * EXT
    modes = matrix_ref.shape[2]
    zero = jnp.zeros((SUB, LANES), F32)
    width = section_ref.shape[2]
    halo = left_ref.shape[1]
    at_top = 3 * modes * SUB + SUB

    def rows_of(i, q):
        if i == 1:
            return top_inverse_ref[:, q * LANES : (q + 1) * LANES]
        if i == 3:
            chunk, at = divmod(q * LANES, far_ref.shape[1])
            return far_ref[pl.ds((3 * modes + chunk) * width, width), pl.ds(at, LANES)]
        chunk, at = divmod(q * LANES, halo)
        return (left_ref if i == 0 else right_ref)[pl.ds(at_top + chunk * width, width), pl.ds(at, LANES)]

    top_answers(parts_ref, rows_of, width, column, [(1,), (2,), (3,), (0, 4)])

    def corrected(b, slot, section_of):
        terms = []
        for p in range(SUB):
            if p < modes:
                value = sum(section_of(k, p) * column[(slot + k) * width : (slot + k + 1) * width, :] for k in range(3))
                terms.append(jnp.sum(value.reshape(width // SUB, SUB, LANES), axis=0))
            else:
                terms.append(zero)
        field[b + 1] = sol_ref[b] + fold_rows(terms)

    def far_block(slot, first):
        def body(b, carry):
            cols = pl.ds(pl.multiple_of((b - first) * LANES, LANES), LANES)
            corrected(b, slot, lambda k, p: far_ref[pl.ds((k * modes + p) * width, width), cols])
            return carry

        return body

    def own_block(b, carry):
        cols = pl.ds(pl.multiple_of((b - EXT) * LANES, LANES), LANES)
        corrected(b, 1, lambda k, p: section_ref[k, p, :, cols].astype(F32))
        return carry

    middle = where_ref[3] + EXT
    low, high = middle - FAR, middle + FAR + 1
    lax.fori_loop(low, jnp.minimum(high, EXT), far_block(0, EXT - FAR), 0)
    lax.fori_loop(jnp.maximum(low, EXT), jnp.minimum(high, EXT + count), own_block, 0)
    lax.fori_loop(jnp.maximum(low, EXT + count), high, far_block(2, EXT + count), 0)

    def smooth_first(b):
        change = inverse_ref[b] * (rhs_ref[b] - coarse_product(matrix_ref, offset_ref, field, b))
        final[b] = change
        other[b + 1] = field[b + 1] + change

    by_two(middle - 3, 7, smooth_first)

    def smooth_second(b):
        second = KEEP * final[b] + FRESH * inverse_ref[b] * (rhs_ref[b] - coarse_product(matrix_ref, offset_ref, other, b))
        final[b] = other[b + 1] + second

    by_two(middle - 2, 5, smooth_second)
    load_halo(where_ref, pair_ref, odd_ref, ext)
    rows = ext.shape[1]
    parity = where_ref[0]
    for which in range(3):
        block = (1, 2 - 2 * parity, 2 * parity)[which]
        side = (None, even_prolong_ref, odd_prolong_ref)[which]
        at = where_ref[3] + EXT + block - 2
        three = [final[at + i] for i in range(3)]
        terms = []
        for k in range(3):
            if which == 0:
                target = targets_ref[k : k + 1, :] - where_ref[1]
            else:
                row = 3 * modes * rows + k
                target = side[row : row + 1, :].astype(jnp.int32) - (where_ref[1] + (block - 1) * LANES)
            terms.append(three[1] if k == 0 else pick(three, target))
        for t in range(rows // SUB):
            part = pl.ds(t * SUB, SUB)
            value = ext[block, part, :]
            for k in range(3):
                for m in range(modes):
                    if which == 0:
                        weight = prolong_ref[k, m, part, :].astype(F32)
                    else:
                        weight = side[pl.ds((k * modes + m) * rows + t * SUB, SUB), :]
                    value = value + weight * terms[k][m : m + 1, :]
            ext[block, part, :] = value
    fine_product(where_ref, fine_matrix_ref, fine_pattern_ref, ext, picked, out)
    change = fine_inverse_ref[...] * (source_ref[...] - out[...])
    change_ref[...] = change
    field_ref[...] = ext[1] + change


def shards(
    source,
    fine_blocks,
    fine_pattern,
    fine_prolong,
    prolong_pattern,
    coarse_blocks,
    coarse_pattern,
    section_prolong,
    coarsest_inverse,
):
    both = ("slab", "sec")
    slabs, secs = lax.axis_size("slab"), lax.axis_size("sec")
    devices = slabs * secs
    rows, own = source.shape
    modes = fine_prolong.shape[2]
    section_rows = coarse_blocks.shape[3]
    width = section_prolong.shape[2]
    count = section_rows // LANES
    blocks = count + 2 * EXT
    halo = EXT * LANES
    section = lax.axis_index("slab")
    place = lax.axis_index("sec")
    device = section * secs + place
    roll = ((section + LANES - 1) * width) % LANES
    from_left = (place < secs // 2).astype(jnp.int32)
    where = jnp.stack([place % 2, device * own, section * section_rows, place, roll, from_left, section % 2]).astype(jnp.int32)

    prolong = jnp.transpose(fine_prolong, (0, 2, 1, 3))
    odd_swap = [(i, i + 1) for i in range(1, devices - 1, 2)] + [(i + 1, i) for i in range(1, devices - 1, 2)]
    even_swap = [(i, i ^ 1) for i in range(devices)]
    pairs = [[2 * i, 2 * i + 1] for i in range(secs // 2)]
    reach = [c for c in range(secs // 2) if c < FAR]

    def one_sided(value, step):
        moves = [(s * secs + c, (s + step) * secs + c) for s in range(slabs - step) for c in reach]
        moves += [((s + step) * secs + secs - 1 - c, s * secs + secs - 1 - c) for s in range(slabs - step) for c in reach]
        return lax.ppermute(value, both, moves)

    slab_odd = [(i, i + 1) for i in range(1, slabs - 1, 2)] + [(i + 1, i) for i in range(1, slabs - 1, 2)]
    slab_pairs = [[2 * i, 2 * i + 1] for i in range(slabs // 2)]

    def nearby(field):
        odd = lax.ppermute(field, both, odd_swap)
        pair = lax.all_gather(field, "sec", axis_index_groups=pairs, axis=0)
        return pair, odd, call(own_body, [fine], [VMEM] * 2)(fine_blocks, field)[0]

    def beside(value, step):
        return lax.ppermute(value, "slab", [(i, i + step) for i in range(max(0, -step), min(slabs, slabs - step))])

    fine = struct(rows, own)
    work = [pltpu.VMEM((3, rows, own), F32), pltpu.VMEM((2, rows, own), F32), pltpu.VMEM((rows, own), F32)]
    inverse, start = call(first_body, [fine, fine], [VMEM] * 2)(fine_blocks, source)

    near = nearby(start)
    pair, later = lax.optimization_barrier((near[0], where))
    near = (pair, *near[1:])
    side = struct(3 * modes * SUB + SUB + width * pl.cdiv(coarsest_inverse.shape[1], halo), halo)
    low, high = call(pack_body, [side, side], [SMEM] + [VMEM] * 3)(later, coarse_blocks, coarse_pattern, coarsest_inverse)
    left_data, right_data = beside(high, 1), beside(low, -1)
    def step(body, outs, near, *rest):
        return call(body, outs, [SMEM] + [VMEM] * (5 + len(rest)), work)(where, *near, fine_blocks, fine_pattern, *rest)

    coarse = struct(blocks, SUB, LANES)
    line = pltpu.VMEM((blocks + 2, SUB, LANES), F32)
    for cycle in range(CYCLES):
        if cycle == 0:
            change = start
        else:
            change, field = step(field_body, [fine, fine], nearby(solution), source, inverse)
            near = nearby(field)
        solution = step(solution_body, [fine], near, source, inverse, change)[0]
        if cycle == 0:
            solution, left_data, right_data = lax.optimization_barrier((solution, left_data, right_data))
            matrix, offset, coarse_inverse = call(
                setup_body,
                [struct(blocks, 3, modes, SUB, LANES), struct(blocks, SUB, LANES, dtype=jnp.int32), struct(blocks, SUB, LANES)],
                [SMEM] + [VMEM] * 4,
            )(where, left_data, right_data, coarse_blocks, coarse_pattern)
        near = nearby(solution)
        if cycle == 0:
            mine, later = lax.optimization_barrier((near[2], where))
            near = (*near[:2], mine)
            fine_pack, far = call(
                pack_prolong_body,
                [struct(3 * modes * rows + SUB, own), struct((3 * modes + pl.cdiv(slabs * width, FAR * LANES)) * width, FAR * LANES)],
                [SMEM] + [VMEM] * 5,
            )(later, prolong, prolong_pattern, section_prolong, left_data, right_data)
            far_data = one_sided(far, 1)
            odd_prolong = lax.ppermute(fine_pack, both, odd_swap)
            even_prolong = lax.ppermute(fine_pack, both, even_swap)
        sums = step(restrict_body, [struct(secs, SUB, 3 * LANES)], near, source, prolong, prolong_pattern)[0]
        parts = lax.all_to_all(sums, "sec", 0, 0, tiled=True)
        ends, everything = call(gather_body, [struct(2 * SPILL, SUB, LANES), struct(secs + 2, SUB, LANES)], [VMEM])(parts)
        odd = lax.ppermute(ends, "slab", slab_odd)
        even = lax.all_gather(ends, "slab", axis_index_groups=slab_pairs, axis=0)
        rhs, coarse_sol, top = call(
            coarse_down_body, [coarse, coarse, struct(slabs, LANES)], [SMEM] + [VMEM] * 7, [line, line]
        )(where, everything, even, odd, matrix, offset, coarse_inverse, section_prolong)
        if cycle == 0:
            top, far_data, odd_prolong, even_prolong = lax.optimization_barrier((top, far_data, odd_prolong, even_prolong))
        tops = lax.all_to_all(top, "slab", 0, 0, tiled=True)
        change, field = call(
            up_body, [fine, fine], [SMEM] + [VMEM] * 21, [pltpu.VMEM((5 * width, LANES), F32), line, line, line] + work
        )(
            *(where, tops, left_data, coarsest_inverse, right_data, section_prolong, far_data, coarse_sol, rhs),
            *(matrix, offset, coarse_inverse, *near[:2], prolong, even_prolong, odd_prolong, prolong_pattern),
            *(fine_blocks, fine_pattern, source, inverse),
        )
        solution = step(solution_body, [fine], nearby(field), source, inverse, change)[0]
    return solution


def solution(mesh):
    in_specs = (
        P(None, ("slab", "sec")),
        P(None, None, None, ("slab", "sec")),
        P(None, ("slab", "sec")),
        P(None, None, None, ("slab", "sec")),
        P(None, ("slab", "sec")),
        P(None, None, None, "slab"),
        P(None, "slab"),
        P(None, None, None, "slab"),
        P("slab", None),
    )
    out_specs = P(None, ("slab", "sec"))
    return jax.shard_map(shards, mesh=mesh, in_specs=in_specs, out_specs=out_specs, check_vma=False)
```

```python
import jax
import jax.numpy as jnp
from jax import lax
from jax.experimental import pallas as pl
from jax.experimental.pallas import tpu as pltpu
from jax.sharding import PartitionSpec as P

CYCLES = 2
KEEP = 1.0 / 7.0
FRESH = 8.0 / 7.0
LANES = 128
SUB = 8
EXT = 4
FAR = 3
SPILL = EXT + 1
F32 = jnp.float32
BF16 = jnp.bfloat16
VMEM = pl.BlockSpec(memory_space=pltpu.VMEM)
SMEM = pl.BlockSpec(memory_space=pltpu.SMEM)


def call(body, outs, in_specs, scratch=(), flops=1 << 20, moved=1 << 20):
    return pl.pallas_call(
        body,
        out_shape=outs,
        in_specs=in_specs,
        out_specs=[VMEM] * len(outs),
        scratch_shapes=list(scratch),
        compiler_params=pltpu.CompilerParams(vmem_limit_bytes=24 << 20),
        cost_estimate=pl.CostEstimate(flops=flops, bytes_accessed=moved, transcendentals=0),
    )


def struct(*shape, dtype=F32):
    return jax.ShapeDtypeStruct(shape, dtype)


def take(x, lane):
    return jnp.take_along_axis(x, lane, axis=1, mode="promise_in_bounds")


def pick(three, target):
    lane = jnp.broadcast_to(target & (LANES - 1), three[0].shape)
    block = jnp.broadcast_to((target + LANES) >> 7, three[0].shape)
    a, b, c = (take(x, lane) for x in three)
    return jnp.where(block == 0, a, jnp.where(block == 1, b, c))


def fold_rows(terms):
    row = lax.broadcasted_iota(jnp.int32, (SUB, LANES), 0)
    for step in (4, 2, 1):
        high = (row & step) != 0
        half = len(terms) // 2
        folded = []
        for i in range(half):
            low_sum = terms[i] + pltpu.roll(terms[i], SUB - step, 0)
            high_sum = terms[i + half] + pltpu.roll(terms[i + half], step, 0)
            folded.append(jnp.where(high, high_sum, low_sum))
        terms = folded
    return terms[0]


def split3(x):
    high = x.astype(BF16)
    rest = x - high.astype(F32)
    middle = rest.astype(BF16)
    low = (rest - middle.astype(F32)).astype(BF16)
    return high, middle, low


def lanes_dot(a, b):
    return lax.dot_general(a, b, (((1,), (1,)), ((), ())), preferred_element_type=F32)


def load_halo(where_ref, pair_ref, odd_ref, ext):
    parity = where_ref[0]
    ext[1] = pair_ref[parity]
    ext[2 - 2 * parity] = pair_ref[1 - parity]
    ext[2 * parity] = odd_ref[...]


def product_rows(matrix_ref, ks, picked, out, before=None):
    rows = out.shape[0]

    def group(g, carry):
        part = pl.ds(pl.multiple_of(g * SUB, SUB), SUB)
        terms = []
        for p in range(SUB):
            total = None
            for k in ks:
                block = matrix_ref[k, g * SUB + p].astype(F32)
                product = jnp.sum((block * picked[k][...]).reshape(rows // SUB, SUB, LANES), axis=0)
                total = product if total is None else total + product
            terms.append(total)
        value = fold_rows(terms)
        out[part, :] = value if before is None else value + before[part, :]
        return carry

    lax.fori_loop(0, rows // SUB, group, 0)


def own_body(matrix_ref, field_ref, out_ref):
    product_rows(matrix_ref, (0,), [field_ref], out_ref)


def fine_product(where_ref, matrix_ref, pattern_ref, ext, picked, out, before=None):
    rows = out.shape[0]
    base = where_ref[1]
    for k in (1, 2):
        target = pattern_ref[k : k + 1, :] - base
        lane = jnp.broadcast_to(target & (LANES - 1), (SUB, LANES))
        block = jnp.broadcast_to((target + LANES) >> 7, (SUB, LANES))
        for t in range(rows // SUB):
            part = pl.ds(t * SUB, SUB)
            a, b, c = (take(ext[i, part, :], lane) for i in range(3))
            picked[k - 1, part, :] = jnp.where(block == 0, a, jnp.where(block == 1, b, c))

    near = {1: picked.at[0], 2: picked.at[1]}
    if before is None:
        near[0] = ext.at[1]
    product_rows(matrix_ref, sorted(near), near, out, before)


def first_body(matrix_ref, source_ref, inverse_ref, field_ref):
    rows = source_ref.shape[0]
    row = lax.broadcasted_iota(jnp.int32, (SUB, LANES), 0)
    for g in range(rows // SUB):
        part = pl.ds(g * SUB, SUB)
        diagonal = jnp.zeros((SUB, LANES), F32)
        for p in range(SUB):
            entry = matrix_ref[0, g * SUB + p].astype(F32)[g * SUB : (g + 1) * SUB]
            diagonal = jnp.where(row == p, entry, diagonal)
        inverse = 1.0 / diagonal
        inverse_ref[part, :] = inverse
        field_ref[part, :] = inverse * source_ref[part, :]


def field_body(where_ref, pair_ref, odd_ref, own_ref, matrix_ref, pattern_ref, source_ref, inverse_ref, change_ref, field_ref, ext, picked, out):
    load_halo(where_ref, pair_ref, odd_ref, ext)
    fine_product(where_ref, matrix_ref, pattern_ref, ext, picked, out, own_ref)
    change = inverse_ref[...] * (source_ref[...] - out[...])
    change_ref[...] = change
    field_ref[...] = ext[1] + change


def solution_body(where_ref, pair_ref, odd_ref, own_ref, matrix_ref, pattern_ref, source_ref, inverse_ref, change_ref, field_ref, ext, picked, out):
    load_halo(where_ref, pair_ref, odd_ref, ext)
    fine_product(where_ref, matrix_ref, pattern_ref, ext, picked, out, own_ref)
    second = KEEP * change_ref[...] + FRESH * inverse_ref[...] * (source_ref[...] - out[...])
    field_ref[...] = ext[1] + second


def restrict_body(where_ref, pair_ref, odd_ref, own_ref, matrix_ref, pattern_ref, source_ref, prolong_ref, targets_ref, sums_ref, ext, picked, out):
    load_halo(where_ref, pair_ref, odd_ref, ext)
    fine_product(where_ref, matrix_ref, pattern_ref, ext, picked, out, own_ref)
    residual = source_ref[...] - out[...]
    modes = prolong_ref.shape[1]
    rows = residual.shape[0]
    slots = lax.broadcasted_iota(jnp.int32, (3 * LANES, LANES), 0)
    total = None
    for k in range(3):
        terms = []
        for m in range(SUB):
            if m < modes:
                product = prolong_ref[k, m].astype(F32) * residual
                terms.append(jnp.sum(product.reshape(rows // SUB, SUB, LANES), axis=0))
            else:
                terms.append(jnp.zeros((SUB, LANES), F32))
        parts = split3(fold_rows(terms))
        target = targets_ref[k : k + 1, :] - where_ref[1] + LANES
        hot = (slots == target).astype(F32).astype(BF16)
        stacked = jnp.concatenate([p.astype(F32) for p in parts] + [jnp.zeros((SUB, LANES), F32)], axis=0)
        spread = lanes_dot(stacked.astype(BF16), hot)
        total = spread if total is None else total + spread
    sums = total[0:SUB] + total[SUB : 2 * SUB] + total[2 * SUB : 3 * SUB]
    for i in range(sums_ref.shape[0]):
        sums_ref[i] = sums


def pack_body(where_ref, blocks_ref, pattern_ref, top_ref, low_ref, high_ref):
    modes = blocks_ref.shape[1]
    total = blocks_ref.shape[3]
    halo = low_ref.shape[1]
    width = top_ref.shape[0]
    column = lax.broadcasted_iota(jnp.int32, (1, halo), 1)
    for out, at in ((low_ref, 0), (high_ref, total - halo)):
        cols = pl.ds(at, halo)
        for k in range(3):
            for p in range(modes):
                row = (k * modes + p) * SUB
                out[row : row + modes, :] = blocks_ref[k, p, :, cols].astype(F32)
        row = 3 * modes * SUB
        for k in range(2):
            offset = pattern_ref[k + 1 : k + 2, cols] - (where_ref[2] + at) - column
            out[row + k : row + k + 1, :] = offset.astype(F32)
        row += SUB
        for i in range(pl.cdiv(top_ref.shape[1], halo)):
            part = top_ref[:, i * halo : (i + 1) * halo]
            out[row + i * width : row + (i + 1) * width, 0 : part.shape[1]] = part


def pack_prolong_body(where_ref, prolong_ref, targets_ref, fine_ref):
    modes, rows = prolong_ref.shape[1:3]
    for k in range(3):
        for m in range(modes):
            at = (k * modes + m) * rows
            fine_ref[at : at + rows, :] = prolong_ref[k, m].astype(F32)
        at = 3 * modes * rows + k
        fine_ref[at : at + 1, :] = targets_ref[k : k + 1, :].astype(F32)


def pack_far_body(where_ref, section_ref, left_ref, right_ref, far_ref):
    modes, width, total = section_ref.shape[1:]
    reach = far_ref.shape[1]
    cols = pl.ds(pl.multiple_of(where_ref[5] * (total - reach), LANES), reach)
    for k in range(3):
        for p in range(modes):
            at = (k * modes + p) * width
            far_ref[at : at + width, :] = section_ref[k, p, :, cols].astype(F32)
    at_top = 3 * modes * SUB + SUB
    at_far = 3 * modes * width
    halo = left_ref.shape[1]
    for q in range((far_ref.shape[0] - at_far) // width * (reach // LANES)):
        chunk, at = divmod(q * LANES, halo)
        place = (pl.ds(at_top + chunk * width, width), pl.ds(at, LANES))
        if at_top + (chunk + 1) * width <= left_ref.shape[0]:
            chunk, at = divmod(q * LANES, reach)
            far_ref[at_far + chunk * width : at_far + (chunk + 1) * width, at : at + LANES] = jnp.where(
                where_ref[5] > 0, left_ref[place], right_ref[place]
            )


def setup_body(where_ref, left_ref, right_ref, blocks_ref, pattern_ref, matrix_ref, offset_ref, inverse_ref):
    modes = blocks_ref.shape[1]
    count = blocks_ref.shape[3] // LANES
    matrix_ref[...] = jnp.zeros_like(matrix_ref)
    row = lax.broadcasted_iota(jnp.int32, (SUB, LANES), 0)
    column = lax.broadcasted_iota(jnp.int32, (1, LANES), 1)
    at_offset = 3 * modes * SUB
    for b in range(count + 2 * EXT):
        inner = EXT <= b < EXT + count
        side = left_ref if b < EXT else right_ref
        at = b - EXT if inner else (b if b < EXT else b - EXT - count)
        cols = pl.ds(at * LANES, LANES)
        diagonal = jnp.zeros((SUB, LANES), F32)
        for k in range(3):
            for p in range(modes):
                if inner:
                    entry = blocks_ref[k, p, :, cols].astype(F32)
                else:
                    entry = side[pl.ds((k * modes + p) * SUB, modes), cols]
                matrix_ref[b, k, p, 0:modes, :] = entry
                if k == 0:
                    diagonal = jnp.where(row == p, entry[p : p + 1, :], diagonal)
        inverse_ref[b] = jnp.where(row < modes, 1.0 / jnp.where(row < modes, diagonal, 1.0), 0.0)
        for k in range(2):
            if inner:
                offset = pattern_ref[k + 1 : k + 2, cols] - (where_ref[2] + at * LANES) - column
            else:
                offset = side[at_offset + k : at_offset + k + 1, cols].astype(jnp.int32)
            offset_ref[b, k : k + 1, :] = jnp.clip(offset, -LANES, LANES)


def coarse_product(matrix_ref, offset_ref, field, b):
    lanes = lax.broadcasted_iota(jnp.int32, (1, LANES), 1)
    three = [field[b + i] for i in range(3)]
    picked = [three[1]] + [pick(three, lanes + offset_ref[b, k : k + 1, :]) for k in range(2)]
    terms = []
    modes = matrix_ref.shape[2]
    for p in range(SUB):
        if p < modes:
            terms.append(sum(matrix_ref[b, k, p] * picked[k] for k in range(3)))
        else:
            terms.append(jnp.zeros((SUB, LANES), F32))
    return fold_rows(terms)


def by_two(first, number, body):
    def trip(i, carry):
        body(first + 2 * i)
        body(first + 2 * i + 1)
        return carry

    lax.fori_loop(0, number // 2, trip, 0)
    if number % 2:
        body(first + number - 1)


def gather_body(parts_ref, ends_ref, all_ref):
    count = parts_ref.shape[0]
    blocks = []
    for b in range(-1, count + 1):
        total = None
        for device in (b - 1, b, b + 1):
            if 0 <= device < count:
                at = (b - device + 1) * LANES
                term = parts_ref[device, :, at : at + LANES]
                total = term if total is None else total + term
        blocks.append(total)
    for i, block in enumerate(blocks):
        all_ref[i] = block
    for i in range(SPILL):
        ends_ref[i] = blocks[i]
        ends_ref[SPILL + i] = blocks[count + 2 - SPILL + i]


def coarse_down_body(where_ref, all_ref, even_ref, odd_ref, matrix_ref, offset_ref, inverse_ref, section_ref, rhs_ref, sol_ref, top_ref, field, other):
    total = matrix_ref.shape[0]
    count = total - 2 * EXT
    modes = matrix_ref.shape[2]
    width = section_ref.shape[2]
    zero = jnp.zeros((SUB, LANES), F32)
    parity = where_ref[6]
    for b in range(total):
        terms = []
        at = b - (EXT - 1)
        if 0 <= at < count + 2:
            terms.append(all_ref[at])
        if b < SPILL:
            terms.append(jnp.where(parity == 0, odd_ref[SPILL + b], even_ref[1 - parity, SPILL + b]))
        if b >= total - SPILL:
            i = b - (total - SPILL)
            terms.append(jnp.where(parity == 0, even_ref[1 - parity, i], odd_ref[i]))
        value = sum(terms[1:], terms[0])
        rhs_ref[b] = value
        field[b + 1] = inverse_ref[b] * value
    for edge in (0, total + 1):
        field[edge] = zero
        other[edge] = zero

    def first(b):
        start = field[b + 1]
        second = KEEP * start + FRESH * inverse_ref[b] * (rhs_ref[b] - coarse_product(matrix_ref, offset_ref, field, b))
        other[b + 1] = start + second
        sol_ref[b] = start + second

    by_two(EXT - FAR, count + 2 * FAR, first)

    def down(i, carry):
        for j in range(2):
            b = 2 * i + j + EXT
            residual = rhs_ref[b] - coarse_product(matrix_ref, offset_ref, other, b)
            cols = pl.ds(pl.multiple_of((2 * i + j) * LANES, LANES), LANES)
            out = []
            for k in range(3):
                value = carry[k]
                for p in range(modes):
                    value = value + section_ref[k, p, :, cols].astype(F32) * residual[p : p + 1, :]
                out.append(value)
            carry = out
        return tuple(carry)

    sums = lax.fori_loop(0, count // 2, down, tuple(jnp.zeros((width, LANES), F32) for _ in range(3)))
    stacked = jnp.concatenate(list(sums) + [jnp.zeros((LANES - 3 * width, LANES), F32)], axis=0)
    ones = jnp.ones((16, LANES), BF16)
    row = sum(lanes_dot(ones, part) for part in split3(stacked))
    top_ref[...] = jnp.broadcast_to(pltpu.roll(row, where_ref[4], 1)[0:1], top_ref.shape)


def top_answers(parts_ref, rows_of, width, column, slots):
    sections = parts_ref.shape[0]
    chunk_count = sections * width // LANES
    sub = lax.broadcasted_iota(jnp.int32, (SUB, LANES), 0)
    lane = lax.broadcasted_iota(jnp.int32, (SUB, LANES), 1)
    chunks = [None] * chunk_count
    for tile in range(sections // SUB):
        first = (sub + (tile * SUB - 1)) * width
        chunk = (first + ((lane - first) & (LANES - 1))) >> 7
        value = parts_ref[tile * SUB : (tile + 1) * SUB, :]
        low = (tile * SUB - 1) * width
        for q in range(max(0, low // LANES), min(chunk_count, (low + (SUB + 2) * width) // LANES + 1)):
            term = jnp.where(chunk == q, value, 0.0)
            chunks[q] = term if chunks[q] is None else chunks[q] + term
    chunks = [jnp.sum(c, axis=0, keepdims=True) for c in chunks]
    for i, places in enumerate(slots):
        total = None
        for q in range(chunk_count):
            term = rows_of(i, q) * chunks[q]
            total = term if total is None else total + term
        answer = jnp.broadcast_to(jnp.sum(total, axis=1, keepdims=True), (width, LANES))
        for place in places:
            column[place * width : (place + 1) * width, :] = answer


def up_body(
    where_ref,
    parts_ref,
    left_ref,
    top_inverse_ref,
    right_ref,
    section_ref,
    far_ref,
    sol_ref,
    rhs_ref,
    matrix_ref,
    offset_ref,
    inverse_ref,
    pair_ref,
    odd_ref,
    prolong_ref,
    even_prolong_ref,
    odd_prolong_ref,
    targets_ref,
    fine_matrix_ref,
    fine_pattern_ref,
    source_ref,
    fine_inverse_ref,
    change_ref,
    field_ref,
    column,
    field,
    other,
    final,
    ext,
    picked,
    out,
):
    total = matrix_ref.shape[0]
    count = total - 2 * EXT
    modes = matrix_ref.shape[2]
    zero = jnp.zeros((SUB, LANES), F32)
    width = section_ref.shape[2]
    halo = left_ref.shape[1]
    at_top = 3 * modes * SUB + SUB

    def rows_of(i, q):
        if i == 1:
            return top_inverse_ref[:, q * LANES : (q + 1) * LANES]
        if i == 3:
            chunk, at = divmod(q * LANES, far_ref.shape[1])
            return far_ref[pl.ds((3 * modes + chunk) * width, width), pl.ds(at, LANES)]
        chunk, at = divmod(q * LANES, halo)
        return (left_ref if i == 0 else right_ref)[pl.ds(at_top + chunk * width, width), pl.ds(at, LANES)]

    top_answers(parts_ref, rows_of, width, column, [(1,), (2,), (3,), (0, 4)])

    def corrected(b, slot, section_of):
        terms = []
        for p in range(SUB):
            if p < modes:
                value = sum(section_of(k, p) * column[(slot + k) * width : (slot + k + 1) * width, :] for k in range(3))
                terms.append(jnp.sum(value.reshape(width // SUB, SUB, LANES), axis=0))
            else:
                terms.append(zero)
        field[b + 1] = sol_ref[b] + fold_rows(terms)

    def far_block(slot, first):
        def body(b, carry):
            cols = pl.ds(pl.multiple_of((b - first) * LANES, LANES), LANES)
            corrected(b, slot, lambda k, p: far_ref[pl.ds((k * modes + p) * width, width), cols])
            return carry

        return body

    def own_block(b, carry):
        cols = pl.ds(pl.multiple_of((b - EXT) * LANES, LANES), LANES)
        corrected(b, 1, lambda k, p: section_ref[k, p, :, cols].astype(F32))
        return carry

    middle = where_ref[3] + EXT
    low, high = middle - FAR, middle + FAR + 1
    lax.fori_loop(low, jnp.minimum(high, EXT), far_block(0, EXT - FAR), 0)
    lax.fori_loop(jnp.maximum(low, EXT), jnp.minimum(high, EXT + count), own_block, 0)
    lax.fori_loop(jnp.maximum(low, EXT + count), high, far_block(2, EXT + count), 0)

    def smooth_first(b):
        change = inverse_ref[b] * (rhs_ref[b] - coarse_product(matrix_ref, offset_ref, field, b))
        final[b] = change
        other[b + 1] = field[b + 1] + change

    by_two(middle - 3, 7, smooth_first)

    def smooth_second(b):
        second = KEEP * final[b] + FRESH * inverse_ref[b] * (rhs_ref[b] - coarse_product(matrix_ref, offset_ref, other, b))
        final[b] = other[b + 1] + second

    by_two(middle - 2, 5, smooth_second)
    load_halo(where_ref, pair_ref, odd_ref, ext)
    rows = ext.shape[1]
    parity = where_ref[0]
    for which in range(3):
        block = (1, 2 - 2 * parity, 2 * parity)[which]
        side = (None, even_prolong_ref, odd_prolong_ref)[which]
        at = where_ref[3] + EXT + block - 2
        three = [final[at + i] for i in range(3)]
        terms = []
        for k in range(3):
            if which == 0:
                target = targets_ref[k : k + 1, :] - where_ref[1]
            else:
                row = 3 * modes * rows + k
                target = side[row : row + 1, :].astype(jnp.int32) - (where_ref[1] + (block - 1) * LANES)
            terms.append(three[1] if k == 0 else pick(three, target))
        for t in range(rows // SUB):
            part = pl.ds(t * SUB, SUB)
            value = ext[block, part, :]
            for k in range(3):
                for m in range(modes):
                    if which == 0:
                        weight = prolong_ref[k, m, part, :].astype(F32)
                    else:
                        weight = side[pl.ds((k * modes + m) * rows + t * SUB, SUB), :]
                    value = value + weight * terms[k][m : m + 1, :]
            ext[block, part, :] = value
    fine_product(where_ref, fine_matrix_ref, fine_pattern_ref, ext, picked, out)
    change = fine_inverse_ref[...] * (source_ref[...] - out[...])
    change_ref[...] = change
    field_ref[...] = ext[1] + change


def shards(
    source,
    fine_blocks,
    fine_pattern,
    fine_prolong,
    prolong_pattern,
    coarse_blocks,
    coarse_pattern,
    section_prolong,
    coarsest_inverse,
):
    both = ("slab", "sec")
    slabs, secs = lax.axis_size("slab"), lax.axis_size("sec")
    devices = slabs * secs
    rows, own = source.shape
    modes = fine_prolong.shape[2]
    section_rows = coarse_blocks.shape[3]
    width = section_prolong.shape[2]
    count = section_rows // LANES
    blocks = count + 2 * EXT
    halo = EXT * LANES
    section = lax.axis_index("slab")
    place = lax.axis_index("sec")
    device = section * secs + place
    roll = ((section + LANES - 1) * width) % LANES
    from_left = (place < secs // 2).astype(jnp.int32)
    where = jnp.stack([place % 2, device * own, section * section_rows, place, roll, from_left, section % 2]).astype(jnp.int32)

    prolong = jnp.transpose(fine_prolong, (0, 2, 1, 3))
    odd_swap = [(i, i + 1) for i in range(1, devices - 1, 2)] + [(i + 1, i) for i in range(1, devices - 1, 2)]
    even_swap = [(i, i ^ 1) for i in range(devices)]
    pairs = [[2 * i, 2 * i + 1] for i in range(secs // 2)]
    reach = [c for c in range(secs // 2) if c < FAR]

    def one_sided(value, step):
        moves = [(s * secs + c, (s + step) * secs + c) for s in range(slabs - step) for c in reach]
        moves += [((s + step) * secs + secs - 1 - c, s * secs + secs - 1 - c) for s in range(slabs - step) for c in reach]
        return lax.ppermute(value, both, moves)

    slab_odd = [(i, i + 1) for i in range(1, slabs - 1, 2)] + [(i + 1, i) for i in range(1, slabs - 1, 2)]
    slab_pairs = [[2 * i, 2 * i + 1] for i in range(slabs // 2)]

    def nearby(field):
        odd = lax.ppermute(field, both, odd_swap)
        pair = lax.all_gather(field, "sec", axis_index_groups=pairs, axis=0)
        return pair, odd, call(own_body, [fine], [VMEM] * 2)(fine_blocks, field)[0]

    def beside(value, step):
        return lax.ppermute(value, "slab", [(i, i + step) for i in range(max(0, -step), min(slabs, slabs - step))])

    fine = struct(rows, own)
    work = [pltpu.VMEM((3, rows, own), F32), pltpu.VMEM((2, rows, own), F32), pltpu.VMEM((rows, own), F32)]
    inverse, start = call(first_body, [fine, fine], [VMEM] * 2)(fine_blocks, source)

    near = nearby(start)
    side = struct(3 * modes * SUB + SUB + width * pl.cdiv(coarsest_inverse.shape[1], halo), halo)
    low, high = call(pack_body, [side, side], [SMEM] + [VMEM] * 3)(where, coarse_blocks, coarse_pattern, coarsest_inverse)
    left_data, right_data = beside(high, 1), beside(low, -1)
    fine_pack = call(pack_prolong_body, [struct(3 * modes * rows + SUB, own)], [SMEM] + [VMEM] * 2)(where, prolong, prolong_pattern)[0]
    def step(body, outs, near, *rest):
        return call(body, outs, [SMEM] + [VMEM] * (5 + len(rest)), work)(where, *near, fine_blocks, fine_pattern, *rest)

    coarse = struct(blocks, SUB, LANES)
    line = pltpu.VMEM((blocks + 2, SUB, LANES), F32)
    for cycle in range(CYCLES):
        if cycle == 0:
            change = start
        else:
            change, field = step(field_body, [fine, fine], nearby(solution), source, inverse)
            near = nearby(field)
        solution = step(solution_body, [fine], near, source, inverse, change)[0]
        if cycle == 0:
            solution, left_data, right_data = lax.optimization_barrier((solution, left_data, right_data))
            matrix, offset, coarse_inverse = call(
                setup_body,
                [struct(blocks, 3, modes, SUB, LANES), struct(blocks, SUB, LANES, dtype=jnp.int32), struct(blocks, SUB, LANES)],
                [SMEM] + [VMEM] * 4,
            )(where, left_data, right_data, coarse_blocks, coarse_pattern)
        near = nearby(solution)
        if cycle == 0:
            mine, later, fine_pack = lax.optimization_barrier((near[2], where, fine_pack))
            near = (*near[:2], mine)
            far = call(
                pack_far_body,
                [struct((3 * modes + pl.cdiv(slabs * width, FAR * LANES)) * width, FAR * LANES)],
                [SMEM] + [VMEM] * 3,
            )(later, section_prolong, left_data, right_data)[0]
            far_data = one_sided(far, 1)
            odd_prolong = lax.ppermute(fine_pack, both, odd_swap)
            even_prolong = lax.ppermute(fine_pack, both, even_swap)
        sums = step(restrict_body, [struct(secs, SUB, 3 * LANES)], near, source, prolong, prolong_pattern)[0]
        parts = lax.all_to_all(sums, "sec", 0, 0, tiled=True)
        ends, everything = call(gather_body, [struct(2 * SPILL, SUB, LANES), struct(secs + 2, SUB, LANES)], [VMEM])(parts)
        odd = lax.ppermute(ends, "slab", slab_odd)
        even = lax.all_gather(ends, "slab", axis_index_groups=slab_pairs, axis=0)
        rhs, coarse_sol, top = call(
            coarse_down_body, [coarse, coarse, struct(slabs, LANES)], [SMEM] + [VMEM] * 7, [line, line]
        )(where, everything, even, odd, matrix, offset, coarse_inverse, section_prolong)
        if cycle == 0:
            top, far_data, odd_prolong, even_prolong = lax.optimization_barrier((top, far_data, odd_prolong, even_prolong))
        tops = lax.all_to_all(top, "slab", 0, 0, tiled=True)
        change, field = call(
            up_body, [fine, fine], [SMEM] + [VMEM] * 21, [pltpu.VMEM((5 * width, LANES), F32), line, line, line] + work
        )(
            *(where, tops, left_data, coarsest_inverse, right_data, section_prolong, far_data, coarse_sol, rhs),
            *(matrix, offset, coarse_inverse, *near[:2], prolong, even_prolong, odd_prolong, prolong_pattern),
            *(fine_blocks, fine_pattern, source, inverse),
        )
        solution = step(solution_body, [fine], nearby(field), source, inverse, change)[0]
    return solution


def solution(mesh):
    in_specs = (
        P(None, ("slab", "sec")),
        P(None, None, None, ("slab", "sec")),
        P(None, ("slab", "sec")),
        P(None, None, None, ("slab", "sec")),
        P(None, ("slab", "sec")),
        P(None, None, None, "slab"),
        P(None, "slab"),
        P(None, None, None, "slab"),
        P("slab", None),
    )
    out_specs = P(None, ("slab", "sec"))
    return jax.shard_map(shards, mesh=mesh, in_specs=in_specs, out_specs=out_specs, check_vma=False)
```

```python
import jax
import jax.numpy as jnp
from jax import lax
from jax.experimental import pallas as pl
from jax.experimental.pallas import tpu as pltpu
from jax.sharding import PartitionSpec as P

CYCLES = 2
KEEP = 1.0 / 7.0
FRESH = 8.0 / 7.0
LANES = 128
SUB = 8
EXT = 4
FAR = 3
SPILL = EXT + 1
F32 = jnp.float32
BF16 = jnp.bfloat16
VMEM = pl.BlockSpec(memory_space=pltpu.VMEM)
SMEM = pl.BlockSpec(memory_space=pltpu.SMEM)


def call(body, outs, in_specs, scratch=(), flops=1 << 20, moved=1 << 20):
    return pl.pallas_call(
        body,
        out_shape=outs,
        in_specs=in_specs,
        out_specs=[VMEM] * len(outs),
        scratch_shapes=list(scratch),
        compiler_params=pltpu.CompilerParams(vmem_limit_bytes=24 << 20),
        cost_estimate=pl.CostEstimate(flops=flops, bytes_accessed=moved, transcendentals=0),
    )


def struct(*shape, dtype=F32):
    return jax.ShapeDtypeStruct(shape, dtype)


def take(x, lane):
    return jnp.take_along_axis(x, lane, axis=1, mode="promise_in_bounds")


def pick(three, target):
    lane = jnp.broadcast_to(target & (LANES - 1), three[0].shape)
    block = jnp.broadcast_to((target + LANES) >> 7, three[0].shape)
    a, b, c = (take(x, lane) for x in three)
    return jnp.where(block == 0, a, jnp.where(block == 1, b, c))


def fold_rows(terms):
    row = lax.broadcasted_iota(jnp.int32, (SUB, LANES), 0)
    for step in (4, 2, 1):
        high = (row & step) != 0
        half = len(terms) // 2
        folded = []
        for i in range(half):
            low_sum = terms[i] + pltpu.roll(terms[i], SUB - step, 0)
            high_sum = terms[i + half] + pltpu.roll(terms[i + half], step, 0)
            folded.append(jnp.where(high, high_sum, low_sum))
        terms = folded
    return terms[0]


def split3(x):
    high = x.astype(BF16)
    rest = x - high.astype(F32)
    middle = rest.astype(BF16)
    low = (rest - middle.astype(F32)).astype(BF16)
    return high, middle, low


def lanes_dot(a, b):
    return lax.dot_general(a, b, (((1,), (1,)), ((), ())), preferred_element_type=F32)


def load_halo(where_ref, pair_ref, odd_ref, ext):
    parity = where_ref[0]
    ext[1] = pair_ref[parity]
    ext[2 - 2 * parity] = pair_ref[1 - parity]
    ext[2 * parity] = odd_ref[...]


def product_rows(matrix_ref, ks, picked, out, before=None):
    rows = out.shape[0]

    def group(g, carry):
        part = pl.ds(pl.multiple_of(g * SUB, SUB), SUB)
        terms = []
        for p in range(SUB):
            total = None
            for k in ks:
                block = matrix_ref[k, g * SUB + p].astype(F32)
                product = jnp.sum((block * picked[k][...]).reshape(rows // SUB, SUB, LANES), axis=0)
                total = product if total is None else total + product
            terms.append(total)
        value = fold_rows(terms)
        out[part, :] = value if before is None else value + before[part, :]
        return carry

    lax.fori_loop(0, rows // SUB, group, 0)


def own_body(matrix_ref, field_ref, out_ref):
    product_rows(matrix_ref, (0,), [field_ref], out_ref)


def fine_product(where_ref, matrix_ref, pattern_ref, ext, picked, out, before=None):
    rows = out.shape[0]
    base = where_ref[1]
    for k in (1, 2):
        target = pattern_ref[k : k + 1, :] - base
        lane = jnp.broadcast_to(target & (LANES - 1), (SUB, LANES))
        block = jnp.broadcast_to((target + LANES) >> 7, (SUB, LANES))
        for t in range(rows // SUB):
            part = pl.ds(t * SUB, SUB)
            a, b, c = (take(ext[i, part, :], lane) for i in range(3))
            picked[k - 1, part, :] = jnp.where(block == 0, a, jnp.where(block == 1, b, c))

    near = {1: picked.at[0], 2: picked.at[1]}
    if before is None:
        near[0] = ext.at[1]
    product_rows(matrix_ref, sorted(near), near, out, before)


def first_body(matrix_ref, source_ref, inverse_ref, field_ref):
    rows = source_ref.shape[0]
    row = lax.broadcasted_iota(jnp.int32, (SUB, LANES), 0)
    for g in range(rows // SUB):
        part = pl.ds(g * SUB, SUB)
        diagonal = jnp.zeros((SUB, LANES), F32)
        for p in range(SUB):
            entry = matrix_ref[0, g * SUB + p].astype(F32)[g * SUB : (g + 1) * SUB]
            diagonal = jnp.where(row == p, entry, diagonal)
        inverse = 1.0 / diagonal
        inverse_ref[part, :] = inverse
        field_ref[part, :] = inverse * source_ref[part, :]


def pick_body(where_ref, pair_ref, pattern_ref, picked_ref):
    parity = where_ref[0]
    for k in (1, 2):
        target = pattern_ref[k : k + 1, :] - where_ref[1]
        lane = jnp.broadcast_to(target & (LANES - 1), (SUB, LANES))
        block = jnp.broadcast_to((target + LANES) >> 7, (SUB, LANES))
        for t in range(picked_ref.shape[1] // SUB):
            part = pl.ds(t * SUB, SUB)
            mine, other = take(pair_ref[parity, part, :], lane), take(pair_ref[1 - parity, part, :], lane)
            picked_ref[k - 1, part, :] = jnp.where(block == 1, mine, other)


def finish_product(where_ref, matrix_ref, pattern_ref, odd_ref, near_ref, own_ref, picked, out):
    odd = 2 * where_ref[0]
    for k in (1, 2):
        target = pattern_ref[k : k + 1, :] - where_ref[1]
        lane = jnp.broadcast_to(target & (LANES - 1), (SUB, LANES))
        block = jnp.broadcast_to((target + LANES) >> 7, (SUB, LANES))
        for t in range(out.shape[0] // SUB):
            part = pl.ds(t * SUB, SUB)
            picked[k - 1, part, :] = jnp.where(block == odd, take(odd_ref[part, :], lane), near_ref[k - 1, part, :])
    product_rows(matrix_ref, (1, 2), {1: picked.at[0], 2: picked.at[1]}, out, own_ref)


def field_body(where_ref, pair_ref, odd_ref, own_ref, near_ref, matrix_ref, pattern_ref, source_ref, inverse_ref, change_ref, field_ref, picked, out):
    finish_product(where_ref, matrix_ref, pattern_ref, odd_ref, near_ref, own_ref, picked, out)
    change = inverse_ref[...] * (source_ref[...] - out[...])
    change_ref[...] = change
    field_ref[...] = pair_ref[where_ref[0]] + change


def solution_body(where_ref, pair_ref, odd_ref, own_ref, near_ref, matrix_ref, pattern_ref, source_ref, inverse_ref, change_ref, field_ref, picked, out):
    finish_product(where_ref, matrix_ref, pattern_ref, odd_ref, near_ref, own_ref, picked, out)
    second = KEEP * change_ref[...] + FRESH * inverse_ref[...] * (source_ref[...] - out[...])
    field_ref[...] = pair_ref[where_ref[0]] + second


def restrict_body(where_ref, pair_ref, odd_ref, own_ref, near_ref, matrix_ref, pattern_ref, source_ref, prolong_ref, targets_ref, sums_ref, picked, out):
    finish_product(where_ref, matrix_ref, pattern_ref, odd_ref, near_ref, own_ref, picked, out)
    residual = source_ref[...] - out[...]
    modes = prolong_ref.shape[1]
    rows = residual.shape[0]
    slots = lax.broadcasted_iota(jnp.int32, (3 * LANES, LANES), 0)
    total = None
    for k in range(3):
        terms = []
        for m in range(SUB):
            if m < modes:
                product = prolong_ref[k, m].astype(F32) * residual
                terms.append(jnp.sum(product.reshape(rows // SUB, SUB, LANES), axis=0))
            else:
                terms.append(jnp.zeros((SUB, LANES), F32))
        parts = split3(fold_rows(terms))
        target = targets_ref[k : k + 1, :] - where_ref[1] + LANES
        hot = (slots == target).astype(F32).astype(BF16)
        stacked = jnp.concatenate([p.astype(F32) for p in parts] + [jnp.zeros((SUB, LANES), F32)], axis=0)
        spread = lanes_dot(stacked.astype(BF16), hot)
        total = spread if total is None else total + spread
    sums = total[0:SUB] + total[SUB : 2 * SUB] + total[2 * SUB : 3 * SUB]
    for i in range(sums_ref.shape[0]):
        sums_ref[i] = sums


def pack_body(where_ref, blocks_ref, pattern_ref, top_ref, low_ref, high_ref):
    modes = blocks_ref.shape[1]
    total = blocks_ref.shape[3]
    halo = low_ref.shape[1]
    width = top_ref.shape[0]
    column = lax.broadcasted_iota(jnp.int32, (1, halo), 1)
    for out, at in ((low_ref, 0), (high_ref, total - halo)):
        cols = pl.ds(at, halo)
        for k in range(3):
            for p in range(modes):
                row = (k * modes + p) * SUB
                out[row : row + modes, :] = blocks_ref[k, p, :, cols].astype(F32)
        row = 3 * modes * SUB
        for k in range(2):
            offset = pattern_ref[k + 1 : k + 2, cols] - (where_ref[2] + at) - column
            out[row + k : row + k + 1, :] = offset.astype(F32)
        row += SUB
        for i in range(pl.cdiv(top_ref.shape[1], halo)):
            part = top_ref[:, i * halo : (i + 1) * halo]
            out[row + i * width : row + (i + 1) * width, 0 : part.shape[1]] = part


def pack_prolong_body(where_ref, prolong_ref, targets_ref, fine_ref):
    modes, rows = prolong_ref.shape[1:3]
    for k in range(3):
        for m in range(modes):
            at = (k * modes + m) * rows
            fine_ref[at : at + rows, :] = prolong_ref[k, m].astype(F32)
        at = 3 * modes * rows + k
        fine_ref[at : at + 1, :] = targets_ref[k : k + 1, :].astype(F32)


def pack_far_body(where_ref, section_ref, left_ref, right_ref, far_ref):
    modes, width, total = section_ref.shape[1:]
    reach = far_ref.shape[1]
    cols = pl.ds(pl.multiple_of(where_ref[5] * (total - reach), LANES), reach)
    for k in range(3):
        for p in range(modes):
            at = (k * modes + p) * width
            far_ref[at : at + width, :] = section_ref[k, p, :, cols].astype(F32)
    at_top = 3 * modes * SUB + SUB
    at_far = 3 * modes * width
    halo = left_ref.shape[1]
    for q in range((far_ref.shape[0] - at_far) // width * (reach // LANES)):
        chunk, at = divmod(q * LANES, halo)
        place = (pl.ds(at_top + chunk * width, width), pl.ds(at, LANES))
        if at_top + (chunk + 1) * width <= left_ref.shape[0]:
            chunk, at = divmod(q * LANES, reach)
            far_ref[at_far + chunk * width : at_far + (chunk + 1) * width, at : at + LANES] = jnp.where(
                where_ref[5] > 0, left_ref[place], right_ref[place]
            )


def setup_body(where_ref, left_ref, right_ref, blocks_ref, pattern_ref, matrix_ref, offset_ref, inverse_ref):
    modes = blocks_ref.shape[1]
    count = blocks_ref.shape[3] // LANES
    matrix_ref[...] = jnp.zeros_like(matrix_ref)
    row = lax.broadcasted_iota(jnp.int32, (SUB, LANES), 0)
    column = lax.broadcasted_iota(jnp.int32, (1, LANES), 1)
    at_offset = 3 * modes * SUB
    for b in range(count + 2 * EXT):
        inner = EXT <= b < EXT + count
        side = left_ref if b < EXT else right_ref
        at = b - EXT if inner else (b if b < EXT else b - EXT - count)
        cols = pl.ds(at * LANES, LANES)
        diagonal = jnp.zeros((SUB, LANES), F32)
        for k in range(3):
            for p in range(modes):
                if inner:
                    entry = blocks_ref[k, p, :, cols].astype(F32)
                else:
                    entry = side[pl.ds((k * modes + p) * SUB, modes), cols]
                matrix_ref[b, k, p, 0:modes, :] = entry
                if k == 0:
                    diagonal = jnp.where(row == p, entry[p : p + 1, :], diagonal)
        inverse_ref[b] = jnp.where(row < modes, 1.0 / jnp.where(row < modes, diagonal, 1.0), 0.0)
        for k in range(2):
            if inner:
                offset = pattern_ref[k + 1 : k + 2, cols] - (where_ref[2] + at * LANES) - column
            else:
                offset = side[at_offset + k : at_offset + k + 1, cols].astype(jnp.int32)
            offset_ref[b, k : k + 1, :] = jnp.clip(offset, -LANES, LANES)


def coarse_product(matrix_ref, offset_ref, field, b):
    lanes = lax.broadcasted_iota(jnp.int32, (1, LANES), 1)
    three = [field[b + i] for i in range(3)]
    picked = [three[1]] + [pick(three, lanes + offset_ref[b, k : k + 1, :]) for k in range(2)]
    terms = []
    modes = matrix_ref.shape[2]
    for p in range(SUB):
        if p < modes:
            terms.append(sum(matrix_ref[b, k, p] * picked[k] for k in range(3)))
        else:
            terms.append(jnp.zeros((SUB, LANES), F32))
    return fold_rows(terms)


def by_two(first, number, body):
    def trip(i, carry):
        body(first + 2 * i)
        body(first + 2 * i + 1)
        return carry

    lax.fori_loop(0, number // 2, trip, 0)
    if number % 2:
        body(first + number - 1)


def gather_body(parts_ref, ends_ref, all_ref):
    count = parts_ref.shape[0]
    blocks = []
    for b in range(-1, count + 1):
        total = None
        for device in (b - 1, b, b + 1):
            if 0 <= device < count:
                at = (b - device + 1) * LANES
                term = parts_ref[device, :, at : at + LANES]
                total = term if total is None else total + term
        blocks.append(total)
    for i, block in enumerate(blocks):
        all_ref[i] = block
    for i in range(SPILL):
        ends_ref[i] = blocks[i]
        ends_ref[SPILL + i] = blocks[count + 2 - SPILL + i]


def coarse_down_body(where_ref, all_ref, even_ref, odd_ref, matrix_ref, offset_ref, inverse_ref, section_ref, rhs_ref, sol_ref, top_ref, field, other):
    total = matrix_ref.shape[0]
    count = total - 2 * EXT
    modes = matrix_ref.shape[2]
    width = section_ref.shape[2]
    zero = jnp.zeros((SUB, LANES), F32)
    parity = where_ref[6]
    for b in range(total):
        terms = []
        at = b - (EXT - 1)
        if 0 <= at < count + 2:
            terms.append(all_ref[at])
        if b < SPILL:
            terms.append(jnp.where(parity == 0, odd_ref[SPILL + b], even_ref[1 - parity, SPILL + b]))
        if b >= total - SPILL:
            i = b - (total - SPILL)
            terms.append(jnp.where(parity == 0, even_ref[1 - parity, i], odd_ref[i]))
        value = sum(terms[1:], terms[0])
        rhs_ref[b] = value
        field[b + 1] = inverse_ref[b] * value
    for edge in (0, total + 1):
        field[edge] = zero
        other[edge] = zero

    def first(b):
        start = field[b + 1]
        second = KEEP * start + FRESH * inverse_ref[b] * (rhs_ref[b] - coarse_product(matrix_ref, offset_ref, field, b))
        other[b + 1] = start + second
        sol_ref[b] = start + second

    by_two(EXT - FAR, count + 2 * FAR, first)

    def down(i, carry):
        for j in range(2):
            b = 2 * i + j + EXT
            residual = rhs_ref[b] - coarse_product(matrix_ref, offset_ref, other, b)
            cols = pl.ds(pl.multiple_of((2 * i + j) * LANES, LANES), LANES)
            out = []
            for k in range(3):
                value = carry[k]
                for p in range(modes):
                    value = value + section_ref[k, p, :, cols].astype(F32) * residual[p : p + 1, :]
                out.append(value)
            carry = out
        return tuple(carry)

    sums = lax.fori_loop(0, count // 2, down, tuple(jnp.zeros((width, LANES), F32) for _ in range(3)))
    stacked = jnp.concatenate(list(sums) + [jnp.zeros((LANES - 3 * width, LANES), F32)], axis=0)
    ones = jnp.ones((16, LANES), BF16)
    row = sum(lanes_dot(ones, part) for part in split3(stacked))
    top_ref[...] = jnp.broadcast_to(pltpu.roll(row, where_ref[4], 1)[0:1], top_ref.shape)


def top_answers(parts_ref, rows_of, width, column, slots):
    sections = parts_ref.shape[0]
    chunk_count = sections * width // LANES
    sub = lax.broadcasted_iota(jnp.int32, (SUB, LANES), 0)
    lane = lax.broadcasted_iota(jnp.int32, (SUB, LANES), 1)
    chunks = [None] * chunk_count
    for tile in range(sections // SUB):
        first = (sub + (tile * SUB - 1)) * width
        chunk = (first + ((lane - first) & (LANES - 1))) >> 7
        value = parts_ref[tile * SUB : (tile + 1) * SUB, :]
        low = (tile * SUB - 1) * width
        for q in range(max(0, low // LANES), min(chunk_count, (low + (SUB + 2) * width) // LANES + 1)):
            term = jnp.where(chunk == q, value, 0.0)
            chunks[q] = term if chunks[q] is None else chunks[q] + term
    chunks = [jnp.sum(c, axis=0, keepdims=True) for c in chunks]
    for i, places in enumerate(slots):
        total = None
        for q in range(chunk_count):
            term = rows_of(i, q) * chunks[q]
            total = term if total is None else total + term
        answer = jnp.broadcast_to(jnp.sum(total, axis=1, keepdims=True), (width, LANES))
        for place in places:
            column[place * width : (place + 1) * width, :] = answer


def up_body(
    where_ref,
    parts_ref,
    left_ref,
    top_inverse_ref,
    right_ref,
    section_ref,
    far_ref,
    sol_ref,
    rhs_ref,
    matrix_ref,
    offset_ref,
    inverse_ref,
    pair_ref,
    odd_ref,
    prolong_ref,
    even_prolong_ref,
    odd_prolong_ref,
    targets_ref,
    fine_matrix_ref,
    fine_pattern_ref,
    source_ref,
    fine_inverse_ref,
    change_ref,
    field_ref,
    column,
    field,
    other,
    final,
    ext,
    picked,
    out,
):
    total = matrix_ref.shape[0]
    count = total - 2 * EXT
    modes = matrix_ref.shape[2]
    zero = jnp.zeros((SUB, LANES), F32)
    width = section_ref.shape[2]
    halo = left_ref.shape[1]
    at_top = 3 * modes * SUB + SUB

    def rows_of(i, q):
        if i == 1:
            return top_inverse_ref[:, q * LANES : (q + 1) * LANES]
        if i == 3:
            chunk, at = divmod(q * LANES, far_ref.shape[1])
            return far_ref[pl.ds((3 * modes + chunk) * width, width), pl.ds(at, LANES)]
        chunk, at = divmod(q * LANES, halo)
        return (left_ref if i == 0 else right_ref)[pl.ds(at_top + chunk * width, width), pl.ds(at, LANES)]

    top_answers(parts_ref, rows_of, width, column, [(1,), (2,), (3,), (0, 4)])

    def corrected(b, slot, section_of):
        terms = []
        for p in range(SUB):
            if p < modes:
                value = sum(section_of(k, p) * column[(slot + k) * width : (slot + k + 1) * width, :] for k in range(3))
                terms.append(jnp.sum(value.reshape(width // SUB, SUB, LANES), axis=0))
            else:
                terms.append(zero)
        field[b + 1] = sol_ref[b] + fold_rows(terms)

    def far_block(slot, first):
        def body(b, carry):
            cols = pl.ds(pl.multiple_of((b - first) * LANES, LANES), LANES)
            corrected(b, slot, lambda k, p: far_ref[pl.ds((k * modes + p) * width, width), cols])
            return carry

        return body

    def own_block(b, carry):
        cols = pl.ds(pl.multiple_of((b - EXT) * LANES, LANES), LANES)
        corrected(b, 1, lambda k, p: section_ref[k, p, :, cols].astype(F32))
        return carry

    middle = where_ref[3] + EXT
    low, high = middle - FAR, middle + FAR + 1
    lax.fori_loop(low, jnp.minimum(high, EXT), far_block(0, EXT - FAR), 0)
    lax.fori_loop(jnp.maximum(low, EXT), jnp.minimum(high, EXT + count), own_block, 0)
    lax.fori_loop(jnp.maximum(low, EXT + count), high, far_block(2, EXT + count), 0)

    def smooth_first(b):
        change = inverse_ref[b] * (rhs_ref[b] - coarse_product(matrix_ref, offset_ref, field, b))
        final[b] = change
        other[b + 1] = field[b + 1] + change

    by_two(middle - 3, 7, smooth_first)

    def smooth_second(b):
        second = KEEP * final[b] + FRESH * inverse_ref[b] * (rhs_ref[b] - coarse_product(matrix_ref, offset_ref, other, b))
        final[b] = other[b + 1] + second

    by_two(middle - 2, 5, smooth_second)
    load_halo(where_ref, pair_ref, odd_ref, ext)
    rows = ext.shape[1]
    parity = where_ref[0]
    for which in range(3):
        block = (1, 2 - 2 * parity, 2 * parity)[which]
        side = (None, even_prolong_ref, odd_prolong_ref)[which]
        at = where_ref[3] + EXT + block - 2
        three = [final[at + i] for i in range(3)]
        terms = []
        for k in range(3):
            if which == 0:
                target = targets_ref[k : k + 1, :] - where_ref[1]
            else:
                row = 3 * modes * rows + k
                target = side[row : row + 1, :].astype(jnp.int32) - (where_ref[1] + (block - 1) * LANES)
            terms.append(three[1] if k == 0 else pick(three, target))
        for t in range(rows // SUB):
            part = pl.ds(t * SUB, SUB)
            value = ext[block, part, :]
            for k in range(3):
                for m in range(modes):
                    if which == 0:
                        weight = prolong_ref[k, m, part, :].astype(F32)
                    else:
                        weight = side[pl.ds((k * modes + m) * rows + t * SUB, SUB), :]
                    value = value + weight * terms[k][m : m + 1, :]
            ext[block, part, :] = value
    fine_product(where_ref, fine_matrix_ref, fine_pattern_ref, ext, picked, out)
    change = fine_inverse_ref[...] * (source_ref[...] - out[...])
    change_ref[...] = change
    field_ref[...] = ext[1] + change


def shards(
    source,
    fine_blocks,
    fine_pattern,
    fine_prolong,
    prolong_pattern,
    coarse_blocks,
    coarse_pattern,
    section_prolong,
    coarsest_inverse,
):
    both = ("slab", "sec")
    slabs, secs = lax.axis_size("slab"), lax.axis_size("sec")
    devices = slabs * secs
    rows, own = source.shape
    modes = fine_prolong.shape[2]
    section_rows = coarse_blocks.shape[3]
    width = section_prolong.shape[2]
    count = section_rows // LANES
    blocks = count + 2 * EXT
    halo = EXT * LANES
    section = lax.axis_index("slab")
    place = lax.axis_index("sec")
    device = section * secs + place
    roll = ((section + LANES - 1) * width) % LANES
    from_left = (place < secs // 2).astype(jnp.int32)
    where = jnp.stack([place % 2, device * own, section * section_rows, place, roll, from_left, section % 2]).astype(jnp.int32)

    prolong = jnp.transpose(fine_prolong, (0, 2, 1, 3))
    odd_swap = [(i, i + 1) for i in range(1, devices - 1, 2)] + [(i + 1, i) for i in range(1, devices - 1, 2)]
    even_swap = [(i, i ^ 1) for i in range(devices)]
    pairs = [[2 * i, 2 * i + 1] for i in range(secs // 2)]
    reach = [c for c in range(secs // 2) if c < FAR]

    def one_sided(value, step):
        moves = [(s * secs + c, (s + step) * secs + c) for s in range(slabs - step) for c in reach]
        moves += [((s + step) * secs + secs - 1 - c, s * secs + secs - 1 - c) for s in range(slabs - step) for c in reach]
        return lax.ppermute(value, both, moves)

    slab_odd = [(i, i + 1) for i in range(1, slabs - 1, 2)] + [(i + 1, i) for i in range(1, slabs - 1, 2)]
    slab_pairs = [[2 * i, 2 * i + 1] for i in range(slabs // 2)]

    def nearby(field):
        odd = lax.ppermute(field, both, odd_swap)
        pair = lax.all_gather(field, "sec", axis_index_groups=pairs, axis=0)
        picked = call(pick_body, [struct(2, rows, own)], [SMEM] + [VMEM] * 2)(where, pair, fine_pattern)[0]
        return pair, odd, call(own_body, [fine], [VMEM] * 2)(fine_blocks, field)[0], picked

    def beside(value, step):
        return lax.ppermute(value, "slab", [(i, i + step) for i in range(max(0, -step), min(slabs, slabs - step))])

    fine = struct(rows, own)
    work = [pltpu.VMEM((3, rows, own), F32), pltpu.VMEM((2, rows, own), F32), pltpu.VMEM((rows, own), F32)]
    inverse, start = call(first_body, [fine, fine], [VMEM] * 2)(fine_blocks, source)

    near = nearby(start)
    side = struct(3 * modes * SUB + SUB + width * pl.cdiv(coarsest_inverse.shape[1], halo), halo)
    low, high = call(pack_body, [side, side], [SMEM] + [VMEM] * 3)(where, coarse_blocks, coarse_pattern, coarsest_inverse)
    left_data, right_data = beside(high, 1), beside(low, -1)
    fine_pack = call(pack_prolong_body, [struct(3 * modes * rows + SUB, own)], [SMEM] + [VMEM] * 2)(where, prolong, prolong_pattern)[0]
    def step(body, outs, near, *rest):
        return call(body, outs, [SMEM] + [VMEM] * (6 + len(rest)), work[1:])(where, *near, fine_blocks, fine_pattern, *rest)

    coarse = struct(blocks, SUB, LANES)
    line = pltpu.VMEM((blocks + 2, SUB, LANES), F32)
    for cycle in range(CYCLES):
        if cycle == 0:
            change = start
        else:
            change, field = step(field_body, [fine, fine], nearby(solution), source, inverse)
            near = nearby(field)
        solution = step(solution_body, [fine], near, source, inverse, change)[0]
        if cycle == 0:
            solution, left_data, right_data = lax.optimization_barrier((solution, left_data, right_data))
            matrix, offset, coarse_inverse = call(
                setup_body,
                [struct(blocks, 3, modes, SUB, LANES), struct(blocks, SUB, LANES, dtype=jnp.int32), struct(blocks, SUB, LANES)],
                [SMEM] + [VMEM] * 4,
            )(where, left_data, right_data, coarse_blocks, coarse_pattern)
        near = nearby(solution)
        if cycle == 0:
            mine, later, fine_pack = lax.optimization_barrier((near[2], where, fine_pack))
            near = (*near[:2], mine, near[3])
            far = call(
                pack_far_body,
                [struct((3 * modes + pl.cdiv(slabs * width, FAR * LANES)) * width, FAR * LANES)],
                [SMEM] + [VMEM] * 3,
            )(later, section_prolong, left_data, right_data)[0]
            far_data = one_sided(far, 1)
            odd_prolong = lax.ppermute(fine_pack, both, odd_swap)
            even_prolong = lax.ppermute(fine_pack, both, even_swap)
        sums = step(restrict_body, [struct(secs, SUB, 3 * LANES)], near, source, prolong, prolong_pattern)[0]
        parts = lax.all_to_all(sums, "sec", 0, 0, tiled=True)
        ends, everything = call(gather_body, [struct(2 * SPILL, SUB, LANES), struct(secs + 2, SUB, LANES)], [VMEM])(parts)
        odd = lax.ppermute(ends, "slab", slab_odd)
        even = lax.all_gather(ends, "slab", axis_index_groups=slab_pairs, axis=0)
        rhs, coarse_sol, top = call(
            coarse_down_body, [coarse, coarse, struct(slabs, LANES)], [SMEM] + [VMEM] * 7, [line, line]
        )(where, everything, even, odd, matrix, offset, coarse_inverse, section_prolong)
        if cycle == 0:
            top, far_data, odd_prolong, even_prolong = lax.optimization_barrier((top, far_data, odd_prolong, even_prolong))
        tops = lax.all_to_all(top, "slab", 0, 0, tiled=True)
        change, field = call(
            up_body, [fine, fine], [SMEM] + [VMEM] * 21, [pltpu.VMEM((5 * width, LANES), F32), line, line, line] + work
        )(
            *(where, tops, left_data, coarsest_inverse, right_data, section_prolong, far_data, coarse_sol, rhs),
            *(matrix, offset, coarse_inverse, *near[:2], prolong, even_prolong, odd_prolong, prolong_pattern),
            *(fine_blocks, fine_pattern, source, inverse),
        )
        solution = step(solution_body, [fine], nearby(field), source, inverse, change)[0]
    return solution


def solution(mesh):
    in_specs = (
        P(None, ("slab", "sec")),
        P(None, None, None, ("slab", "sec")),
        P(None, ("slab", "sec")),
        P(None, None, None, ("slab", "sec")),
        P(None, ("slab", "sec")),
        P(None, None, None, "slab"),
        P(None, "slab"),
        P(None, None, None, "slab"),
        P("slab", None),
    )
    out_specs = P(None, ("slab", "sec"))
    return jax.shard_map(shards, mesh=mesh, in_specs=in_specs, out_specs=out_specs, check_vma=False)
```

```python
import jax
import jax.numpy as jnp
from jax import lax
from jax.experimental import pallas as pl
from jax.experimental.pallas import tpu as pltpu
from jax.sharding import PartitionSpec as P

CYCLES = 2
KEEP = 1.0 / 7.0
FRESH = 8.0 / 7.0
LANES = 128
SUB = 8
EXT = 4
FAR = 3
SPILL = EXT + 1
F32 = jnp.float32
BF16 = jnp.bfloat16
VMEM = pl.BlockSpec(memory_space=pltpu.VMEM)
SMEM = pl.BlockSpec(memory_space=pltpu.SMEM)


def call(body, outs, in_specs, scratch=(), flops=1 << 20, moved=1 << 20):
    return pl.pallas_call(
        body,
        out_shape=outs,
        in_specs=in_specs,
        out_specs=[VMEM] * len(outs),
        scratch_shapes=list(scratch),
        compiler_params=pltpu.CompilerParams(vmem_limit_bytes=24 << 20),
        cost_estimate=pl.CostEstimate(flops=flops, bytes_accessed=moved, transcendentals=0),
    )


def struct(*shape, dtype=F32):
    return jax.ShapeDtypeStruct(shape, dtype)


def take(x, lane):
    return jnp.take_along_axis(x, lane, axis=1, mode="promise_in_bounds")


def pick(three, target):
    lane = jnp.broadcast_to(target & (LANES - 1), three[0].shape)
    block = jnp.broadcast_to((target + LANES) >> 7, three[0].shape)
    a, b, c = (take(x, lane) for x in three)
    return jnp.where(block == 0, a, jnp.where(block == 1, b, c))


def fold_rows(terms):
    row = lax.broadcasted_iota(jnp.int32, (SUB, LANES), 0)
    for step in (4, 2, 1):
        high = (row & step) != 0
        half = len(terms) // 2
        folded = []
        for i in range(half):
            low_sum = terms[i] + pltpu.roll(terms[i], SUB - step, 0)
            high_sum = terms[i + half] + pltpu.roll(terms[i + half], step, 0)
            folded.append(jnp.where(high, high_sum, low_sum))
        terms = folded
    return terms[0]


def split3(x):
    high = x.astype(BF16)
    rest = x - high.astype(F32)
    middle = rest.astype(BF16)
    low = (rest - middle.astype(F32)).astype(BF16)
    return high, middle, low


def lanes_dot(a, b):
    return lax.dot_general(a, b, (((1,), (1,)), ((), ())), preferred_element_type=F32)


def load_halo(where_ref, pair_ref, odd_ref, ext):
    parity = where_ref[0]
    ext[1] = pair_ref[parity]
    ext[2 - 2 * parity] = pair_ref[1 - parity]
    ext[2 * parity] = odd_ref[...]


def product_rows(matrix_ref, ks, picked, out, before=None):
    rows = out.shape[0]

    def group(g, carry):
        part = pl.ds(pl.multiple_of(g * SUB, SUB), SUB)
        terms = []
        for p in range(SUB):
            total = None
            for k in ks:
                block = matrix_ref[k, g * SUB + p].astype(F32)
                product = jnp.sum((block * picked[k][...]).reshape(rows // SUB, SUB, LANES), axis=0)
                total = product if total is None else total + product
            terms.append(total)
        value = fold_rows(terms)
        out[part, :] = value if before is None else value + before[part, :]
        return carry

    lax.fori_loop(0, rows // SUB, group, 0)


def own_body(matrix_ref, field_ref, out_ref):
    product_rows(matrix_ref, (0,), [field_ref], out_ref)


def fine_product(where_ref, matrix_ref, pattern_ref, ext, picked, out, before=None):
    rows = out.shape[0]
    base = where_ref[1]
    for k in (1, 2):
        target = pattern_ref[k : k + 1, :] - base
        lane = jnp.broadcast_to(target & (LANES - 1), (SUB, LANES))
        block = jnp.broadcast_to((target + LANES) >> 7, (SUB, LANES))
        for t in range(rows // SUB):
            part = pl.ds(t * SUB, SUB)
            a, b, c = (take(ext[i, part, :], lane) for i in range(3))
            picked[k - 1, part, :] = jnp.where(block == 0, a, jnp.where(block == 1, b, c))

    near = {1: picked.at[0], 2: picked.at[1]}
    if before is None:
        near[0] = ext.at[1]
    product_rows(matrix_ref, sorted(near), near, out, before)


def first_body(matrix_ref, source_ref, inverse_ref, field_ref):
    rows = source_ref.shape[0]
    row = lax.broadcasted_iota(jnp.int32, (SUB, LANES), 0)
    for g in range(rows // SUB):
        part = pl.ds(g * SUB, SUB)
        diagonal = jnp.zeros((SUB, LANES), F32)
        for p in range(SUB):
            entry = matrix_ref[0, g * SUB + p].astype(F32)[g * SUB : (g + 1) * SUB]
            diagonal = jnp.where(row == p, entry, diagonal)
        inverse = 1.0 / diagonal
        inverse_ref[part, :] = inverse
        field_ref[part, :] = inverse * source_ref[part, :]


def pick_body(where_ref, pair_ref, pattern_ref, picked_ref):
    parity = where_ref[0]
    for k in (1, 2):
        target = pattern_ref[k : k + 1, :] - where_ref[1]
        lane = jnp.broadcast_to(target & (LANES - 1), (SUB, LANES))
        block = jnp.broadcast_to((target + LANES) >> 7, (SUB, LANES))
        for t in range(picked_ref.shape[1] // SUB):
            part = pl.ds(t * SUB, SUB)
            mine, other = take(pair_ref[parity, part, :], lane), take(pair_ref[1 - parity, part, :], lane)
            picked_ref[k - 1, part, :] = jnp.where(block == 1, mine, other)


def finish_product(where_ref, matrix_ref, pattern_ref, odd_ref, near_ref, own_ref, picked, out):
    odd = 2 * where_ref[0]
    for k in (1, 2):
        target = pattern_ref[k : k + 1, :] - where_ref[1]
        lane = jnp.broadcast_to(target & (LANES - 1), (SUB, LANES))
        block = jnp.broadcast_to((target + LANES) >> 7, (SUB, LANES))
        for t in range(out.shape[0] // SUB):
            part = pl.ds(t * SUB, SUB)
            picked[k - 1, part, :] = jnp.where(block == odd, take(odd_ref[part, :], lane), near_ref[k - 1, part, :])
    product_rows(matrix_ref, (1, 2), {1: picked.at[0], 2: picked.at[1]}, out, own_ref)


def field_body(where_ref, pair_ref, odd_ref, own_ref, near_ref, matrix_ref, pattern_ref, source_ref, inverse_ref, change_ref, field_ref, picked, out):
    finish_product(where_ref, matrix_ref, pattern_ref, odd_ref, near_ref, own_ref, picked, out)
    change = inverse_ref[...] * (source_ref[...] - out[...])
    change_ref[...] = change
    field_ref[...] = pair_ref[where_ref[0]] + change


def solution_body(where_ref, pair_ref, odd_ref, own_ref, near_ref, matrix_ref, pattern_ref, source_ref, inverse_ref, change_ref, field_ref, picked, out):
    finish_product(where_ref, matrix_ref, pattern_ref, odd_ref, near_ref, own_ref, picked, out)
    second = KEEP * change_ref[...] + FRESH * inverse_ref[...] * (source_ref[...] - out[...])
    field_ref[...] = pair_ref[where_ref[0]] + second


def restrict_body(where_ref, pair_ref, odd_ref, own_ref, near_ref, matrix_ref, pattern_ref, source_ref, prolong_ref, targets_ref, sums_ref, picked, out):
    finish_product(where_ref, matrix_ref, pattern_ref, odd_ref, near_ref, own_ref, picked, out)
    residual = source_ref[...] - out[...]
    modes = prolong_ref.shape[1]
    rows = residual.shape[0]
    slots = lax.broadcasted_iota(jnp.int32, (3 * LANES, LANES), 0)
    total = None
    for k in range(3):
        terms = []
        for m in range(SUB):
            if m < modes:
                product = prolong_ref[k, m].astype(F32) * residual
                terms.append(jnp.sum(product.reshape(rows // SUB, SUB, LANES), axis=0))
            else:
                terms.append(jnp.zeros((SUB, LANES), F32))
        parts = split3(fold_rows(terms))
        target = targets_ref[k : k + 1, :] - where_ref[1] + LANES
        hot = (slots == target).astype(F32).astype(BF16)
        stacked = jnp.concatenate([p.astype(F32) for p in parts] + [jnp.zeros((SUB, LANES), F32)], axis=0)
        spread = lanes_dot(stacked.astype(BF16), hot)
        total = spread if total is None else total + spread
    sums = total[0:SUB] + total[SUB : 2 * SUB] + total[2 * SUB : 3 * SUB]
    for i in range(sums_ref.shape[0]):
        sums_ref[i] = sums


def pack_body(where_ref, blocks_ref, pattern_ref, top_ref, low_ref, high_ref):
    modes = blocks_ref.shape[1]
    total = blocks_ref.shape[3]
    halo = low_ref.shape[1]
    width = top_ref.shape[0]
    column = lax.broadcasted_iota(jnp.int32, (1, halo), 1)
    for out, at in ((low_ref, 0), (high_ref, total - halo)):
        cols = pl.ds(at, halo)
        for k in range(3):
            for p in range(modes):
                row = (k * modes + p) * SUB
                out[row : row + modes, :] = blocks_ref[k, p, :, cols].astype(F32)
        row = 3 * modes * SUB
        for k in range(2):
            offset = pattern_ref[k + 1 : k + 2, cols] - (where_ref[2] + at) - column
            out[row + k : row + k + 1, :] = offset.astype(F32)
        row += SUB
        for i in range(pl.cdiv(top_ref.shape[1], halo)):
            part = top_ref[:, i * halo : (i + 1) * halo]
            out[row + i * width : row + (i + 1) * width, 0 : part.shape[1]] = part


def pack_prolong_body(where_ref, prolong_ref, targets_ref, fine_ref):
    modes, rows = prolong_ref.shape[1:3]
    for k in range(3):
        for m in range(modes):
            at = (k * modes + m) * rows
            fine_ref[at : at + rows, :] = prolong_ref[k, m].astype(F32)
        at = 3 * modes * rows + k
        fine_ref[at : at + 1, :] = targets_ref[k : k + 1, :].astype(F32)


def pack_far_body(where_ref, section_ref, left_ref, right_ref, far_ref):
    modes, width, total = section_ref.shape[1:]
    reach = far_ref.shape[1]
    cols = pl.ds(pl.multiple_of(where_ref[5] * (total - reach), LANES), reach)
    for k in range(3):
        for p in range(modes):
            at = (k * modes + p) * width
            far_ref[at : at + width, :] = section_ref[k, p, :, cols].astype(F32)
    at_top = 3 * modes * SUB + SUB
    at_far = 3 * modes * width
    halo = left_ref.shape[1]
    for q in range((far_ref.shape[0] - at_far) // width * (reach // LANES)):
        chunk, at = divmod(q * LANES, halo)
        place = (pl.ds(at_top + chunk * width, width), pl.ds(at, LANES))
        if at_top + (chunk + 1) * width <= left_ref.shape[0]:
            chunk, at = divmod(q * LANES, reach)
            far_ref[at_far + chunk * width : at_far + (chunk + 1) * width, at : at + LANES] = jnp.where(
                where_ref[5] > 0, left_ref[place], right_ref[place]
            )


def setup_body(where_ref, left_ref, right_ref, blocks_ref, pattern_ref, matrix_ref, offset_ref, inverse_ref):
    modes = blocks_ref.shape[1]
    count = blocks_ref.shape[3] // LANES
    matrix_ref[...] = jnp.zeros_like(matrix_ref)
    row = lax.broadcasted_iota(jnp.int32, (SUB, LANES), 0)
    column = lax.broadcasted_iota(jnp.int32, (1, LANES), 1)
    at_offset = 3 * modes * SUB
    for b in range(count + 2 * EXT):
        inner = EXT <= b < EXT + count
        side = left_ref if b < EXT else right_ref
        at = b - EXT if inner else (b if b < EXT else b - EXT - count)
        cols = pl.ds(at * LANES, LANES)
        diagonal = jnp.zeros((SUB, LANES), F32)
        for k in range(3):
            for p in range(modes):
                if inner:
                    entry = blocks_ref[k, p, :, cols].astype(F32)
                else:
                    entry = side[pl.ds((k * modes + p) * SUB, modes), cols]
                matrix_ref[b, k, p, 0:modes, :] = entry
                if k == 0:
                    diagonal = jnp.where(row == p, entry[p : p + 1, :], diagonal)
        inverse_ref[b] = jnp.where(row < modes, 1.0 / jnp.where(row < modes, diagonal, 1.0), 0.0)
        for k in range(2):
            if inner:
                offset = pattern_ref[k + 1 : k + 2, cols] - (where_ref[2] + at * LANES) - column
            else:
                offset = side[at_offset + k : at_offset + k + 1, cols].astype(jnp.int32)
            offset_ref[b, k : k + 1, :] = jnp.clip(offset, -LANES, LANES)


def coarse_product(matrix_ref, offset_ref, field, b):
    lanes = lax.broadcasted_iota(jnp.int32, (1, LANES), 1)
    three = [field[b + i] for i in range(3)]
    picked = [three[1]] + [pick(three, lanes + offset_ref[b, k : k + 1, :]) for k in range(2)]
    terms = []
    modes = matrix_ref.shape[2]
    for p in range(SUB):
        if p < modes:
            terms.append(sum(matrix_ref[b, k, p] * picked[k] for k in range(3)))
        else:
            terms.append(jnp.zeros((SUB, LANES), F32))
    return fold_rows(terms)


def by_many(first, number, body, unroll=7):
    each = min(unroll, number)

    def trip(i, carry):
        for j in range(each):
            body(first + each * i + j)
        return carry

    lax.fori_loop(0, number // each, trip, 0)
    for j in range(number - number % each, number):
        body(first + j)


def gather_body(parts_ref, ends_ref, all_ref):
    count = parts_ref.shape[0]
    blocks = []
    for b in range(-1, count + 1):
        total = None
        for device in (b - 1, b, b + 1):
            if 0 <= device < count:
                at = (b - device + 1) * LANES
                term = parts_ref[device, :, at : at + LANES]
                total = term if total is None else total + term
        blocks.append(total)
    for i, block in enumerate(blocks):
        all_ref[i] = block
    for i in range(SPILL):
        ends_ref[i] = blocks[i]
        ends_ref[SPILL + i] = blocks[count + 2 - SPILL + i]


def coarse_down_body(where_ref, all_ref, even_ref, odd_ref, matrix_ref, offset_ref, inverse_ref, section_ref, rhs_ref, sol_ref, top_ref, field, other):
    total = matrix_ref.shape[0]
    count = total - 2 * EXT
    modes = matrix_ref.shape[2]
    width = section_ref.shape[2]
    zero = jnp.zeros((SUB, LANES), F32)
    parity = where_ref[6]
    for b in range(total):
        terms = []
        at = b - (EXT - 1)
        if 0 <= at < count + 2:
            terms.append(all_ref[at])
        if b < SPILL:
            terms.append(jnp.where(parity == 0, odd_ref[SPILL + b], even_ref[1 - parity, SPILL + b]))
        if b >= total - SPILL:
            i = b - (total - SPILL)
            terms.append(jnp.where(parity == 0, even_ref[1 - parity, i], odd_ref[i]))
        value = sum(terms[1:], terms[0])
        rhs_ref[b] = value
        field[b + 1] = inverse_ref[b] * value
    for edge in (0, total + 1):
        field[edge] = zero
        other[edge] = zero

    def first(b):
        start = field[b + 1]
        second = KEEP * start + FRESH * inverse_ref[b] * (rhs_ref[b] - coarse_product(matrix_ref, offset_ref, field, b))
        other[b + 1] = start + second
        sol_ref[b] = start + second

    by_many(EXT - FAR, count + 2 * FAR, first)

    def down(i, carry):
        for j in range(2):
            b = 2 * i + j + EXT
            residual = rhs_ref[b] - coarse_product(matrix_ref, offset_ref, other, b)
            cols = pl.ds(pl.multiple_of((2 * i + j) * LANES, LANES), LANES)
            out = []
            for k in range(3):
                value = carry[k]
                for p in range(modes):
                    value = value + section_ref[k, p, :, cols].astype(F32) * residual[p : p + 1, :]
                out.append(value)
            carry = out
        return tuple(carry)

    sums = lax.fori_loop(0, count // 2, down, tuple(jnp.zeros((width, LANES), F32) for _ in range(3)))
    stacked = jnp.concatenate(list(sums) + [jnp.zeros((LANES - 3 * width, LANES), F32)], axis=0)
    ones = jnp.ones((16, LANES), BF16)
    row = sum(lanes_dot(ones, part) for part in split3(stacked))
    top_ref[...] = jnp.broadcast_to(pltpu.roll(row, where_ref[4], 1)[0:1], top_ref.shape)


def top_answers(parts_ref, rows_of, width, column, slots):
    sections = parts_ref.shape[0]
    chunk_count = sections * width // LANES
    sub = lax.broadcasted_iota(jnp.int32, (SUB, LANES), 0)
    lane = lax.broadcasted_iota(jnp.int32, (SUB, LANES), 1)
    chunks = [None] * chunk_count
    for tile in range(sections // SUB):
        first = (sub + (tile * SUB - 1)) * width
        chunk = (first + ((lane - first) & (LANES - 1))) >> 7
        value = parts_ref[tile * SUB : (tile + 1) * SUB, :]
        low = (tile * SUB - 1) * width
        for q in range(max(0, low // LANES), min(chunk_count, (low + (SUB + 2) * width) // LANES + 1)):
            term = jnp.where(chunk == q, value, 0.0)
            chunks[q] = term if chunks[q] is None else chunks[q] + term
    chunks = [jnp.sum(c, axis=0, keepdims=True) for c in chunks]
    for i, places in enumerate(slots):
        total = None
        for q in range(chunk_count):
            term = rows_of(i, q) * chunks[q]
            total = term if total is None else total + term
        answer = jnp.broadcast_to(jnp.sum(total, axis=1, keepdims=True), (width, LANES))
        for place in places:
            column[place * width : (place + 1) * width, :] = answer


def up_body(
    where_ref,
    parts_ref,
    left_ref,
    top_inverse_ref,
    right_ref,
    section_ref,
    far_ref,
    sol_ref,
    rhs_ref,
    matrix_ref,
    offset_ref,
    inverse_ref,
    pair_ref,
    odd_ref,
    prolong_ref,
    even_prolong_ref,
    odd_prolong_ref,
    targets_ref,
    fine_matrix_ref,
    fine_pattern_ref,
    source_ref,
    fine_inverse_ref,
    change_ref,
    field_ref,
    column,
    field,
    other,
    final,
    ext,
    picked,
    out,
):
    total = matrix_ref.shape[0]
    count = total - 2 * EXT
    modes = matrix_ref.shape[2]
    zero = jnp.zeros((SUB, LANES), F32)
    width = section_ref.shape[2]
    halo = left_ref.shape[1]
    at_top = 3 * modes * SUB + SUB

    def rows_of(i, q):
        if i == 1:
            return top_inverse_ref[:, q * LANES : (q + 1) * LANES]
        if i == 3:
            chunk, at = divmod(q * LANES, far_ref.shape[1])
            return far_ref[pl.ds((3 * modes + chunk) * width, width), pl.ds(at, LANES)]
        chunk, at = divmod(q * LANES, halo)
        return (left_ref if i == 0 else right_ref)[pl.ds(at_top + chunk * width, width), pl.ds(at, LANES)]

    top_answers(parts_ref, rows_of, width, column, [(1,), (2,), (3,), (0, 4)])

    def corrected(b, slot, section_of):
        terms = []
        for p in range(SUB):
            if p < modes:
                value = sum(section_of(k, p) * column[(slot + k) * width : (slot + k + 1) * width, :] for k in range(3))
                terms.append(jnp.sum(value.reshape(width // SUB, SUB, LANES), axis=0))
            else:
                terms.append(zero)
        field[b + 1] = sol_ref[b] + fold_rows(terms)

    def far_block(slot, first):
        def body(b, carry):
            cols = pl.ds(pl.multiple_of((b - first) * LANES, LANES), LANES)
            corrected(b, slot, lambda k, p: far_ref[pl.ds((k * modes + p) * width, width), cols])
            return carry

        return body

    def own_block(b, carry):
        cols = pl.ds(pl.multiple_of((b - EXT) * LANES, LANES), LANES)
        corrected(b, 1, lambda k, p: section_ref[k, p, :, cols].astype(F32))
        return carry

    middle = where_ref[3] + EXT
    low, high = middle - FAR, middle + FAR + 1
    lax.fori_loop(low, jnp.minimum(high, EXT), far_block(0, EXT - FAR), 0)
    lax.fori_loop(jnp.maximum(low, EXT), jnp.minimum(high, EXT + count), own_block, 0)
    lax.fori_loop(jnp.maximum(low, EXT + count), high, far_block(2, EXT + count), 0)

    def smooth_first(b):
        change = inverse_ref[b] * (rhs_ref[b] - coarse_product(matrix_ref, offset_ref, field, b))
        final[b] = change
        other[b + 1] = field[b + 1] + change

    by_many(middle - 3, 7, smooth_first)

    def smooth_second(b):
        second = KEEP * final[b] + FRESH * inverse_ref[b] * (rhs_ref[b] - coarse_product(matrix_ref, offset_ref, other, b))
        final[b] = other[b + 1] + second

    by_many(middle - 2, 5, smooth_second)
    load_halo(where_ref, pair_ref, odd_ref, ext)
    rows = ext.shape[1]
    parity = where_ref[0]
    for which in range(3):
        block = (1, 2 - 2 * parity, 2 * parity)[which]
        side = (None, even_prolong_ref, odd_prolong_ref)[which]
        at = where_ref[3] + EXT + block - 2
        three = [final[at + i] for i in range(3)]
        terms = []
        for k in range(3):
            if which == 0:
                target = targets_ref[k : k + 1, :] - where_ref[1]
            else:
                row = 3 * modes * rows + k
                target = side[row : row + 1, :].astype(jnp.int32) - (where_ref[1] + (block - 1) * LANES)
            terms.append(three[1] if k == 0 else pick(three, target))
        for t in range(rows // SUB):
            part = pl.ds(t * SUB, SUB)
            value = ext[block, part, :]
            for k in range(3):
                for m in range(modes):
                    if which == 0:
                        weight = prolong_ref[k, m, part, :].astype(F32)
                    else:
                        weight = side[pl.ds((k * modes + m) * rows + t * SUB, SUB), :]
                    value = value + weight * terms[k][m : m + 1, :]
            ext[block, part, :] = value
    fine_product(where_ref, fine_matrix_ref, fine_pattern_ref, ext, picked, out)
    change = fine_inverse_ref[...] * (source_ref[...] - out[...])
    change_ref[...] = change
    field_ref[...] = ext[1] + change


def shards(
    source,
    fine_blocks,
    fine_pattern,
    fine_prolong,
    prolong_pattern,
    coarse_blocks,
    coarse_pattern,
    section_prolong,
    coarsest_inverse,
):
    both = ("slab", "sec")
    slabs, secs = lax.axis_size("slab"), lax.axis_size("sec")
    devices = slabs * secs
    rows, own = source.shape
    modes = fine_prolong.shape[2]
    section_rows = coarse_blocks.shape[3]
    width = section_prolong.shape[2]
    count = section_rows // LANES
    blocks = count + 2 * EXT
    halo = EXT * LANES
    section = lax.axis_index("slab")
    place = lax.axis_index("sec")
    device = section * secs + place
    roll = ((section + LANES - 1) * width) % LANES
    from_left = (place < secs // 2).astype(jnp.int32)
    where = jnp.stack([place % 2, device * own, section * section_rows, place, roll, from_left, section % 2]).astype(jnp.int32)

    prolong = jnp.transpose(fine_prolong, (0, 2, 1, 3))
    odd_swap = [(i, i + 1) for i in range(1, devices - 1, 2)] + [(i + 1, i) for i in range(1, devices - 1, 2)]
    even_swap = [(i, i ^ 1) for i in range(devices)]
    pairs = [[2 * i, 2 * i + 1] for i in range(secs // 2)]
    reach = [c for c in range(secs // 2) if c < FAR]

    def one_sided(value, step):
        moves = [(s * secs + c, (s + step) * secs + c) for s in range(slabs - step) for c in reach]
        moves += [((s + step) * secs + secs - 1 - c, s * secs + secs - 1 - c) for s in range(slabs - step) for c in reach]
        return lax.ppermute(value, both, moves)

    slab_odd = [(i, i + 1) for i in range(1, slabs - 1, 2)] + [(i + 1, i) for i in range(1, slabs - 1, 2)]
    slab_pairs = [[2 * i, 2 * i + 1] for i in range(slabs // 2)]

    def nearby(field):
        odd = lax.ppermute(field, both, odd_swap)
        pair = lax.all_gather(field, "sec", axis_index_groups=pairs, axis=0)
        picked = call(pick_body, [struct(2, rows, own)], [SMEM] + [VMEM] * 2)(where, pair, fine_pattern)[0]
        return pair, odd, call(own_body, [fine], [VMEM] * 2)(fine_blocks, field)[0], picked

    def beside(value, step):
        return lax.ppermute(value, "slab", [(i, i + step) for i in range(max(0, -step), min(slabs, slabs - step))])

    fine = struct(rows, own)
    work = [pltpu.VMEM((3, rows, own), F32), pltpu.VMEM((2, rows, own), F32), pltpu.VMEM((rows, own), F32)]
    inverse, start = call(first_body, [fine, fine], [VMEM] * 2)(fine_blocks, source)

    near = nearby(start)
    side = struct(3 * modes * SUB + SUB + width * pl.cdiv(coarsest_inverse.shape[1], halo), halo)
    low, high = call(pack_body, [side, side], [SMEM] + [VMEM] * 3)(where, coarse_blocks, coarse_pattern, coarsest_inverse)
    left_data, right_data = beside(high, 1), beside(low, -1)
    fine_pack = call(pack_prolong_body, [struct(3 * modes * rows + SUB, own)], [SMEM] + [VMEM] * 2)(where, prolong, prolong_pattern)[0]
    def step(body, outs, near, *rest):
        return call(body, outs, [SMEM] + [VMEM] * (6 + len(rest)), work[1:])(where, *near, fine_blocks, fine_pattern, *rest)

    coarse = struct(blocks, SUB, LANES)
    line = pltpu.VMEM((blocks + 2, SUB, LANES), F32)
    for cycle in range(CYCLES):
        if cycle == 0:
            change = start
        else:
            change, field = step(field_body, [fine, fine], nearby(solution), source, inverse)
            near = nearby(field)
        solution = step(solution_body, [fine], near, source, inverse, change)[0]
        if cycle == 0:
            solution, left_data, right_data = lax.optimization_barrier((solution, left_data, right_data))
            matrix, offset, coarse_inverse = call(
                setup_body,
                [struct(blocks, 3, modes, SUB, LANES), struct(blocks, SUB, LANES, dtype=jnp.int32), struct(blocks, SUB, LANES)],
                [SMEM] + [VMEM] * 4,
            )(where, left_data, right_data, coarse_blocks, coarse_pattern)
        near = nearby(solution)
        if cycle == 0:
            mine, later, fine_pack = lax.optimization_barrier((near[2], where, fine_pack))
            near = (*near[:2], mine, near[3])
            far = call(
                pack_far_body,
                [struct((3 * modes + pl.cdiv(slabs * width, FAR * LANES)) * width, FAR * LANES)],
                [SMEM] + [VMEM] * 3,
            )(later, section_prolong, left_data, right_data)[0]
            far_data = one_sided(far, 1)
            odd_prolong = lax.ppermute(fine_pack, both, odd_swap)
            even_prolong = lax.ppermute(fine_pack, both, even_swap)
        sums = step(restrict_body, [struct(secs, SUB, 3 * LANES)], near, source, prolong, prolong_pattern)[0]
        parts = lax.all_to_all(sums, "sec", 0, 0, tiled=True)
        ends, everything = call(gather_body, [struct(2 * SPILL, SUB, LANES), struct(secs + 2, SUB, LANES)], [VMEM])(parts)
        odd = lax.ppermute(ends, "slab", slab_odd)
        even = lax.all_gather(ends, "slab", axis_index_groups=slab_pairs, axis=0)
        rhs, coarse_sol, top = call(
            coarse_down_body, [coarse, coarse, struct(slabs, LANES)], [SMEM] + [VMEM] * 7, [line, line]
        )(where, everything, even, odd, matrix, offset, coarse_inverse, section_prolong)
        if cycle == 0:
            top, far_data, odd_prolong, even_prolong = lax.optimization_barrier((top, far_data, odd_prolong, even_prolong))
        tops = lax.all_to_all(top, "slab", 0, 0, tiled=True)
        change, field = call(
            up_body, [fine, fine], [SMEM] + [VMEM] * 21, [pltpu.VMEM((5 * width, LANES), F32), line, line, line] + work
        )(
            *(where, tops, left_data, coarsest_inverse, right_data, section_prolong, far_data, coarse_sol, rhs),
            *(matrix, offset, coarse_inverse, *near[:2], prolong, even_prolong, odd_prolong, prolong_pattern),
            *(fine_blocks, fine_pattern, source, inverse),
        )
        solution = step(solution_body, [fine], nearby(field), source, inverse, change)[0]
    return solution


def solution(mesh):
    in_specs = (
        P(None, ("slab", "sec")),
        P(None, None, None, ("slab", "sec")),
        P(None, ("slab", "sec")),
        P(None, None, None, ("slab", "sec")),
        P(None, ("slab", "sec")),
        P(None, None, None, "slab"),
        P(None, "slab"),
        P(None, None, None, "slab"),
        P("slab", None),
    )
    out_specs = P(None, ("slab", "sec"))
    return jax.shard_map(shards, mesh=mesh, in_specs=in_specs, out_specs=out_specs, check_vma=False)
```
